512 devices in a mesh: context: 8 (over z), expert: 32 (over x, y), dp: 2 (over core).
Axes of the slice: x: 4, y: 8, z: 8, core: 2. Of those that a mesh axis runs over, the one named last changes fastest.
Arguments:
- residual: bfloat16 [32768, 1024], P(('dp', 'expert', 'context')), parts along dimension 0, may hold values from -6 to 6
- queries: bfloat16 [32768, 2048], P(('dp', 'expert', 'context')), parts along dimension 0, may hold values from -4.6 to 4.6
- key_vectors: bfloat16 [32768, 256], P(('dp', 'expert', 'context')), parts along dimension 0, may hold values from -5 to 5
- value_vectors: bfloat16 [32768, 256], P(('dp', 'expert', 'context')), parts along dimension 0, may hold values from -5 to 5
- output_weight: bfloat16 [2048, 1024], P('context'), may hold values from -0.875 to 0.875
- norm_gain: float32 [1024], replicated, may hold values from 0.1 to 1.9
- routes: int32 [32768, 8], P(('dp', 'expert', 'context')), parts along dimension 0, may hold values from 0 to 127, all different within a row; in each aligned block of 64 rows (0 to 63, 64 to 127, ...) at most 5 rows name the same one
- gate_levels: int32 [32768, 8], P(('dp', 'expert', 'context')), parts along dimension 0, may hold values from 16 to 96
- expert_in: bfloat16 [256, 1024, 384], P(('context', 'expert')), may hold values from -0.1875 to 0.1875
- expert_out: bfloat16 [256, 192, 1024], P(('context', 'expert')), may hold values from -0.3125 to 0.3125
Outputs:
- layer_out: float32 [32768, 1024], P(('dp', 'expert', 'context')), parts along dimension 0
The draws below stay inside these ranges and needn't reach their ends.
There are 2 independent parts, one for each index of `dp`. The reference program is written for one: setup_inputs(seed, part) draws one part's arguments, and reference() takes and returns one part's arrays. A program takes and returns all parts, laid end to end along the dimension named above; an argument that names none is the same for every part. Nothing has to cross between parts.
Inputs may be any that keep to these rules, and one draw needn't show every extreme that they name: `routes`: in the rows of one device no expert is named more than 5 times, and in every draw some expert reaches 5 in some device's rows; each row names 8 different experts.
All inputs are finite; a program needn't handle non-finite values.
Results may differ from the reference program's by a relative error of at most 0.022.
Values may be sent and summed in bfloat16 or wider, within the bound.
No kernel may reach another device: no remote copies, remote signals or barrier semaphores. Data moves between devices by JAX's collectives and lax.ppermute only.
A program may use at most 192 MiB of HBM per device.

```python
import math
import jax
import jax.numpy as jnp
import numpy as np
from jax import lax

D = 1024
HEADS = 16
KV_HEADS = 2
HD = 128
FF = 384
TOPK = 8
TOK_DEV = 64
SEQ = 16384
EXPERTS = 128
CAP = 5
HALF = 192
N_CONTEXT = 8
N_EXPERT = 32


def draw_residual(key, part):
    row_scale = jnp.exp(jax.random.uniform(jax.random.fold_in(key, 3), (SEQ, 1), jnp.float32, -1.15, 1.15))
    column_scale = jnp.exp(jax.random.uniform(jax.random.fold_in(key, 4), (1, D), jnp.float32, -1.15, 1.15))
    normal_part = jnp.clip(jax.random.normal(jax.random.fold_in(key, 5), (SEQ, D), jnp.float32), -3.0, 3.0)
    return (0.2 * row_scale * column_scale * normal_part).astype(jnp.bfloat16)


def draw_queries(key, part):
    return jnp.clip(jax.random.normal(jax.random.fold_in(key, 1), (SEQ, HEADS * HD), jnp.float32), -4.5, 4.5).astype(jnp.bfloat16)


def draw_key_vectors(key, part):
    return jnp.clip(1.5 * jax.random.normal(jax.random.fold_in(key, 2), (SEQ, KV_HEADS * HD), jnp.float32), -5.0, 5.0).astype(jnp.bfloat16)


def plant(drawn, rng, least, top_value):
    longest = drawn.shape.index(max(drawn.shape))
    spots = []
    for shift in (0, 1):
        where = [jax.random.randint(jax.random.fold_in(rng, axis), (), 0, length) for axis, length in enumerate(drawn.shape)]
        where[longest] = (where[longest] + shift) % drawn.shape[longest]
        spots.append(tuple(where))
    return drawn.at[spots[0]].set(least).at[spots[1]].set(top_value)


def level_of(own_key, extent, shards, least, high):
    def one(position, parts):
        steps = jax.random.uniform(jax.random.fold_in(jax.random.fold_in(own_key, 6), position), (parts,), jnp.float32, least / len(shards), high / len(shards))
        return jnp.repeat(jnp.exp(steps), extent[position] // parts).reshape((-1,) + (1,) * (len(extent) - position - 1))

    gain = one(*shards[0])
    for cut in shards[1:]:
        gain = gain * one(*cut)
    return gain


def shared_out(own_key, own, number, rows, count, top, reach, skew):
    ranking = jax.random.permutation(own_key, count)
    packed, usual = portions_of(count, rows * top, reach, skew, True), portions_of(count, rows * top, reach, skew, False)
    places = jnp.arange(count)

    def named(lengths, rotation):
        used = int((lengths > 0).sum())
        fixed = max(1, used // 4)
        moved = fixed + (places - fixed + rotation * (used - fixed)) % max(1, count - fixed)
        return jnp.zeros((count,), jnp.int32).at[ranking[jnp.where(places < fixed, places, moved)]].set(jnp.asarray(lengths, jnp.int32))

    lengths = jnp.where(number % 4 == 0, named(packed, number // 4), named(usual, number - number // 4 - 1))
    mixed = jax.random.permutation(jax.random.fold_in(own, 3), count)
    donor, sink = mixed[0:count // 2 * 2:2], mixed[1:count // 2 * 2:2]
    margin = jnp.minimum(lengths[donor] - 1, reach - lengths[sink]) // 2
    margin = jnp.where((donor == ranking[0]) | (sink == ranking[0]) | (lengths[sink] == 0), 0, jnp.maximum(margin, 0))
    moved = jax.random.randint(jax.random.fold_in(own, 4), (count // 2,), 0, 1 << 20) % (margin + 1)
    lengths = lengths.at[donor].add(-moved).at[sink].add(moved)
    members = jnp.searchsorted(jnp.cumsum(lengths), jnp.arange(rows * top), side="right").astype(jnp.int32)
    listing = members.reshape(top, rows).T
    listing = listing[jax.random.permutation(jax.random.fold_in(own, 1), rows)]
    rotation = jax.random.randint(jax.random.fold_in(own, 2), (rows, 1), 0, top)
    return jnp.take_along_axis(listing, (jnp.arange(top)[None, :] + rotation) % top, axis=1)


def portions_of(amount, total, reach, skew, full):
    portions = [(1 << 20) // math.isqrt(standing ** skew) + 1 for standing in range(1, amount + 1)]
    largest = reach if full else min(reach, max(-(-total // amount), total * portions[0] // sum(portions)))
    least = 1 if total - largest >= amount - 1 else 0
    holding, spare = [largest] + [least] * (amount - 1), total - largest - least * (amount - 1)
    while spare > 0:
        free = [i for i in range(1, amount) if holding[i] < largest] or [i for i in range(1, amount) if holding[i] < reach]
        mass, budget = sum([portions[i] for i in free]), spare
        for i in free:
            addition = min(reach - holding[i], max(1, budget * portions[i] // mass), spare)
            holding[i] = holding[i] + addition
            spare = spare - addition
    return np.array(holding)


def gaussian(rng, dims, deviation, reach, shards=(), held_as=jnp.bfloat16):
    values = deviation * jax.random.normal(rng, dims, jnp.float32)
    if shards:
        values = values * level_of(rng, dims, shards, -0.22, 0.18)
    return jnp.clip(values, -reach, reach).astype(held_as)


def setup_inputs(seed: int = 0, part: int = 0) -> dict:
    keys = jax.random.split(jax.random.key(seed), 11)
    part_splits = jax.random.split(jax.random.fold_in(keys[10], part), 11)
    residual = draw_residual(jax.random.fold_in(jax.random.fold_in(keys[10], part), 71), part)
    queries = draw_queries(jax.random.fold_in(jax.random.fold_in(keys[10], part), 71), part)
    key_vectors = draw_key_vectors(jax.random.fold_in(jax.random.fold_in(keys[10], part), 71), part)
    value_vectors = gaussian(part_splits[3], (SEQ, KV_HEADS * HD), 1.0, 5.0, ((0, 256),))
    output_weight = gaussian(keys[4], (HEADS * HD, D), 48 ** -0.5, 0.875, ((0, 8),))
    norm_gain = jnp.clip(1.0 + 0.18 * jax.random.normal(keys[5], (D,), jnp.float32), 0.1, 1.9)
    routes_keys = jax.random.split(jax.random.fold_in(part_splits[6], 1), SEQ // TOK_DEV)
    routes_turns = jax.random.permutation(jax.random.fold_in(part_splits[6], 3), SEQ // TOK_DEV)
    routes = jax.vmap(lambda own, number: shared_out(jax.random.fold_in(part_splits[6], 2), own, number, TOK_DEV, EXPERTS, TOPK, CAP, 1))(routes_keys, routes_turns).reshape((SEQ, TOPK))
    gate_levels = plant(jax.random.randint(part_splits[7], (SEQ, TOPK), 16, 97), jax.random.fold_in(part_splits[7], 1), 16, 96).astype(jnp.int32)
    expert_in = gaussian(keys[8], (2 * EXPERTS, D, FF), D ** -0.5, 0.1875, ((0, 256),))
    expert_out = gaussian(keys[9], (2 * EXPERTS, HALF, D), FF ** -0.5, 0.3125, ((0, 256),))
    return dict(residual=residual, queries=queries, key_vectors=key_vectors, value_vectors=value_vectors, output_weight=output_weight, norm_gain=norm_gain, routes=routes, gate_levels=gate_levels, expert_in=expert_in, expert_out=expert_out)


def attend_head(query_rows, key_rows, value_rows, block_rows):
    length = key_rows.shape[0]
    scaling = 1.0 / math.sqrt(query_rows.shape[1])
    key_position = jnp.arange(length, dtype=jnp.int32)

    def one_block(block_index):
        begin_row = (block_index * block_rows).astype(jnp.int32)
        query_block = lax.dynamic_slice_in_dim(query_rows, begin_row, block_rows, 0)
        scores = jnp.dot(query_block, key_rows.T, preferred_element_type=jnp.float32) * scaling
        query_position = begin_row + jnp.arange(block_rows, dtype=jnp.int32)
        allowed = key_position[None, :] <= query_position[:, None]
        masked = jnp.where(allowed, scores, -jnp.inf)
        row_max = lax.optimization_barrier(jnp.max(masked, axis=1, keepdims=True))
        weights = jnp.where(allowed, jnp.exp(masked - row_max), 0.0)
        denominator = lax.optimization_barrier(jnp.sum(weights, axis=1, keepdims=True))
        weighted = jnp.dot(weights.astype(jnp.bfloat16), value_rows, preferred_element_type=jnp.float32)
        return (weighted / denominator).astype(jnp.bfloat16)
    blocks = lax.map(one_block, jnp.arange(length // block_rows, dtype=jnp.int32))
    return blocks.reshape(length, query_rows.shape[1])

def reference(residual, queries, key_vectors, value_vectors, output_weight, norm_gain, routes, gate_levels, expert_in, expert_out):
    length, width = residual.shape
    head_count = queries.shape[1] // HD
    key_head_count = key_vectors.shape[1] // HD
    group_size = head_count // key_head_count
    block_rows = math.gcd(length, 1024)
    query_heads = queries.reshape(length, head_count, HD).transpose(1, 0, 2)
    key_heads = key_vectors.reshape(length, key_head_count, HD).transpose(1, 0, 2)
    value_heads = value_vectors.reshape(length, key_head_count, HD).transpose(1, 0, 2)

    def one_head(head_index):
        shared = head_index // group_size
        return attend_head(query_heads[head_index], key_heads[shared], value_heads[shared], block_rows)
    attention = lax.map(one_head, jnp.arange(head_count, dtype=jnp.int32))
    attention = attention.transpose(1, 0, 2).reshape(length, head_count * HD)
    columns_dev = head_count // N_CONTEXT * HD
    projected = jnp.zeros((length, width), jnp.float32)
    for context_index in range(N_CONTEXT):
        lower = context_index * columns_dev
        head_part = jnp.dot(attention[:, lower:lower + columns_dev], output_weight[lower:lower + columns_dev], preferred_element_type=jnp.float32).astype(jnp.bfloat16)
        projected = projected + lax.optimization_barrier(head_part).astype(jnp.float32)
    hidden_state = residual.astype(jnp.float32) + projected
    mean_square = lax.optimization_barrier(jnp.mean(hidden_state * hidden_state, axis=1, keepdims=True))
    normed = (hidden_state * lax.rsqrt(mean_square + 1e-06) * norm_gain).astype(jnp.bfloat16)
    top_count = routes.shape[1]
    expert_count = expert_in.shape[0] // 2
    inner_half = expert_out.shape[1]
    flat_routes = routes.reshape(-1)
    flat_gates = gate_levels.reshape(-1).astype(jnp.float32) / 256.0
    most_rows = CAP * N_CONTEXT * N_EXPERT
    row_index = jnp.arange(most_rows, dtype=jnp.int32)

    def one_expert(combined, expert_index):
        chosen = flat_routes == expert_index
        picked = jnp.nonzero(chosen, size=most_rows, fill_value=0)[0].astype(jnp.int32)
        usable = row_index < jnp.sum(chosen.astype(jnp.int32))
        token_index = picked // top_count
        gathered = normed[token_index]
        summed = jnp.zeros((most_rows, width), jnp.float32)
        for half_index in range(2):
            block_index = 2 * expert_index + half_index
            projection = jnp.dot(gathered, expert_in[block_index], preferred_element_type=jnp.float32)
            activated = (jax.nn.silu(projection[:, :inner_half]) * projection[:, inner_half:]).astype(jnp.bfloat16)
            partial_out = jnp.dot(activated, expert_out[block_index], preferred_element_type=jnp.float32).astype(jnp.bfloat16)
            summed = summed + lax.optimization_barrier(partial_out).astype(jnp.float32)
        expert_rows = lax.optimization_barrier(summed.astype(jnp.bfloat16)).astype(jnp.float32)
        scaled = jnp.where(usable, flat_gates[picked], 0.0)
        combined = combined.at[token_index].add(scaled[:, None] * expert_rows)
        return (combined, None)
    moe_sum, unused_tail = lax.scan(one_expert, jnp.zeros((length, width), jnp.float32), jnp.arange(expert_count, dtype=jnp.int32))
    return hidden_state + moe_sum
```

```python
import math

import jax
import jax.numpy as jnp
from jax import lax
from jax.experimental import pallas as pl
from jax.experimental.pallas import tpu as pltpu
from jax.sharding import Mesh
from jax.sharding import PartitionSpec as P

HD = 128
CAP = 5
LOG2E = 1.4426950408889634
BF = jnp.bfloat16
F32 = jnp.float32
NEG = -1e30
STAT = 8


def flash_kernel(pos_ref, q_ref, kv_ref, o_ref, vt_ref, m_ref, acc_ref):
    block = pl.program_id(0)
    own_x = pos_ref[0]
    own_y = pos_ref[1]
    nz = q_ref.shape[1]
    cols = nz * 128
    scale = LOG2E / math.sqrt(HD)

    @pl.when((block == 0) & (pl.program_id(1) == 0))
    def _():
        for c in range(8):
            v = kv_ref[4 * (c % 2) : 4 * (c % 2) + 4, c // 2, :, 128:256].reshape(512, HD)
            vt_ref[c, 0:HD, :] = v.astype(F32).T.astype(BF)
            vt_ref[c, HD : HD + 16, :] = jnp.ones((16, 512), BF)

    tiles = block * 8 + own_y
    chunk_count = tiles // 4
    q_raw = q_ref[0]
    q = jnp.concatenate([q_raw[:, :, 0:HD], q_raw[:, :, HD : 2 * HD]], axis=1).reshape(cols, HD)
    group = 256
    groups = [(g * group, q[g * group : (g + 1) * group]) for g in range(cols // group)]

    def keys(c):
        return kv_ref[pl.ds(4 * (c % 2), 4), c // 2, :, 0:HD].reshape(512, HD)

    def scores(k, q_group):
        return lax.dot_general(
            k, q_group, (((1,), (1,)), ((), ())), preferred_element_type=F32
        )

    last_keys = keys(chunk_count)
    last_values = vt_ref[chunk_count]
    row = lax.broadcasted_iota(jnp.int32, (512, group), 0)
    col = lax.broadcasted_iota(jnp.int32, (512, group), 1)
    inner = row % 128
    key_pos = (4 * chunk_count + row // 128) * 512 + (inner // 16) * 64 + inner % 16 + 16 * own_x
    for start, q_group in groups:
        z_first = pl.program_id(1) * nz + start // 128
        q_pos = tiles * 512 + (z_first + col // 128) * 64 + col % 64
        allowed = key_pos <= q_pos
        s = jnp.where(allowed, scores(last_keys, q_group), NEG)
        m = jnp.max(s, axis=0, keepdims=True)
        p = jnp.where(allowed, jnp.exp2((s - m) * scale), 0.0).astype(BF)
        m_ref[:, start : start + group] = m
        acc_ref[:, start : start + group] = jnp.dot(last_values, p, preferred_element_type=F32)

    def step(c, carry):
        k = keys(c)
        values = vt_ref[c]
        for start, q_group in groups:
            s = scores(k, q_group)
            m_old = m_ref[:, start : start + group]
            m = jnp.maximum(m_old, jnp.max(s, axis=0, keepdims=True))
            p = jnp.exp2((s - m) * scale).astype(BF)
            alpha = jnp.exp2((m_old - m) * scale)
            m_ref[:, start : start + group] = m
            acc_ref[:, start : start + group] = acc_ref[
                :, start : start + group
            ] * alpha + jnp.dot(values, p, preferred_element_type=F32)
        return carry

    lax.fori_loop(0, chunk_count, step, 0)
    total = acc_ref[HD : HD + 1, :]
    seen = total > 0.0
    safe = jnp.where(seen, total, 1.0)
    out = (acc_ref[0:HD, :] * (1.0 / safe)).astype(BF)
    level = jnp.where(seen, m_ref[...] * scale + jnp.log(safe) * LOG2E, NEG)
    first = level.astype(BF).astype(F32)
    second = (level - first).astype(BF).astype(F32)
    third = level - first - second
    pick = lax.broadcasted_iota(jnp.int32, (STAT, cols), 0)
    stats = jnp.where(pick == 0, first, jnp.where(pick == 1, second, jnp.where(pick == 2, third, 0.0)))
    stats = stats.astype(BF)
    for i in range(nz):
        o_ref[0, i, 0:HD, :] = out[:, i * 128 : (i + 1) * 128]
        o_ref[0, i, HD : HD + STAT, :] = stats[:, i * 128 : (i + 1) * 128]


def flash(position, queries, key_values):
    nz = 4
    return pl.pallas_call(
        flash_kernel,
        grid_spec=pltpu.PrefetchScalarGridSpec(
            num_scalar_prefetch=1,
            grid=(4, 8 // nz),
            in_specs=[
                pl.BlockSpec((1, nz, 64, 256), lambda i, j, s: (i, j, 0, 0)),
                pl.BlockSpec((8, 4, 128, 256), lambda i, j, s: (0, 0, 0, 0)),
            ],
            out_specs=pl.BlockSpec((1, nz, HD + STAT, 128), lambda i, j, s: (i, j, 0, 0)),
            scratch_shapes=[
                pltpu.VMEM((8, HD + 16, 512), BF),
                pltpu.VMEM((1, nz * 128), F32),
                pltpu.VMEM((HD + 16, nz * 128), F32),
            ],
        ),
        out_shape=jax.ShapeDtypeStruct((4, 8, HD + STAT, 128), BF),
        compiler_params=pltpu.CompilerParams(vmem_limit_bytes=40 * 1024 * 1024),
        name="flash",
    )(position, queries, key_values)


def merge_kernel(parts_ref, w_ref, res_ref, gain_ref, hidden_ref, normed_ref, acc_ref):
    c = pl.program_id(0)
    levels = []
    for x in range(4):
        st = parts_ref[x, 0, HD : HD + STAT, :].astype(F32)
        levels.append(st[0:1] + st[1:2] + st[2:3])
    top = jnp.maximum(jnp.maximum(levels[0], levels[1]), jnp.maximum(levels[2], levels[3]))
    shares = [jnp.exp2(level - top) for level in levels]
    inverse = 1.0 / (shares[0] + shares[1] + shares[2] + shares[3])
    mixed = parts_ref[0, 0, 0:HD, :].astype(F32) * (shares[0] * inverse)
    for x in range(1, 4):
        mixed = mixed + parts_ref[x, 0, 0:HD, :].astype(F32) * (shares[x] * inverse)
    rows = mixed.T.astype(BF)
    attention = jnp.concatenate([rows[0:64], rows[64:128]], axis=1)
    part = jnp.dot(attention, w_ref[...], preferred_element_type=F32)

    @pl.when(c == 0)
    def _():
        acc_ref[...] = res_ref[...].astype(F32) + part

    @pl.when(c > 0)
    def _():
        acc_ref[...] = acc_ref[...] + part

    @pl.when(c == 7)
    def _():
        hidden = acc_ref[...]
        hidden_ref[...] = hidden
        mean_square = jnp.mean(hidden * hidden, axis=1, keepdims=True)
        normed_ref[...] = (hidden * lax.rsqrt(mean_square + 1e-6) * gain_ref[...]).astype(BF)


def merge(parts, weight, residual, gain):
    tokens, width = residual.shape
    return pl.pallas_call(
        merge_kernel,
        grid=(8,),
        in_specs=[
            pl.BlockSpec((4, 1, HD + STAT, 128), lambda c: (0, c, 0, 0)),
            pl.BlockSpec((256, width), lambda c: (c, 0)),
            pl.BlockSpec((tokens, width), lambda c: (0, 0)),
            pl.BlockSpec((1, width), lambda c: (0, 0)),
        ],
        out_specs=[
            pl.BlockSpec((tokens, width), lambda c: (0, 0)),
            pl.BlockSpec((tokens, width), lambda c: (0, 0)),
        ],
        out_shape=[
            jax.ShapeDtypeStruct((tokens, width), F32),
            jax.ShapeDtypeStruct((tokens, width), BF),
        ],
        scratch_shapes=[pltpu.VMEM((tokens, width), F32)],
        name="merge",
    )(parts, weight, residual, gain)


def select_kernel(sel_ref, x_ref, o_ref, tmp_ref):
    count = sel_ref.shape[0]
    sel = sel_ref[...]
    for j in range(0, 8, 2):
        got = jnp.dot(sel, x_ref[:, j * 128 : (j + 2) * 128], preferred_element_type=F32)
        tmp_ref[pl.ds(j, count, stride=8), :] = got[:, 0:128]
        tmp_ref[pl.ds(j + 1, count, stride=8), :] = got[:, 128:256]
    o_ref[...] = tmp_ref[...].astype(BF)


def select(chosen, tokens):
    count = chosen.shape[0]
    return pl.pallas_call(
        select_kernel,
        out_shape=jax.ShapeDtypeStruct((count * 8, 128), BF),
        scratch_shapes=[pltpu.VMEM((count * 8, 128), F32)],
        compiler_params=pltpu.CompilerParams(vmem_limit_bytes=40 * 1024 * 1024),
        name="select",
    )(chosen, tokens)


def expert_kernel(x_ref, win_ref, wout_ref, o_ref, tmp_ref):
    rows = x_ref.shape[0] // 8
    inner = wout_ref.shape[0]
    tmp_ref[...] = x_ref[...].astype(F32)
    x = jnp.concatenate(
        [tmp_ref[pl.ds(j, rows, stride=8), :].astype(BF) for j in range(8)], axis=1
    )
    projection = jnp.dot(x, win_ref[...], preferred_element_type=F32)
    gate = projection[:, 0:inner]
    activated = (gate / (1.0 + jnp.exp(-gate)) * projection[:, inner:]).astype(BF)
    out = jnp.dot(activated, wout_ref[...], preferred_element_type=F32)
    for j in range(8):
        tmp_ref[pl.ds(j, rows, stride=8), :] = out[:, j * 128 : (j + 1) * 128]
    o_ref[...] = tmp_ref[...].astype(BF)


def expert(rows_in, weight_in, weight_out):
    total = rows_in.shape[0]
    block = total // 4
    return pl.pallas_call(
        expert_kernel,
        grid=(4,),
        in_specs=[
            pl.BlockSpec((block, 128), lambda i: (i, 0)),
            pl.BlockSpec(weight_in.shape, lambda i: (0, 0)),
            pl.BlockSpec(weight_out.shape, lambda i: (0, 0)),
        ],
        out_specs=pl.BlockSpec((block, 128), lambda i: (i, 0)),
        out_shape=jax.ShapeDtypeStruct((total, 128), BF),
        scratch_shapes=[pltpu.VMEM((block, 128), F32)],
        compiler_params=pltpu.CompilerParams(vmem_limit_bytes=40 * 1024 * 1024),
        name="expert",
    )(rows_in, weight_in, weight_out)


def gather_kernel(gates_ref, x_ref, o_ref, tmp_ref):
    count = gates_ref.shape[1]
    gates = gates_ref[...]
    tmp_ref[...] = x_ref[...].astype(F32)
    for j in range(0, 8, 2):
        x = jnp.concatenate(
            [
                tmp_ref[pl.ds(j, count, stride=8), :].astype(BF),
                tmp_ref[pl.ds(j + 1, count, stride=8), :].astype(BF),
            ],
            axis=1,
        )
        o_ref[:, j * 128 : (j + 2) * 128] = jnp.dot(
            gates, x, preferred_element_type=F32
        ).astype(BF)


def gather(gates, rows):
    count = gates.shape[1]
    return pl.pallas_call(
        gather_kernel,
        out_shape=jax.ShapeDtypeStruct((gates.shape[0], 1024), BF),
        scratch_shapes=[pltpu.VMEM((count * 8, 128), F32)],
        compiler_params=pltpu.CompilerParams(vmem_limit_bytes=40 * 1024 * 1024),
        name="gather",
    )(gates, rows)


def local(
    residual,
    queries,
    key_vectors,
    value_vectors,
    output_weight,
    norm_gain,
    routes,
    gate_levels,
    expert_in,
    expert_out,
):
    tokens, width = residual.shape
    own_x = lax.axis_index("x")
    own_y = lax.axis_index("y2") * 2 + lax.axis_index("y1")

    key_value = jnp.concatenate(
        [key_vectors.reshape(4, 16, 2, HD), value_vectors.reshape(4, 16, 2, HD)], axis=3
    ).transpose(0, 2, 1, 3)
    key_value = jnp.broadcast_to(key_value[:, :, None], (4, 2, 4, 16, 2 * HD)).reshape(
        32, 16, 2 * HD
    )
    key_value = lax.all_to_all(key_value, ("x", "z"), split_axis=0, concat_axis=0, tiled=True)
    key_values = lax.all_gather(
        key_value.reshape(512, 2 * HD), ("y2", "y1"), axis=0, tiled=True
    ).reshape(8, 4, 128, 2 * HD)

    query = queries.reshape(tokens, 8, 2 * HD).transpose(1, 0, 2)
    query = jnp.broadcast_to(query[None], (4, 8, tokens, 2 * HD)).reshape(32, tokens, 2 * HD)
    query, _ = lax.optimization_barrier((query, key_value))
    query = lax.all_to_all(query, ("x", "z"), split_axis=0, concat_axis=0, tiled=True).reshape(
        4, 8, tokens, 2 * HD
    )

    listing = jnp.concatenate([routes, gate_levels], axis=1)
    listing = jnp.broadcast_to(listing[None], (4, tokens, 16))
    listing, _ = lax.optimization_barrier((listing, query))
    listing = lax.all_to_all(listing, "x", split_axis=0, concat_axis=0, tiled=True)
    named, levels = listing[:, :, 0:8], listing[:, :, 8:16]
    local_expert = jnp.arange(32, dtype=jnp.int32)
    wanted = (local_expert // 4) * 16 + own_x * 4 + local_expert % 4
    match = named[:, :, :, None] == wanted
    hits = jnp.any(match, axis=2)
    gates = jnp.sum(jnp.where(match, levels[:, :, :, None], 0), axis=2).astype(F32) / 256.0
    before = jnp.tril(jnp.ones((tokens, tokens), BF), -1)
    ranks = jnp.einsum(
        "ab,sbq->saq", before, hits.astype(BF), preferred_element_type=F32
    ).astype(jnp.int32)
    ranks = jnp.where(hits, ranks, -1)
    slots = jnp.arange(CAP, dtype=jnp.int32)
    same = jnp.eye(4, dtype=jnp.bool_)
    placed = (ranks.transpose(2, 0, 1)[:, None, None, :, :] == slots[None, None, :, None, None]) & (
        same[None, :, None, :, None]
    )
    chosen = placed.astype(BF).reshape(32 * 4 * CAP, 4 * tokens)
    back = (ranks[:, :, :, None, None] == slots) & same[:, None, None, :, None]
    shares = jnp.where(back, gates[:, :, :, None, None], 0.0).astype(BF)
    shares = shares.reshape(4 * tokens, 32 * 4 * CAP)

    swap = [(0, 1), (1, 0)]
    own_in, own_out, _ = lax.optimization_barrier((expert_in[0], expert_out[0], query))
    other_in = lax.ppermute(own_in, "y1", swap)
    other_out = lax.ppermute(own_out, "y1", swap)
    half = own_in.shape[1] // 2
    weight_in = jnp.concatenate(
        [own_in[:, :half], other_in[:, :half], own_in[:, half:], other_in[:, half:]], axis=1
    )
    weight_out = jnp.concatenate([own_out, other_out], axis=0)

    output_weight, _ = lax.optimization_barrier((output_weight, key_values))
    whole_weight = lax.all_gather(output_weight, "z", axis=0, tiled=True)

    position = jnp.stack([own_x, own_y]).astype(jnp.int32)
    parts = flash(position, query, key_values)
    parts = lax.all_to_all(
        parts.reshape(32, HD + STAT, 128), ("x", "z"), split_axis=0, concat_axis=0, tiled=True
    ).reshape(4, 8, HD + STAT, 128)
    hidden, normed = merge(parts, whole_weight, residual, norm_gain.reshape(1, width))

    spread = jnp.broadcast_to(normed[None], (4, tokens, width))
    spread = lax.all_to_all(spread, "x", split_axis=0, concat_axis=0, tiled=True)
    outgoing = select(chosen, spread.reshape(4 * tokens, width))
    arrived = lax.all_to_all(
        outgoing.reshape(32, 4 * CAP * 8, 128), ("z", "y2"), split_axis=0, concat_axis=0, tiled=True
    )
    done = expert(arrived.reshape(-1, 128), weight_in, weight_out)
    answers = lax.all_to_all(
        done.reshape(32, 4 * CAP * 8, 128), ("z", "y2"), split_axis=0, concat_axis=0, tiled=True
    )
    sums = gather(shares, answers.reshape(-1, 128))
    sums = lax.all_to_all(
        sums.reshape(4, tokens, width), "x", split_axis=0, concat_axis=0, tiled=True
    )
    return hidden + jnp.sum(sums.astype(F32), axis=0)


def solution(mesh):
    fine = Mesh(mesh.devices.reshape(8, 4, 4, 2, 2), ("z", "x", "y2", "y1", "dp"))
    rows = P(("dp", "x", "y2", "y1", "z"), None)
    halves = P(("z", "x", "y2", "y1"), None, None)
    return jax.shard_map(
        local,
        mesh=fine,
        in_specs=(rows, rows, rows, rows, P("z", None), P(), rows, rows, halves, halves),
        out_specs=rows,
        check_vma=False,
    )
```

```python
import math

import jax
import jax.numpy as jnp
from jax import lax
from jax.experimental import pallas as pl
from jax.experimental.pallas import tpu as pltpu
from jax.sharding import Mesh
from jax.sharding import PartitionSpec as P

HD = 128
CAP = 5
LOG2E = 1.4426950408889634
BF = jnp.bfloat16
F32 = jnp.float32
NEG = -1e30
STAT = 8


def flash_kernel(pos_ref, q_ref, kv_ref, o_ref, vt_ref, m_ref, acc_ref):
    block = pl.program_id(0)
    own_x = pos_ref[0]
    own_y = pos_ref[1]
    nz = q_ref.shape[1]
    cols = nz * 128
    scale = LOG2E / math.sqrt(HD)

    @pl.when((block == 0) & (pl.program_id(1) == 0))
    def _():
        for c in range(8):
            v = kv_ref[4 * (c % 2) : 4 * (c % 2) + 4, c // 2, :, 128:256].reshape(512, HD)
            vt_ref[c, 0:HD, :] = v.astype(F32).T.astype(BF)
            vt_ref[c, HD : HD + 16, :] = jnp.ones((16, 512), BF)

    tiles = block * 8 + own_y
    chunk_count = tiles // 4
    q_raw = q_ref[0]
    q = jnp.concatenate([q_raw[:, :, 0:HD], q_raw[:, :, HD : 2 * HD]], axis=1).reshape(cols, HD)
    group = 256
    groups = [(g * group, q[g * group : (g + 1) * group]) for g in range(cols // group)]

    def keys(c):
        return kv_ref[pl.ds(4 * (c % 2), 4), c // 2, :, 0:HD].reshape(512, HD)

    def scores(k, q_group):
        return lax.dot_general(
            k, q_group, (((1,), (1,)), ((), ())), preferred_element_type=F32
        )

    last_keys = keys(chunk_count)
    last_values = vt_ref[chunk_count]
    row = lax.broadcasted_iota(jnp.int32, (512, group), 0)
    col = lax.broadcasted_iota(jnp.int32, (512, group), 1)
    inner = row % 128
    key_pos = (4 * chunk_count + row // 128) * 512 + (inner // 16) * 64 + inner % 16 + 16 * own_x
    for start, q_group in groups:
        z_first = pl.program_id(1) * nz + start // 128
        q_pos = tiles * 512 + (z_first + col // 128) * 64 + col % 64
        allowed = key_pos <= q_pos
        s = jnp.where(allowed, scores(last_keys, q_group), NEG)
        m = jnp.max(s, axis=0, keepdims=True)
        p = jnp.where(allowed, jnp.exp2((s - m) * scale), 0.0).astype(BF)
        m_ref[:, start : start + group] = m
        acc_ref[:, start : start + group] = jnp.dot(last_values, p, preferred_element_type=F32)

    def step(c, carry):
        k = keys(c)
        values = vt_ref[c]
        for start, q_group in groups:
            s = scores(k, q_group)
            m_old = m_ref[:, start : start + group]
            m = jnp.maximum(m_old, jnp.max(s, axis=0, keepdims=True))
            p = jnp.exp2((s - m) * scale).astype(BF)
            alpha = jnp.exp2((m_old - m) * scale)
            m_ref[:, start : start + group] = m
            acc_ref[:, start : start + group] = acc_ref[
                :, start : start + group
            ] * alpha + jnp.dot(values, p, preferred_element_type=F32)
        return carry

    lax.fori_loop(0, chunk_count, step, 0)
    total = acc_ref[HD : HD + 1, :]
    seen = total > 0.0
    safe = jnp.where(seen, total, 1.0)
    out = (acc_ref[0:HD, :] * (1.0 / safe)).astype(BF)
    level = jnp.where(seen, m_ref[...] * scale + jnp.log(safe) * LOG2E, NEG)
    first = level.astype(BF).astype(F32)
    second = (level - first).astype(BF).astype(F32)
    third = level - first - second
    pick = lax.broadcasted_iota(jnp.int32, (STAT, cols), 0)
    stats = jnp.where(pick == 0, first, jnp.where(pick == 1, second, jnp.where(pick == 2, third, 0.0)))
    stats = stats.astype(BF)
    for i in range(nz):
        o_ref[0, i, 0:HD, :] = out[:, i * 128 : (i + 1) * 128]
        o_ref[0, i, HD : HD + STAT, :] = stats[:, i * 128 : (i + 1) * 128]


def flash(position, queries, key_values):
    nz = 4
    return pl.pallas_call(
        flash_kernel,
        grid_spec=pltpu.PrefetchScalarGridSpec(
            num_scalar_prefetch=1,
            grid=(4, 8 // nz),
            in_specs=[
                pl.BlockSpec((1, nz, 64, 256), lambda i, j, s: (i, j, 0, 0)),
                pl.BlockSpec((8, 4, 128, 256), lambda i, j, s: (0, 0, 0, 0)),
            ],
            out_specs=pl.BlockSpec((1, nz, HD + STAT, 128), lambda i, j, s: (i, j, 0, 0)),
            scratch_shapes=[
                pltpu.VMEM((8, HD + 16, 512), BF),
                pltpu.VMEM((1, nz * 128), F32),
                pltpu.VMEM((HD + 16, nz * 128), F32),
            ],
        ),
        out_shape=jax.ShapeDtypeStruct((4, 8, HD + STAT, 128), BF),
        compiler_params=pltpu.CompilerParams(vmem_limit_bytes=40 * 1024 * 1024),
        cost_estimate=pl.CostEstimate(
            flops=4 * 4096 * 2560 * HD, bytes_accessed=5 << 20, transcendentals=4096 * 2560
        ),
        name="flash",
    )(position, queries, key_values)


def merge_kernel(pos_ref, parts_ref, w_ref, v_ref, res_ref, gain_ref, hidden_ref, normed_ref, acc_ref):
    c = pl.program_id(0)
    levels = []
    for x in range(4):
        st = parts_ref[x, 0, HD : HD + STAT, :].astype(F32)
        levels.append(st[0:1] + st[1:2] + st[2:3])
    top = jnp.maximum(jnp.maximum(levels[0], levels[1]), jnp.maximum(levels[2], levels[3]))
    shares = [jnp.exp2(level - top) for level in levels]
    inverse = 1.0 / (shares[0] + shares[1] + shares[2] + shares[3])
    mixed = parts_ref[0, 0, 0:HD, :].astype(F32) * (shares[0] * inverse)
    for x in range(1, 4):
        mixed = mixed + parts_ref[x, 0, 0:HD, :].astype(F32) * (shares[x] * inverse)
    rows = mixed.T.astype(BF)
    first = pos_ref[2] == 0
    attention = jnp.concatenate(
        [jnp.where(first, rows[0:64], rows[64:128]), jnp.where(first, rows[64:128], rows[0:64])],
        axis=1,
    )
    weight = jnp.concatenate([w_ref[...], v_ref[...]], axis=0)
    part = jnp.dot(attention, weight, preferred_element_type=F32)

    @pl.when(c == 0)
    def _():
        acc_ref[...] = res_ref[...].astype(F32) + part

    @pl.when(c > 0)
    def _():
        acc_ref[...] = acc_ref[...] + part

    @pl.when(c == 7)
    def _():
        hidden = acc_ref[...]
        hidden_ref[...] = hidden
        mean_square = jnp.mean(hidden * hidden, axis=1, keepdims=True)
        normed_ref[...] = (hidden * lax.rsqrt(mean_square + 1e-6) * gain_ref[...]).astype(BF)


def merge(position, parts, weight, weight_other, residual, gain):
    tokens, width = residual.shape
    return pl.pallas_call(
        merge_kernel,
        grid_spec=pltpu.PrefetchScalarGridSpec(
            num_scalar_prefetch=1,
            grid=(8,),
            in_specs=[
                pl.BlockSpec((4, 1, HD + STAT, 128), lambda c, s: (0, c, 0, 0)),
                pl.BlockSpec((128, width), lambda c, s: (c, 0)),
                pl.BlockSpec((128, width), lambda c, s: (c, 0)),
                pl.BlockSpec((tokens, width), lambda c, s: (0, 0)),
                pl.BlockSpec((1, width), lambda c, s: (0, 0)),
            ],
            out_specs=[
                pl.BlockSpec((tokens, width), lambda c, s: (0, 0)),
                pl.BlockSpec((tokens, width), lambda c, s: (0, 0)),
            ],
            scratch_shapes=[pltpu.VMEM((tokens, width), F32)],
        ),
        out_shape=[
            jax.ShapeDtypeStruct((tokens, width), F32),
            jax.ShapeDtypeStruct((tokens, width), BF),
        ],
        name="merge",
    )(position, parts, weight, weight_other, residual, gain)


def select_kernel(sel_ref, x_ref, o_ref, tmp_ref):
    count = sel_ref.shape[0]
    sel = sel_ref[...]
    for j in range(0, 8, 2):
        got = jnp.dot(sel, x_ref[:, j * 128 : (j + 2) * 128], preferred_element_type=F32)
        tmp_ref[pl.ds(j, count, stride=8), :] = got[:, 0:128]
        tmp_ref[pl.ds(j + 1, count, stride=8), :] = got[:, 128:256]
    o_ref[...] = tmp_ref[...].astype(BF)


def select(chosen, tokens):
    count = chosen.shape[0]
    return pl.pallas_call(
        select_kernel,
        out_shape=jax.ShapeDtypeStruct((count * 8, 128), BF),
        scratch_shapes=[pltpu.VMEM((count * 8, 128), F32)],
        compiler_params=pltpu.CompilerParams(vmem_limit_bytes=40 * 1024 * 1024),
        name="select",
    )(chosen, tokens)


def expert_kernel(x_ref, win_ref, wout_ref, o_ref, tmp_ref):
    rows = x_ref.shape[0] // 8
    inner = wout_ref.shape[0]
    tmp_ref[...] = x_ref[...].astype(F32)
    x = jnp.concatenate(
        [tmp_ref[pl.ds(j, rows, stride=8), :].astype(BF) for j in range(8)], axis=1
    )
    projection = jnp.dot(x, win_ref[...], preferred_element_type=F32)
    gate = projection[:, 0:inner]
    activated = (gate / (1.0 + jnp.exp(-gate)) * projection[:, inner:]).astype(BF)
    out = jnp.dot(activated, wout_ref[...], preferred_element_type=F32)
    for j in range(8):
        tmp_ref[pl.ds(j, rows, stride=8), :] = out[:, j * 128 : (j + 1) * 128]
    o_ref[...] = tmp_ref[...].astype(BF)


def expert(rows_in, weight_in, weight_out):
    total = rows_in.shape[0]
    block = total // 4
    return pl.pallas_call(
        expert_kernel,
        grid=(4,),
        in_specs=[
            pl.BlockSpec((block, 128), lambda i: (i, 0)),
            pl.BlockSpec(weight_in.shape, lambda i: (0, 0)),
            pl.BlockSpec(weight_out.shape, lambda i: (0, 0)),
        ],
        out_specs=pl.BlockSpec((block, 128), lambda i: (i, 0)),
        out_shape=jax.ShapeDtypeStruct((total, 128), BF),
        scratch_shapes=[pltpu.VMEM((block, 128), F32)],
        compiler_params=pltpu.CompilerParams(vmem_limit_bytes=40 * 1024 * 1024),
        name="expert",
    )(rows_in, weight_in, weight_out)


def gather_kernel(gates_ref, x_ref, o_ref, tmp_ref):
    count = gates_ref.shape[1]
    gates = gates_ref[...]
    tmp_ref[...] = x_ref[...].astype(F32)
    for j in range(0, 8, 2):
        x = jnp.concatenate(
            [
                tmp_ref[pl.ds(j, count, stride=8), :].astype(BF),
                tmp_ref[pl.ds(j + 1, count, stride=8), :].astype(BF),
            ],
            axis=1,
        )
        o_ref[:, j * 128 : (j + 2) * 128] = jnp.dot(
            gates, x, preferred_element_type=F32
        ).astype(BF)


def gather(gates, rows):
    count = gates.shape[1]
    return pl.pallas_call(
        gather_kernel,
        out_shape=jax.ShapeDtypeStruct((gates.shape[0], 1024), BF),
        scratch_shapes=[pltpu.VMEM((count * 8, 128), F32)],
        compiler_params=pltpu.CompilerParams(vmem_limit_bytes=40 * 1024 * 1024),
        name="gather",
    )(gates, rows)


def local(
    residual,
    queries,
    key_vectors,
    value_vectors,
    output_weight,
    norm_gain,
    routes,
    gate_levels,
    expert_in,
    expert_out,
):
    tokens, width = residual.shape
    own_x = lax.axis_index("x")
    own_y2 = lax.axis_index("y2")
    own_y = own_y2 * 2 + lax.axis_index("y1")
    own_core = lax.axis_index("dp")
    position = jnp.stack([own_x, own_y, own_core]).astype(jnp.int32)

    key_value = jnp.concatenate(
        [key_vectors.reshape(4, 16, 2, HD), value_vectors.reshape(4, 16, 2, HD)], axis=3
    ).transpose(0, 2, 1, 3)
    key_value = jnp.broadcast_to(key_value[:, :, None], (4, 2, 4, 16, 2 * HD)).reshape(
        32, 16, 2 * HD
    )
    key_value = lax.all_to_all(key_value, ("x", "z"), split_axis=0, concat_axis=0, tiled=True)
    key_values = lax.all_gather(
        key_value.reshape(512, 2 * HD), ("y2", "y1"), axis=0, tiled=True
    ).reshape(8, 4, 128, 2 * HD)

    query = queries.reshape(tokens, 8, 2 * HD).transpose(1, 0, 2)
    query = jnp.broadcast_to(query[None], (4, 8, tokens, 2 * HD)).reshape(32, tokens, 2 * HD)
    query, _ = lax.optimization_barrier((query, key_value))
    query = lax.all_to_all(query, ("x", "z"), split_axis=0, concat_axis=0, tiled=True).reshape(
        4, 8, tokens, 2 * HD
    )

    listing = jnp.concatenate([routes, gate_levels], axis=1)
    listing = jnp.broadcast_to(listing[None], (4, tokens, 16))
    listing, _ = lax.optimization_barrier((listing, query))
    listing = lax.all_to_all(listing, "y2", split_axis=0, concat_axis=0, tiled=True)
    named, levels = listing[:, :, 0:8], listing[:, :, 8:16]
    local_expert = jnp.arange(32, dtype=jnp.int32)
    wanted = (local_expert % 8) * 16 + (local_expert // 8) * 4 + own_y2
    match = named[:, :, :, None] == wanted
    hits = jnp.any(match, axis=2)
    gates = jnp.sum(jnp.where(match, levels[:, :, :, None], 0), axis=2).astype(F32) / 256.0
    before = jnp.tril(jnp.ones((tokens, tokens), BF), -1)
    ranks = jnp.einsum(
        "ab,sbq->saq", before, hits.astype(BF), preferred_element_type=F32
    ).astype(jnp.int32)
    ranks = jnp.where(hits, ranks, -1)
    slots = jnp.arange(CAP, dtype=jnp.int32)
    same = jnp.eye(4, dtype=jnp.bool_)
    placed = (ranks.transpose(2, 0, 1)[:, None, None, :, :] == slots[None, None, :, None, None]) & (
        same[None, :, None, :, None]
    )
    chosen = placed.astype(BF).reshape(32 * 4 * CAP, 4 * tokens)
    back = (ranks[:, :, :, None, None] == slots) & same[:, None, None, :, None]
    shares = jnp.where(back, gates[:, :, :, None, None], 0.0).astype(BF)
    shares = shares.reshape(4 * tokens, 32 * 4 * CAP)

    swap = [(0, 1), (1, 0)]
    own_in, own_out, _ = lax.optimization_barrier((expert_in[0], expert_out[0], query))
    other_in = lax.ppermute(own_in, "y1", swap)
    other_out = lax.ppermute(own_out, "y1", swap)
    head_weight = lax.dynamic_slice_in_dim(output_weight, own_core * HD, HD, 0)
    head_weight, _ = lax.optimization_barrier((head_weight, query))
    gathered = lax.all_gather(head_weight, "z", axis=0, tiled=True)
    gathered_other = lax.ppermute(gathered, "dp", swap)

    parts = flash(position, query, key_values)
    parts, other_in, other_out = lax.optimization_barrier((parts, other_in, other_out))
    parts = lax.all_to_all(
        parts.reshape(32, HD + STAT, 128), ("x", "z"), split_axis=0, concat_axis=0, tiled=True
    ).reshape(4, 8, HD + STAT, 128)
    half = own_in.shape[1] // 2
    weight_in = jnp.concatenate(
        [own_in[:, :half], other_in[:, :half], own_in[:, half:], other_in[:, half:]], axis=1
    )
    weight_out = jnp.concatenate([own_out, other_out], axis=0)
    hidden, normed = merge(
        position, parts, gathered, gathered_other, residual, norm_gain.reshape(1, width)
    )

    spread = jnp.broadcast_to(normed[None], (4, tokens, width))
    spread = lax.all_to_all(spread, "y2", split_axis=0, concat_axis=0, tiled=True)
    outgoing = select(chosen, spread.reshape(4 * tokens, width))
    arrived = lax.all_to_all(
        outgoing.reshape(32, 4 * CAP * 8, 128), ("x", "z"), split_axis=0, concat_axis=0, tiled=True
    )
    done = expert(arrived.reshape(-1, 128), weight_in, weight_out)
    answers = lax.all_to_all(
        done.reshape(32, 4 * CAP * 8, 128), ("x", "z"), split_axis=0, concat_axis=0, tiled=True
    )
    sums = gather(shares, answers.reshape(-1, 128))
    sums = lax.all_to_all(
        sums.reshape(4, tokens, width), "y2", split_axis=0, concat_axis=0, tiled=True
    )
    return hidden + jnp.sum(sums.astype(F32), axis=0)


def solution(mesh):
    fine = Mesh(mesh.devices.reshape(8, 4, 4, 2, 2), ("z", "x", "y2", "y1", "dp"))
    rows = P(("dp", "x", "y2", "y1", "z"), None)
    halves = P(("z", "x", "y2", "y1"), None, None)
    return jax.shard_map(
        local,
        mesh=fine,
        in_specs=(rows, rows, rows, rows, P("z", None), P(), rows, rows, halves, halves),
        out_specs=rows,
        check_vma=False,
    )
```

```python
import math

import jax
import jax.numpy as jnp
from jax import lax
from jax.experimental import pallas as pl
from jax.experimental.pallas import tpu as pltpu
from jax.sharding import Mesh
from jax.sharding import PartitionSpec as P

HD = 128
CAP = 5
LOG2E = 1.4426950408889634
BF = jnp.bfloat16
F32 = jnp.float32
NEG = -1e30
LOW = -1e29
STAT = 8
SWAP = [(0, 1), (1, 0)]


def flash_kernel(pos_ref, q_ref, kv_ref, o_ref, vt_ref, bias_ref, acc_ref, m_ref, top_ref):
    block = pl.program_id(0)
    own_x = pos_ref[0]
    own_y = pos_ref[1]
    cols = 1024
    scale = LOG2E / math.sqrt(HD)

    def keys(c):
        return kv_ref[pl.ds(4 * (c % 2), 4), c // 2, :, 0:HD].reshape(512, HD)

    @pl.when(block == 0)
    def _():
        eye = (
            lax.broadcasted_iota(jnp.int32, (HD, HD), 0)
            == lax.broadcasted_iota(jnp.int32, (HD, HD), 1)
        ).astype(BF)
        for c in range(8):
            v = kv_ref[4 * (c % 2) : 4 * (c % 2) + 4, c // 2, :, HD : 2 * HD].reshape(512, HD)
            turned = lax.dot_general(eye, v, (((1,), (1,)), ((), ())), preferred_element_type=F32)
            vt_ref[c, 0:HD, :] = turned.astype(BF)
            vt_ref[c, HD : HD + 16, :] = jnp.ones((16, 512), BF)
        row = lax.broadcasted_iota(jnp.int32, (512, 128), 0)
        col = lax.broadcasted_iota(jnp.int32, (512, 128), 1)
        inner = row % 128
        key_pos = (
            (row // 128 - own_y % 4) * 512 + (inner // 16) * 64 + inner % 16 + 16 * own_x - col % 64
        )
        for z in range(8):
            bias_ref[:, z * 128 : (z + 1) * 128] = jnp.where(key_pos <= z * 64, 0.0, NEG)

    tiles = block * 8 + own_y
    chunk_count = tiles // 4
    q_raw = q_ref[0]
    q = jnp.concatenate([q_raw[:, :, 0:HD], q_raw[:, :, HD : 2 * HD]], axis=1).reshape(cols, HD)
    group = 1024
    groups = [(g * group, q[g * group : (g + 1) * group]) for g in range(cols // group)]

    def scores(k, q_group):
        return lax.dot_general(k, q_group, (((1,), (1,)), ((), ())), preferred_element_type=F32)

    first_keys = kv_ref[0, 0, :, 0:HD]
    hide = jnp.where(tiles == 0, 1.0, 0.0)
    for start, q_group in groups:
        part = slice(start, start + group)
        s = scores(first_keys, q_group) + bias_ref[0:128, part] * hide
        m_ref[:, part] = jnp.maximum(jnp.max(s, axis=0, keepdims=True), LOW)
        top_ref[:, part] = jnp.max(s.reshape(16, 8, group), axis=0)
        acc_ref[:, part] = jnp.zeros((HD + 16, group), F32)

    def quick(c, masked):
        k = keys(c)
        values = vt_ref[c]
        found = [scores(k, q_group) for _, q_group in groups]
        for (start, _), s in zip(groups, found):
            part = slice(start, start + group)
            if masked:
                s = s + bias_ref[:, part]
            p = jnp.exp2(s * scale - m_ref[:, part] * scale).astype(BF)
            top_ref[:, part] = jnp.maximum(
                top_ref[:, part], jnp.max(s.reshape(64, 8, group), axis=0)
            )
            acc_ref[:, part] = acc_ref[:, part] + jnp.dot(values, p, preferred_element_type=F32)

    def quick_step(c, carry):
        quick(c, False)
        return carry

    lax.fori_loop(0, chunk_count, quick_step, 0)
    quick(chunk_count, True)

    def careful(c, masked):
        k = keys(c)
        values = vt_ref[c]
        for start, q_group in groups:
            part = slice(start, start + group)
            s = scores(k, q_group)
            if masked:
                s = s + bias_ref[:, part]
            m_old = m_ref[:, part]
            m = jnp.maximum(m_old, jnp.max(s, axis=0, keepdims=True))
            p = jnp.exp2((s - m) * scale).astype(BF)
            alpha = jnp.exp2((m_old - m) * scale)
            m_ref[:, part] = m
            acc_ref[:, part] = acc_ref[:, part] * alpha + jnp.dot(
                values, p, preferred_element_type=F32
            )

    def careful_step(c, carry):
        careful(c, False)
        return carry

    rise = jnp.max((top_ref[...] - m_ref[...]) * scale)

    @pl.when(rise > 64.0)
    def _():
        m_ref[...] = jnp.full((1, cols), LOW, F32)
        acc_ref[...] = jnp.zeros((HD + 16, cols), F32)
        lax.fori_loop(0, chunk_count, careful_step, 0)
        careful(chunk_count, True)

    total = acc_ref[HD : HD + 1, :]
    seen = total > 0.0
    safe = jnp.where(seen, total, 1.0)
    out = (acc_ref[0:HD, :] * (1.0 / safe)).astype(BF)
    level = jnp.where(seen, m_ref[...] * scale + jnp.log(safe) * LOG2E, NEG)
    first = level.astype(BF).astype(F32)
    second = (level - first).astype(BF).astype(F32)
    third = level - first - second
    pick = lax.broadcasted_iota(jnp.int32, (STAT, cols), 0)
    stats = jnp.where(pick == 0, first, jnp.where(pick == 1, second, jnp.where(pick == 2, third, 0.0)))
    stats = stats.astype(BF)
    for i in range(8):
        o_ref[0, i, 0:HD, :] = out[:, i * 128 : (i + 1) * 128]
        o_ref[0, i, HD : HD + STAT, :] = stats[:, i * 128 : (i + 1) * 128]


def flash(position, queries, key_values):
    return pl.pallas_call(
        flash_kernel,
        grid_spec=pltpu.PrefetchScalarGridSpec(
            num_scalar_prefetch=1,
            grid=(4,),
            in_specs=[
                pl.BlockSpec((1, 8, 64, 256), lambda i, s: (i, 0, 0, 0)),
                pl.BlockSpec((8, 4, 128, 256), lambda i, s: (0, 0, 0, 0)),
            ],
            out_specs=pl.BlockSpec((1, 8, HD + STAT, 128), lambda i, s: (i, 0, 0, 0)),
            scratch_shapes=[
                pltpu.VMEM((8, HD + 16, 512), BF),
                pltpu.VMEM((512, 1024), F32),
                pltpu.VMEM((HD + 16, 1024), F32),
                pltpu.VMEM((1, 1024), F32),
                pltpu.VMEM((8, 1024), F32),
            ],
        ),
        out_shape=jax.ShapeDtypeStruct((4, 8, HD + STAT, 128), BF),
        compiler_params=pltpu.CompilerParams(vmem_limit_bytes=40 * 1024 * 1024),
        cost_estimate=pl.CostEstimate(
            flops=4 * 4096 * 2560 * HD, bytes_accessed=5 << 20, transcendentals=4096 * 2560
        ),
        name="flash",
    )(position, queries, key_values)


def merged_heads(pos_ref, parts_ref, second):
    found = []
    for c in range(2):
        levels = []
        for x in range(4):
            st = parts_ref[x, c, HD : HD + STAT, :].astype(F32)
            levels.append(st[0:1] + st[1:2] + st[2:3])
        top = jnp.maximum(jnp.maximum(levels[0], levels[1]), jnp.maximum(levels[2], levels[3]))
        shares = [jnp.exp2(level - top) for level in levels]
        inverse = 1.0 / (shares[0] + shares[1] + shares[2] + shares[3])
        mixed = parts_ref[0, c, 0:HD, :].astype(F32) * (shares[0] * inverse)
        for x in range(1, 4):
            mixed = mixed + parts_ref[x, c, 0:HD, :].astype(F32) * (shares[x] * inverse)
        rows = mixed.T.astype(BF)
        found.append(jnp.where((pos_ref[2] == 0) != second, rows[0:64], rows[64:128]))
    return jnp.concatenate(found, axis=1)


def merge_own_kernel(pos_ref, parts_ref, w_ref, res_ref, o_ref):
    part = jnp.dot(merged_heads(pos_ref, parts_ref, False), w_ref[...], preferred_element_type=F32)

    @pl.when(pl.program_id(0) == 0)
    def _():
        o_ref[...] = res_ref[...].astype(F32) + part

    @pl.when(pl.program_id(0) > 0)
    def _():
        o_ref[...] = o_ref[...] + part


def merge_other_kernel(pos_ref, parts_ref, w_ref, sum_ref, gain_ref, hidden_ref, normed_ref):
    step = pl.program_id(0)
    part = jnp.dot(merged_heads(pos_ref, parts_ref, True), w_ref[...], preferred_element_type=F32)

    @pl.when(step == 0)
    def _():
        hidden_ref[...] = sum_ref[...] + part

    @pl.when(step > 0)
    def _():
        hidden_ref[...] = hidden_ref[...] + part

    @pl.when(step == 3)
    def _():
        hidden = hidden_ref[...]
        mean_square = jnp.mean(hidden * hidden, axis=1, keepdims=True)
        normed_ref[...] = (hidden * lax.rsqrt(mean_square + 1e-6) * gain_ref[...]).astype(BF)


def merge_specs(tokens, width):
    return [
        pl.BlockSpec((4, 2, HD + STAT, 128), lambda c, s: (0, c, 0, 0)),
        pl.BlockSpec((256, width), lambda c, s: (c, 0)),
        pl.BlockSpec((tokens, width), lambda c, s: (0, 0)),
    ]


def merge(position, parts, weight, weight_other, residual, gain):
    tokens, width = residual.shape
    whole = pl.BlockSpec((tokens, width), lambda c, s: (0, 0))
    half_sum = pl.pallas_call(
        merge_own_kernel,
        grid_spec=pltpu.PrefetchScalarGridSpec(
            num_scalar_prefetch=1,
            grid=(4,),
            in_specs=merge_specs(tokens, width),
            out_specs=whole,
        ),
        out_shape=jax.ShapeDtypeStruct((tokens, width), F32),
        name="merge_own",
    )(position, parts, weight, residual)
    return pl.pallas_call(
        merge_other_kernel,
        grid_spec=pltpu.PrefetchScalarGridSpec(
            num_scalar_prefetch=1,
            grid=(4,),
            in_specs=merge_specs(tokens, width) + [pl.BlockSpec((1, width), lambda c, s: (0, 0))],
            out_specs=[whole, whole],
        ),
        out_shape=[
            jax.ShapeDtypeStruct((tokens, width), F32),
            jax.ShapeDtypeStruct((tokens, width), BF),
        ],
        name="merge_other",
    )(position, parts, weight_other, half_sum, gain)


def select_kernel(sel_ref, x_ref, o_ref, tmp_ref):
    count = sel_ref.shape[0]
    sel = sel_ref[...]
    for j in range(0, 8, 2):
        got = jnp.dot(sel, x_ref[:, j * 128 : (j + 2) * 128], preferred_element_type=F32)
        tmp_ref[pl.ds(j, count, stride=8), :] = got[:, 0:128]
        tmp_ref[pl.ds(j + 1, count, stride=8), :] = got[:, 128:256]
    o_ref[...] = tmp_ref[...].astype(BF)


def select(chosen, tokens):
    count = chosen.shape[0]
    return pl.pallas_call(
        select_kernel,
        out_shape=jax.ShapeDtypeStruct((count * 8, 128), BF),
        scratch_shapes=[pltpu.VMEM((count * 8, 128), F32)],
        compiler_params=pltpu.CompilerParams(vmem_limit_bytes=40 * 1024 * 1024),
        name="select",
    )(chosen, tokens)


def expert_kernel(x_ref, win_ref, wout_ref, o_ref, tmp_ref):
    rows = x_ref.shape[0] // 8
    inner = wout_ref.shape[0]
    tmp_ref[...] = x_ref[...].astype(F32)
    x = jnp.concatenate(
        [tmp_ref[pl.ds(j, rows, stride=8), :].astype(BF) for j in range(8)], axis=1
    )
    projection = jnp.dot(x, win_ref[...], preferred_element_type=F32)
    gate = projection[:, 0:inner]
    activated = (gate / (1.0 + jnp.exp(-gate)) * projection[:, inner:]).astype(BF)
    out = jnp.dot(activated, wout_ref[...], preferred_element_type=F32)
    for j in range(8):
        tmp_ref[pl.ds(j, rows, stride=8), :] = out[:, j * 128 : (j + 1) * 128]
    o_ref[...] = tmp_ref[...].astype(BF)


def expert(rows_in, weight_in, weight_out):
    total = rows_in.shape[0]
    block = total // 4
    return pl.pallas_call(
        expert_kernel,
        grid=(4,),
        in_specs=[
            pl.BlockSpec((block, 128), lambda i: (i, 0)),
            pl.BlockSpec(weight_in.shape, lambda i: (0, 0)),
            pl.BlockSpec(weight_out.shape, lambda i: (0, 0)),
        ],
        out_specs=pl.BlockSpec((block, 128), lambda i: (i, 0)),
        out_shape=jax.ShapeDtypeStruct((total, 128), BF),
        scratch_shapes=[pltpu.VMEM((block, 128), F32)],
        compiler_params=pltpu.CompilerParams(vmem_limit_bytes=40 * 1024 * 1024),
        name="expert",
    )(rows_in, weight_in, weight_out)


def gather_kernel(gates_ref, x_ref, o_ref, tmp_ref):
    count = gates_ref.shape[1]
    gates = gates_ref[...]
    tmp_ref[...] = x_ref[...].astype(F32)
    for j in range(0, 8, 2):
        x = jnp.concatenate(
            [
                tmp_ref[pl.ds(j, count, stride=8), :].astype(BF),
                tmp_ref[pl.ds(j + 1, count, stride=8), :].astype(BF),
            ],
            axis=1,
        )
        o_ref[:, j * 128 : (j + 2) * 128] = jnp.dot(
            gates, x, preferred_element_type=F32
        ).astype(BF)


def gather(gates, rows):
    count = gates.shape[1]
    return pl.pallas_call(
        gather_kernel,
        out_shape=jax.ShapeDtypeStruct((gates.shape[0], 1024), BF),
        scratch_shapes=[pltpu.VMEM((count * 8, 128), F32)],
        compiler_params=pltpu.CompilerParams(vmem_limit_bytes=40 * 1024 * 1024),
        name="gather",
    )(gates, rows)


def local(
    residual,
    queries,
    key_vectors,
    value_vectors,
    output_weight,
    norm_gain,
    routes,
    gate_levels,
    expert_in,
    expert_out,
):
    tokens, width = residual.shape
    own_x = lax.axis_index("x")
    own_y2 = lax.axis_index("y2")
    own_y = own_y2 * 2 + lax.axis_index("y1")
    own_core = lax.axis_index("dp")
    position = jnp.stack([own_x, own_y, own_core]).astype(jnp.int32)

    key_value = jnp.concatenate(
        [key_vectors.reshape(4, 16, 2, HD), value_vectors.reshape(4, 16, 2, HD)], axis=3
    ).transpose(0, 2, 1, 3)
    key_value = jnp.broadcast_to(key_value[:, :, None], (4, 2, 4, 16, 2 * HD)).reshape(
        32, 16, 2 * HD
    )
    key_value = lax.all_to_all(key_value, ("x", "z"), split_axis=0, concat_axis=0, tiled=True)
    key_values = lax.all_gather(
        key_value.reshape(512, 2 * HD), ("y2", "y1"), axis=0, tiled=True
    ).reshape(8, 4, 128, 2 * HD)

    query = queries.reshape(tokens, 8, 2 * HD).transpose(1, 0, 2)
    query = jnp.broadcast_to(query[None], (4, 8, tokens, 2 * HD)).reshape(32, tokens, 2 * HD)
    query, _ = lax.optimization_barrier((query, key_value))
    query = lax.all_to_all(query, ("x", "z"), split_axis=0, concat_axis=0, tiled=True).reshape(
        4, 8, tokens, 2 * HD
    )

    head_weight = lax.dynamic_slice_in_dim(output_weight, own_core * HD, HD, 0)
    head_weight, _ = lax.optimization_barrier((head_weight, query))
    gathered = lax.all_gather(head_weight, "z", axis=0, tiled=True)
    gathered_other = lax.ppermute(gathered, "dp", SWAP)

    own_in, own_out, _ = lax.optimization_barrier((expert_in[0], expert_out[0], query))
    other_in = lax.ppermute(own_in, "y1", SWAP)
    other_out = lax.ppermute(own_out, "y1", SWAP)

    shards = flash(position, query, key_values)
    shards, other_in, other_out = lax.optimization_barrier((shards, other_in, other_out))
    parts = lax.all_to_all(
        shards.reshape(32, HD + STAT, 128), ("x", "z"), split_axis=0, concat_axis=0, tiled=True
    ).reshape(4, 8, HD + STAT, 128)
    listing = jnp.concatenate([routes, gate_levels], axis=1)
    listing = jnp.broadcast_to(listing[None], (4, tokens, 16))
    listing, _ = lax.optimization_barrier((listing, shards))
    listing = lax.all_to_all(listing, "y2", split_axis=0, concat_axis=0, tiled=True)
    named, levels = listing[:, :, 0:8], listing[:, :, 8:16]
    local_expert = jnp.arange(32, dtype=jnp.int32)
    wanted = (local_expert % 8) * 16 + (local_expert // 8) * 4 + own_y2
    match = named[:, :, :, None] == wanted
    hits = jnp.any(match, axis=2)
    gates = jnp.sum(jnp.where(match, levels[:, :, :, None], 0), axis=2).astype(F32) / 256.0
    before = jnp.tril(jnp.ones((tokens, tokens), BF), -1)
    ranks = jnp.einsum(
        "ab,sbq->saq", before, hits.astype(BF), preferred_element_type=F32
    ).astype(jnp.int32)
    ranks = jnp.where(hits, ranks, -1)
    slots = jnp.arange(CAP, dtype=jnp.int32)
    same = jnp.eye(4, dtype=jnp.bool_)
    placed = (ranks.transpose(2, 0, 1)[:, None, None, :, :] == slots[None, None, :, None, None]) & (
        same[None, :, None, :, None]
    )
    chosen = placed.astype(BF).reshape(32 * 4 * CAP, 4 * tokens)
    back = (ranks[:, :, :, None, None] == slots) & same[:, None, None, :, None]
    shares = jnp.where(back, gates[:, :, :, None, None], 0.0).astype(BF)
    shares = shares.reshape(4 * tokens, 32 * 4 * CAP)

    half = own_in.shape[1] // 2
    weight_in = jnp.concatenate(
        [own_in[:, :half], other_in[:, :half], own_in[:, half:], other_in[:, half:]], axis=1
    )
    weight_out = jnp.concatenate([own_out, other_out], axis=0)
    hidden, normed = merge(
        position, parts, gathered, gathered_other, residual, norm_gain.reshape(1, width)
    )

    spread = jnp.broadcast_to(normed[None], (4, tokens, width))
    spread = lax.all_to_all(spread, "y2", split_axis=0, concat_axis=0, tiled=True)
    outgoing = select(chosen, spread.reshape(4 * tokens, width))
    arrived = lax.all_to_all(
        outgoing.reshape(32, 4 * CAP * 8, 128), ("x", "z"), split_axis=0, concat_axis=0, tiled=True
    )
    done = expert(arrived.reshape(-1, 128), weight_in, weight_out)
    answers = lax.all_to_all(
        done.reshape(32, 4 * CAP * 8, 128), ("x", "z"), split_axis=0, concat_axis=0, tiled=True
    )
    sums = gather(shares, answers.reshape(-1, 128))
    sums = lax.all_to_all(
        sums.reshape(4, tokens, width), "y2", split_axis=0, concat_axis=0, tiled=True
    )
    return hidden + jnp.sum(sums.astype(F32), axis=0)


def solution(mesh):
    fine = Mesh(mesh.devices.reshape(8, 4, 4, 2, 2), ("z", "x", "y2", "y1", "dp"))
    rows = P(("dp", "x", "y2", "y1", "z"), None)
    halves = P(("z", "x", "y2", "y1"), None, None)
    return jax.shard_map(
        local,
        mesh=fine,
        in_specs=(rows, rows, rows, rows, P("z", None), P(), rows, rows, halves, halves),
        out_specs=rows,
        check_vma=False,
    )
```

```python
import math

import jax
import jax.numpy as jnp
from jax import lax
from jax.experimental import pallas as pl
from jax.experimental.pallas import tpu as pltpu
from jax.sharding import Mesh
from jax.sharding import PartitionSpec as P

HD = 128
CAP = 5
LOG2E = 1.4426950408889634
BF = jnp.bfloat16
F32 = jnp.float32
NEG = -1e30
LOW = -1e29
STAT = 8
SWAP = [(0, 1), (1, 0)]


def flash_kernel(pos_ref, q_ref, kv_ref, o_ref, vt_ref, bias_ref, acc_ref, m_ref, top_ref):
    block = pl.program_id(0)
    own_x = pos_ref[0]
    own_y = pos_ref[1]
    cols = 1024
    scale = LOG2E / math.sqrt(HD)

    def keys(c):
        return kv_ref[pl.ds(4 * (c % 2), 4), c // 2, :, 0:HD].reshape(512, HD)

    @pl.when(block == 0)
    def _():
        eye = (
            lax.broadcasted_iota(jnp.int32, (HD, HD), 0)
            == lax.broadcasted_iota(jnp.int32, (HD, HD), 1)
        ).astype(BF)
        for c in range(8):
            v = kv_ref[4 * (c % 2) : 4 * (c % 2) + 4, c // 2, :, HD : 2 * HD].reshape(512, HD)
            turned = lax.dot_general(eye, v, (((1,), (1,)), ((), ())), preferred_element_type=F32)
            vt_ref[c, 0:HD, :] = turned.astype(BF)
            vt_ref[c, HD : HD + 16, :] = jnp.ones((16, 512), BF)
        row = lax.broadcasted_iota(jnp.int32, (512, 128), 0)
        col = lax.broadcasted_iota(jnp.int32, (512, 128), 1)
        inner = row % 128
        key_pos = (
            (row // 128 - own_y % 4) * 512 + (inner // 16) * 64 + inner % 16 + 16 * own_x - col % 64
        )
        for z in range(8):
            bias_ref[:, z * 128 : (z + 1) * 128] = jnp.where(key_pos <= z * 64, 0.0, NEG)

    tiles = block * 8 + own_y
    chunk_count = tiles // 4
    q_raw = q_ref[0]
    q = jnp.concatenate([q_raw[:, :, 0:HD], q_raw[:, :, HD : 2 * HD]], axis=1).reshape(cols, HD)
    group = 1024
    groups = [(g * group, q[g * group : (g + 1) * group]) for g in range(cols // group)]

    def scores(k, q_group):
        return lax.dot_general(k, q_group, (((1,), (1,)), ((), ())), preferred_element_type=F32)

    first_keys = kv_ref[0, 0, :, 0:HD]
    hide = jnp.where(tiles == 0, 1.0, 0.0)
    for start, q_group in groups:
        part = slice(start, start + group)
        s = scores(first_keys, q_group) + bias_ref[0:128, part] * hide
        m_ref[:, part] = jnp.maximum(jnp.max(s, axis=0, keepdims=True), LOW)
        top_ref[:, part] = jnp.max(s.reshape(16, 8, group), axis=0)
        acc_ref[:, part] = jnp.zeros((HD + 16, group), F32)

    def quick(c, masked):
        k = keys(c)
        values = vt_ref[c]
        found = [scores(k, q_group) for _, q_group in groups]
        for (start, _), s in zip(groups, found):
            part = slice(start, start + group)
            if masked:
                s = s + bias_ref[:, part]
            p = jnp.exp2(s * scale - m_ref[:, part] * scale).astype(BF)
            top_ref[:, part] = jnp.maximum(
                top_ref[:, part], jnp.max(s.reshape(64, 8, group), axis=0)
            )
            acc_ref[:, part] = acc_ref[:, part] + jnp.dot(values, p, preferred_element_type=F32)

    def quick_step(c, carry):
        quick(c, False)
        return carry

    lax.fori_loop(0, chunk_count, quick_step, 0)
    quick(chunk_count, True)

    def careful(c, masked):
        k = keys(c)
        values = vt_ref[c]
        for start, q_group in groups:
            part = slice(start, start + group)
            s = scores(k, q_group)
            if masked:
                s = s + bias_ref[:, part]
            m_old = m_ref[:, part]
            m = jnp.maximum(m_old, jnp.max(s, axis=0, keepdims=True))
            p = jnp.exp2((s - m) * scale).astype(BF)
            alpha = jnp.exp2((m_old - m) * scale)
            m_ref[:, part] = m
            acc_ref[:, part] = acc_ref[:, part] * alpha + jnp.dot(
                values, p, preferred_element_type=F32
            )

    def careful_step(c, carry):
        careful(c, False)
        return carry

    rise = jnp.max((top_ref[...] - m_ref[...]) * scale)

    @pl.when(rise > 64.0)
    def _():
        m_ref[...] = jnp.full((1, cols), LOW, F32)
        acc_ref[...] = jnp.zeros((HD + 16, cols), F32)
        lax.fori_loop(0, chunk_count, careful_step, 0)
        careful(chunk_count, True)

    total = acc_ref[HD : HD + 1, :]
    seen = total > 0.0
    safe = jnp.where(seen, total, 1.0)
    out = (acc_ref[0:HD, :] * (1.0 / safe)).astype(BF)
    level = jnp.where(seen, m_ref[...] * scale + jnp.log(safe) * LOG2E, NEG)
    first = level.astype(BF).astype(F32)
    second = (level - first).astype(BF).astype(F32)
    third = level - first - second
    pick = lax.broadcasted_iota(jnp.int32, (STAT, cols), 0)
    stats = jnp.where(pick == 0, first, jnp.where(pick == 1, second, jnp.where(pick == 2, third, 0.0)))
    stats = stats.astype(BF)
    for i in range(8):
        o_ref[0, i, 0:HD, :] = out[:, i * 128 : (i + 1) * 128]
        o_ref[0, i, HD : HD + STAT, :] = stats[:, i * 128 : (i + 1) * 128]


def flash(position, queries, key_values):
    return pl.pallas_call(
        flash_kernel,
        grid_spec=pltpu.PrefetchScalarGridSpec(
            num_scalar_prefetch=1,
            grid=(4,),
            in_specs=[
                pl.BlockSpec((1, 8, 64, 256), lambda i, s: (i, 0, 0, 0)),
                pl.BlockSpec((8, 4, 128, 256), lambda i, s: (0, 0, 0, 0)),
            ],
            out_specs=pl.BlockSpec((1, 8, HD + STAT, 128), lambda i, s: (i, 0, 0, 0)),
            scratch_shapes=[
                pltpu.VMEM((8, HD + 16, 512), BF),
                pltpu.VMEM((512, 1024), F32),
                pltpu.VMEM((HD + 16, 1024), F32),
                pltpu.VMEM((1, 1024), F32),
                pltpu.VMEM((8, 1024), F32),
            ],
        ),
        out_shape=jax.ShapeDtypeStruct((4, 8, HD + STAT, 128), BF),
        compiler_params=pltpu.CompilerParams(vmem_limit_bytes=40 * 1024 * 1024),
        cost_estimate=pl.CostEstimate(
            flops=4 * 4096 * 2560 * HD, bytes_accessed=5 << 20, transcendentals=4096 * 2560
        ),
        name="flash",
    )(position, queries, key_values)


def merged_heads(pos_ref, parts_ref, second):
    found = []
    for c in range(2):
        levels = []
        for x in range(4):
            st = parts_ref[x, c, HD : HD + STAT, :].astype(F32)
            levels.append(st[0:1] + st[1:2] + st[2:3])
        top = jnp.maximum(jnp.maximum(levels[0], levels[1]), jnp.maximum(levels[2], levels[3]))
        shares = [jnp.exp2(level - top) for level in levels]
        inverse = 1.0 / (shares[0] + shares[1] + shares[2] + shares[3])
        mixed = parts_ref[0, c, 0:HD, :].astype(F32) * (shares[0] * inverse)
        for x in range(1, 4):
            mixed = mixed + parts_ref[x, c, 0:HD, :].astype(F32) * (shares[x] * inverse)
        rows = mixed.T.astype(BF)
        found.append(jnp.where((pos_ref[2] == 0) != second, rows[0:64], rows[64:128]))
    return jnp.concatenate(found, axis=1)


def merge_own_kernel(pos_ref, parts_ref, w_ref, res_ref, o_ref):
    part = jnp.dot(merged_heads(pos_ref, parts_ref, False), w_ref[...], preferred_element_type=F32)

    @pl.when(pl.program_id(0) == 0)
    def _():
        o_ref[...] = res_ref[...].astype(F32) + part

    @pl.when(pl.program_id(0) > 0)
    def _():
        o_ref[...] = o_ref[...] + part


def merge_other_kernel(pos_ref, parts_ref, w_ref, sum_ref, gain_ref, hidden_ref, normed_ref):
    step = pl.program_id(0)
    part = jnp.dot(merged_heads(pos_ref, parts_ref, True), w_ref[...], preferred_element_type=F32)

    @pl.when(step == 0)
    def _():
        hidden_ref[...] = sum_ref[...] + part

    @pl.when(step > 0)
    def _():
        hidden_ref[...] = hidden_ref[...] + part

    @pl.when(step == 3)
    def _():
        hidden = hidden_ref[...]
        mean_square = jnp.mean(hidden * hidden, axis=1, keepdims=True)
        normed = (hidden * lax.rsqrt(mean_square + 1e-6) * gain_ref[...]).astype(BF)
        for x in range(4):
            normed_ref[x] = normed


def merge_specs(tokens, width):
    return [
        pl.BlockSpec((4, 2, HD + STAT, 128), lambda c, s: (0, c, 0, 0)),
        pl.BlockSpec((256, width), lambda c, s: (c, 0)),
        pl.BlockSpec((tokens, width), lambda c, s: (0, 0)),
    ]


def merge(position, parts, weight, weight_other, residual, gain):
    tokens, width = residual.shape
    whole = pl.BlockSpec((tokens, width), lambda c, s: (0, 0))
    half_sum = pl.pallas_call(
        merge_own_kernel,
        grid_spec=pltpu.PrefetchScalarGridSpec(
            num_scalar_prefetch=1,
            grid=(4,),
            in_specs=merge_specs(tokens, width),
            out_specs=whole,
        ),
        out_shape=jax.ShapeDtypeStruct((tokens, width), F32),
        name="merge_own",
    )(position, parts, weight, residual)
    return pl.pallas_call(
        merge_other_kernel,
        grid_spec=pltpu.PrefetchScalarGridSpec(
            num_scalar_prefetch=1,
            grid=(4,),
            in_specs=merge_specs(tokens, width) + [pl.BlockSpec((1, width), lambda c, s: (0, 0))],
            out_specs=[whole, pl.BlockSpec((4, tokens, width), lambda c, s: (0, 0, 0))],
        ),
        out_shape=[
            jax.ShapeDtypeStruct((tokens, width), F32),
            jax.ShapeDtypeStruct((4, tokens, width), BF),
        ],
        name="merge_other",
    )(position, parts, weight_other, half_sum, gain)


def select_kernel(sel_ref, x_ref, o_ref, tmp_ref):
    count = sel_ref.shape[0]
    sel = sel_ref[...]
    for j in range(0, 8, 2):
        got = jnp.dot(sel, x_ref[:, j * 128 : (j + 2) * 128], preferred_element_type=F32)
        tmp_ref[pl.ds(j, count, stride=8), :] = got[:, 0:128]
        tmp_ref[pl.ds(j + 1, count, stride=8), :] = got[:, 128:256]
    o_ref[...] = tmp_ref[...].astype(BF)


def select(chosen, tokens):
    count = chosen.shape[0]
    return pl.pallas_call(
        select_kernel,
        out_shape=jax.ShapeDtypeStruct((count * 8, 128), BF),
        scratch_shapes=[pltpu.VMEM((count * 8, 128), F32)],
        compiler_params=pltpu.CompilerParams(vmem_limit_bytes=40 * 1024 * 1024),
        name="select",
    )(chosen, tokens)


def expert_kernel(x_ref, win_ref, wout_ref, o_ref, tmp_ref):
    rows = x_ref.shape[0] // 8
    inner = wout_ref.shape[0]
    tmp_ref[...] = x_ref[...].astype(F32)
    x = jnp.concatenate(
        [tmp_ref[pl.ds(j, rows, stride=8), :].astype(BF) for j in range(8)], axis=1
    )
    projection = jnp.dot(x, win_ref[...], preferred_element_type=F32)
    gate = projection[:, 0:inner]
    activated = (gate / (1.0 + jnp.exp(-gate)) * projection[:, inner:]).astype(BF)
    out = jnp.dot(activated, wout_ref[...], preferred_element_type=F32)
    for j in range(8):
        tmp_ref[pl.ds(j, rows, stride=8), :] = out[:, j * 128 : (j + 1) * 128]
    o_ref[...] = tmp_ref[...].astype(BF)


def expert(rows_in, weight_in, weight_out):
    total = rows_in.shape[0]
    block = total // 4
    return pl.pallas_call(
        expert_kernel,
        grid=(4,),
        in_specs=[
            pl.BlockSpec((block, 128), lambda i: (i, 0)),
            pl.BlockSpec(weight_in.shape, lambda i: (0, 0)),
            pl.BlockSpec(weight_out.shape, lambda i: (0, 0)),
        ],
        out_specs=pl.BlockSpec((block, 128), lambda i: (i, 0)),
        out_shape=jax.ShapeDtypeStruct((total, 128), BF),
        scratch_shapes=[pltpu.VMEM((block, 128), F32)],
        compiler_params=pltpu.CompilerParams(vmem_limit_bytes=40 * 1024 * 1024),
        name="expert",
    )(rows_in, weight_in, weight_out)


def gather_kernel(gates_ref, x_ref, o_ref, tmp_ref):
    count = gates_ref.shape[1]
    gates = gates_ref[...]
    tmp_ref[...] = x_ref[...].astype(F32)
    for j in range(0, 8, 2):
        x = jnp.concatenate(
            [
                tmp_ref[pl.ds(j, count, stride=8), :].astype(BF),
                tmp_ref[pl.ds(j + 1, count, stride=8), :].astype(BF),
            ],
            axis=1,
        )
        o_ref[:, j * 128 : (j + 2) * 128] = jnp.dot(
            gates, x, preferred_element_type=F32
        ).astype(BF)


def gather(gates, rows):
    count = gates.shape[1]
    return pl.pallas_call(
        gather_kernel,
        out_shape=jax.ShapeDtypeStruct((gates.shape[0], 1024), BF),
        scratch_shapes=[pltpu.VMEM((count * 8, 128), F32)],
        compiler_params=pltpu.CompilerParams(vmem_limit_bytes=40 * 1024 * 1024),
        name="gather",
    )(gates, rows)


def after(value, other):
    first = other[(0,) * other.ndim]
    return value + jnp.where(first > 1 << 30, 1, 0).astype(value.dtype)


def local(
    residual,
    queries,
    key_vectors,
    value_vectors,
    output_weight,
    norm_gain,
    routes,
    gate_levels,
    expert_in,
    expert_out,
):
    tokens, width = residual.shape
    own_x = lax.axis_index("x")
    own_y = lax.axis_index("y2") * 2 + lax.axis_index("y1")
    own_core = lax.axis_index("dp")
    position = jnp.stack([own_x, own_y, own_core]).astype(jnp.int32)

    key_value = jnp.stack(
        [
            jnp.concatenate(
                [key_vectors[:, g : g + HD], value_vectors[:, g : g + HD]], axis=1
            ).reshape(4, 16, 2 * HD)
            for g in (0, HD)
        ],
        axis=1,
    )
    key_value = jnp.broadcast_to(key_value[:, :, None], (4, 2, 4, 16, 2 * HD)).reshape(
        32, 16, 2 * HD
    )
    key_value = lax.all_to_all(key_value, ("x", "z"), split_axis=0, concat_axis=0, tiled=True)
    key_values = lax.all_gather(
        key_value.reshape(512, 2 * HD), ("y2", "y1"), axis=0, tiled=True
    ).reshape(8, 4, 128, 2 * HD)

    query = queries.reshape(tokens, 8, 2 * HD).transpose(1, 0, 2)
    query = jnp.broadcast_to(query[None], (4, 8, tokens, 2 * HD)).reshape(32, tokens, 2 * HD)
    query, _ = lax.optimization_barrier((query, key_value))
    query = lax.all_to_all(query, ("x", "z"), split_axis=0, concat_axis=0, tiled=True).reshape(
        4, 8, tokens, 2 * HD
    )

    head_weight = lax.dynamic_slice_in_dim(output_weight, own_core * HD, HD, 0)
    head_weight, _ = lax.optimization_barrier((head_weight, query))
    gathered = lax.all_gather(head_weight, "z", axis=0, tiled=True)

    own_in, own_out, _ = lax.optimization_barrier((expert_in[0], expert_out[0], query))
    other_in = lax.ppermute(own_in, "y1", SWAP)
    other_out = lax.ppermute(own_out, "y1", SWAP)

    shards = flash(position, query, key_values)
    parts = lax.all_to_all(
        shards.reshape(32, HD + STAT, 128), ("x", "z"), split_axis=0, concat_axis=0, tiled=True
    ).reshape(4, 8, HD + STAT, 128)
    gathered, other_in, other_out = lax.optimization_barrier((gathered, other_in, other_out))
    gathered_other = lax.ppermute(gathered, "dp", SWAP)
    listing = after(jnp.concatenate([routes, gate_levels], axis=1), other_out)
    listing = lax.all_gather(listing, "x", axis=0, tiled=True).reshape(4, tokens, 16)
    named, levels = listing[:, :, 0:8], listing[:, :, 8:16]
    local_expert = jnp.arange(32, dtype=jnp.int32)
    wanted = (local_expert // 4) * 16 + own_x * 4 + local_expert % 4
    match = named[:, :, :, None] == wanted
    hits = jnp.any(match, axis=2)
    gates = jnp.sum(jnp.where(match, levels[:, :, :, None], 0), axis=2).astype(F32) / 256.0
    before = jnp.tril(jnp.ones((tokens, tokens), BF), -1)
    ranks = jnp.einsum(
        "ab,sbq->saq", before, hits.astype(BF), preferred_element_type=F32
    ).astype(jnp.int32)
    ranks = jnp.where(hits, ranks, -1)
    slots = jnp.arange(CAP, dtype=jnp.int32)
    same = jnp.eye(4, dtype=jnp.bool_)
    placed = (ranks.transpose(2, 0, 1)[:, None, None, :, :] == slots[None, None, :, None, None]) & (
        same[None, :, None, :, None]
    )
    chosen = placed.astype(BF).reshape(32 * 4 * CAP, 4 * tokens)
    back = (ranks[:, :, :, None, None] == slots) & same[:, None, None, :, None]
    shares = jnp.where(back, gates[:, :, :, None, None], 0.0).astype(BF)
    shares = shares.reshape(4 * tokens, 32 * 4 * CAP)

    half = own_in.shape[1] // 2
    weight_in = jnp.concatenate(
        [own_in[:, :half], other_in[:, :half], own_in[:, half:], other_in[:, half:]], axis=1
    )
    weight_out = jnp.concatenate([own_out, other_out], axis=0)
    hidden, spread = merge(
        position, parts, gathered, gathered_other, residual, norm_gain.reshape(1, width)
    )

    spread = lax.all_to_all(spread, "x", split_axis=0, concat_axis=0, tiled=True)
    outgoing = select(chosen, spread.reshape(4 * tokens, width))
    arrived = lax.all_to_all(
        outgoing.reshape(32, 4 * CAP * 8, 128), ("z", "y2"), split_axis=0, concat_axis=0, tiled=True
    )
    done = expert(arrived.reshape(-1, 128), weight_in, weight_out)
    answers = lax.all_to_all(
        done.reshape(32, 4 * CAP * 8, 128), ("z", "y2"), split_axis=0, concat_axis=0, tiled=True
    )
    sums = gather(shares, answers.reshape(-1, 128))
    sums = lax.all_to_all(
        sums.reshape(4, tokens, width), "x", split_axis=0, concat_axis=0, tiled=True
    )
    return hidden + jnp.sum(sums.astype(F32), axis=0)


def solution(mesh):
    fine = Mesh(mesh.devices.reshape(8, 4, 4, 2, 2), ("z", "x", "y2", "y1", "dp"))
    rows = P(("dp", "x", "y2", "y1", "z"), None)
    halves = P(("z", "x", "y2", "y1"), None, None)
    return jax.shard_map(
        local,
        mesh=fine,
        in_specs=(rows, rows, rows, rows, P("z", None), P(), rows, rows, halves, halves),
        out_specs=rows,
        check_vma=False,
    )
```

```python
import math

import jax
import jax.numpy as jnp
from jax import lax
from jax.experimental import pallas as pl
from jax.experimental.pallas import tpu as pltpu
from jax.sharding import Mesh
from jax.sharding import PartitionSpec as P

HD = 128
CAP = 5
LOG2E = 1.4426950408889634
BF = jnp.bfloat16
F32 = jnp.float32
NEG = -1e30
LOW = -1e29
STAT = 8
SWAP = [(0, 1), (1, 0)]


def flash_kernel(
    pos_ref, q_ref, b0, b1, b2, b3, b4, b5, b6, b7, b8, o_ref, kv_ref, vt_ref, bias_ref, acc_ref, m_ref, top_ref
):
    block = pl.program_id(0)
    own_x = pos_ref[0]
    own_y = pos_ref[1]
    cols = 1024
    scale = LOG2E / math.sqrt(HD)

    def keys(c):
        return kv_ref[pl.ds(4 * (c % 2), 4), c // 2, :, 0:HD].reshape(512, HD)

    @pl.when(block == 0)
    def _():
        eye = (
            lax.broadcasted_iota(jnp.int32, (HD, HD), 0)
            == lax.broadcasted_iota(jnp.int32, (HD, HD), 1)
        ).astype(BF)
        for far, ref in ((0, b0), (7, b1), (6, b2), (5, b3), (1, b4), (2, b5), (3, b6)):
            kv_ref[(own_y + far) % 8] = ref[...]
        kv_ref[(own_y + 4) % 8, 0:2] = b7[...]
        kv_ref[(own_y + 4) % 8, 2:4] = b8[...]
        for c in range(8):
            v = kv_ref[4 * (c % 2) : 4 * (c % 2) + 4, c // 2, :, HD : 2 * HD].reshape(512, HD)
            turned = lax.dot_general(eye, v, (((1,), (1,)), ((), ())), preferred_element_type=F32)
            vt_ref[c, 0:HD, :] = turned.astype(BF)
            vt_ref[c, HD : HD + 16, :] = jnp.ones((16, 512), BF)
        row = lax.broadcasted_iota(jnp.int32, (512, 128), 0)
        col = lax.broadcasted_iota(jnp.int32, (512, 128), 1)
        inner = row % 128
        key_pos = (
            (row // 128 - own_y % 4) * 512 + (inner // 16) * 64 + inner % 16 + 16 * own_x - col % 64
        )
        for z in range(8):
            bias_ref[:, z * 128 : (z + 1) * 128] = jnp.where(key_pos <= z * 64, 0.0, NEG)

    tiles = block * 8 + own_y
    chunk_count = tiles // 4
    q_raw = q_ref[0]
    q = jnp.concatenate([q_raw[:, :, 0:HD], q_raw[:, :, HD : 2 * HD]], axis=1).reshape(cols, HD)
    group = 1024
    groups = [(g * group, q[g * group : (g + 1) * group]) for g in range(cols // group)]

    def scores(k, q_group):
        return lax.dot_general(k, q_group, (((1,), (1,)), ((), ())), preferred_element_type=F32)

    first_keys = kv_ref[0, 0, :, 0:HD]
    hide = jnp.where(tiles == 0, 1.0, 0.0)
    for start, q_group in groups:
        part = slice(start, start + group)
        s = scores(first_keys, q_group) + bias_ref[0:128, part] * hide
        m_ref[:, part] = jnp.maximum(jnp.max(s, axis=0, keepdims=True), LOW)
        top_ref[:, part] = jnp.max(s.reshape(16, 8, group), axis=0)
        acc_ref[:, part] = jnp.zeros((HD + 16, group), F32)

    def quick(c, masked):
        k = keys(c)
        values = vt_ref[c]
        found = [scores(k, q_group) for _, q_group in groups]
        for (start, _), s in zip(groups, found):
            part = slice(start, start + group)
            if masked:
                s = s + bias_ref[:, part]
            p = jnp.exp2(s * scale - m_ref[:, part] * scale).astype(BF)
            top_ref[:, part] = jnp.maximum(
                top_ref[:, part], jnp.max(s.reshape(64, 8, group), axis=0)
            )
            acc_ref[:, part] = acc_ref[:, part] + jnp.dot(values, p, preferred_element_type=F32)

    def quick_step(c, carry):
        quick(c, False)
        return carry

    lax.fori_loop(0, chunk_count, quick_step, 0)
    quick(chunk_count, True)

    def careful(c, masked):
        k = keys(c)
        values = vt_ref[c]
        for start, q_group in groups:
            part = slice(start, start + group)
            s = scores(k, q_group)
            if masked:
                s = s + bias_ref[:, part]
            m_old = m_ref[:, part]
            m = jnp.maximum(m_old, jnp.max(s, axis=0, keepdims=True))
            p = jnp.exp2((s - m) * scale).astype(BF)
            alpha = jnp.exp2((m_old - m) * scale)
            m_ref[:, part] = m
            acc_ref[:, part] = acc_ref[:, part] * alpha + jnp.dot(
                values, p, preferred_element_type=F32
            )

    def careful_step(c, carry):
        careful(c, False)
        return carry

    rise = jnp.max((top_ref[...] - m_ref[...]) * scale)

    @pl.when(rise > 64.0)
    def _():
        m_ref[...] = jnp.full((1, cols), LOW, F32)
        acc_ref[...] = jnp.zeros((HD + 16, cols), F32)
        lax.fori_loop(0, chunk_count, careful_step, 0)
        careful(chunk_count, True)

    total = acc_ref[HD : HD + 1, :]
    seen = total > 0.0
    safe = jnp.where(seen, total, 1.0)
    out = (acc_ref[0:HD, :] * (1.0 / safe)).astype(BF)
    level = jnp.where(seen, m_ref[...] * scale + jnp.log(safe) * LOG2E, NEG)
    first = level.astype(BF).astype(F32)
    second = (level - first).astype(BF).astype(F32)
    third = level - first - second
    pick = lax.broadcasted_iota(jnp.int32, (STAT, cols), 0)
    stats = jnp.where(pick == 0, first, jnp.where(pick == 1, second, jnp.where(pick == 2, third, 0.0)))
    stats = stats.astype(BF)
    for i in range(8):
        o_ref[0, i, 0:HD, :] = out[:, i * 128 : (i + 1) * 128]
        o_ref[0, i, HD : HD + STAT, :] = stats[:, i * 128 : (i + 1) * 128]


def flash(position, queries, key_values):
    return pl.pallas_call(
        flash_kernel,
        grid_spec=pltpu.PrefetchScalarGridSpec(
            num_scalar_prefetch=1,
            grid=(4,),
            in_specs=[
                pl.BlockSpec((1, 8, 64, 256), lambda i, s: (i, 0, 0, 0)),
            ]
            + [pl.BlockSpec(block.shape, lambda i, s: (0, 0, 0)) for block in key_values],
            out_specs=pl.BlockSpec((1, 8, HD + STAT, 128), lambda i, s: (i, 0, 0, 0)),
            scratch_shapes=[
                pltpu.VMEM((8, 4, 128, 2 * HD), BF),
                pltpu.VMEM((8, HD + 16, 512), BF),
                pltpu.VMEM((512, 1024), F32),
                pltpu.VMEM((HD + 16, 1024), F32),
                pltpu.VMEM((1, 1024), F32),
                pltpu.VMEM((8, 1024), F32),
            ],
        ),
        out_shape=jax.ShapeDtypeStruct((4, 8, HD + STAT, 128), BF),
        compiler_params=pltpu.CompilerParams(vmem_limit_bytes=40 * 1024 * 1024),
        cost_estimate=pl.CostEstimate(
            flops=4 * 4096 * 2560 * HD, bytes_accessed=5 << 20, transcendentals=4096 * 2560
        ),
        name="flash",
    )(position, queries, *key_values)


def merged_heads(pos_ref, parts_ref, second):
    found = []
    for c in range(2):
        levels = []
        for x in range(4):
            st = parts_ref[x, c, HD : HD + STAT, :].astype(F32)
            levels.append(st[0:1] + st[1:2] + st[2:3])
        top = jnp.maximum(jnp.maximum(levels[0], levels[1]), jnp.maximum(levels[2], levels[3]))
        shares = [jnp.exp2(level - top) for level in levels]
        inverse = 1.0 / (shares[0] + shares[1] + shares[2] + shares[3])
        mixed = parts_ref[0, c, 0:HD, :].astype(F32) * (shares[0] * inverse)
        for x in range(1, 4):
            mixed = mixed + parts_ref[x, c, 0:HD, :].astype(F32) * (shares[x] * inverse)
        rows = mixed.T.astype(BF)
        found.append(jnp.where((pos_ref[2] == 0) != second, rows[0:64], rows[64:128]))
    return jnp.concatenate(found, axis=1)


def merge_own_kernel(pos_ref, parts_ref, w_ref, res_ref, o_ref):
    part = jnp.dot(merged_heads(pos_ref, parts_ref, False), w_ref[...], preferred_element_type=F32)

    @pl.when(pl.program_id(0) == 0)
    def _():
        o_ref[...] = res_ref[...].astype(F32) + part

    @pl.when(pl.program_id(0) > 0)
    def _():
        o_ref[...] = o_ref[...] + part


def merge_other_kernel(pos_ref, parts_ref, w_ref, sum_ref, gain_ref, hidden_ref, normed_ref):
    step = pl.program_id(0)
    part = jnp.dot(merged_heads(pos_ref, parts_ref, True), w_ref[...], preferred_element_type=F32)

    @pl.when(step == 0)
    def _():
        hidden_ref[...] = sum_ref[...] + part

    @pl.when(step > 0)
    def _():
        hidden_ref[...] = hidden_ref[...] + part

    @pl.when(step == 3)
    def _():
        hidden = hidden_ref[...]
        mean_square = jnp.mean(hidden * hidden, axis=1, keepdims=True)
        normed = (hidden * lax.rsqrt(mean_square + 1e-6) * gain_ref[...]).astype(BF)
        for x in range(4):
            normed_ref[x] = normed


def merge_specs(tokens, width):
    return [
        pl.BlockSpec((4, 2, HD + STAT, 128), lambda c, s: (0, c, 0, 0)),
        pl.BlockSpec((256, width), lambda c, s: (c, 0)),
        pl.BlockSpec((tokens, width), lambda c, s: (0, 0)),
    ]


def merge(position, parts, weight, weight_other, residual, gain):
    tokens, width = residual.shape
    whole = pl.BlockSpec((tokens, width), lambda c, s: (0, 0))
    half_sum = pl.pallas_call(
        merge_own_kernel,
        grid_spec=pltpu.PrefetchScalarGridSpec(
            num_scalar_prefetch=1,
            grid=(4,),
            in_specs=merge_specs(tokens, width),
            out_specs=whole,
        ),
        out_shape=jax.ShapeDtypeStruct((tokens, width), F32),
        name="merge_own",
    )(position, parts, weight, residual)
    return pl.pallas_call(
        merge_other_kernel,
        grid_spec=pltpu.PrefetchScalarGridSpec(
            num_scalar_prefetch=1,
            grid=(4,),
            in_specs=merge_specs(tokens, width) + [pl.BlockSpec((1, width), lambda c, s: (0, 0))],
            out_specs=[whole, pl.BlockSpec((4, tokens, width), lambda c, s: (0, 0, 0))],
        ),
        out_shape=[
            jax.ShapeDtypeStruct((tokens, width), F32),
            jax.ShapeDtypeStruct((4, tokens, width), BF),
        ],
        name="merge_other",
    )(position, parts, weight_other, half_sum, gain)


def select_kernel(sel_ref, x_ref, o_ref, tmp_ref):
    count = sel_ref.shape[0]
    sel = sel_ref[...]
    for j in range(0, 8, 2):
        got = jnp.dot(sel, x_ref[:, j * 128 : (j + 2) * 128], preferred_element_type=F32)
        tmp_ref[pl.ds(j, count, stride=8), :] = got[:, 0:128]
        tmp_ref[pl.ds(j + 1, count, stride=8), :] = got[:, 128:256]
    o_ref[...] = tmp_ref[...].astype(BF)


def select(chosen, tokens):
    count = chosen.shape[0]
    return pl.pallas_call(
        select_kernel,
        out_shape=jax.ShapeDtypeStruct((count * 8, 128), BF),
        scratch_shapes=[pltpu.VMEM((count * 8, 128), F32)],
        compiler_params=pltpu.CompilerParams(vmem_limit_bytes=40 * 1024 * 1024),
        name="select",
    )(chosen, tokens)


def expert_kernel(x_ref, win_ref, wout_ref, o_ref, tmp_ref):
    rows = x_ref.shape[0] // 8
    inner = wout_ref.shape[0]
    tmp_ref[...] = x_ref[...].astype(F32)
    x = jnp.concatenate(
        [tmp_ref[pl.ds(j, rows, stride=8), :].astype(BF) for j in range(8)], axis=1
    )
    projection = jnp.dot(x, win_ref[...], preferred_element_type=F32)
    gate = projection[:, 0:inner]
    activated = (gate / (1.0 + jnp.exp(-gate)) * projection[:, inner:]).astype(BF)
    out = jnp.dot(activated, wout_ref[...], preferred_element_type=F32)
    for j in range(8):
        tmp_ref[pl.ds(j, rows, stride=8), :] = out[:, j * 128 : (j + 1) * 128]
    o_ref[...] = tmp_ref[...].astype(BF)


def expert(rows_in, weight_in, weight_out):
    total = rows_in.shape[0]
    block = total // 4
    return pl.pallas_call(
        expert_kernel,
        grid=(4,),
        in_specs=[
            pl.BlockSpec((block, 128), lambda i: (i, 0)),
            pl.BlockSpec(weight_in.shape, lambda i: (0, 0)),
            pl.BlockSpec(weight_out.shape, lambda i: (0, 0)),
        ],
        out_specs=pl.BlockSpec((block, 128), lambda i: (i, 0)),
        out_shape=jax.ShapeDtypeStruct((total, 128), BF),
        scratch_shapes=[pltpu.VMEM((block, 128), F32)],
        compiler_params=pltpu.CompilerParams(vmem_limit_bytes=40 * 1024 * 1024),
        name="expert",
    )(rows_in, weight_in, weight_out)


def gather_kernel(gates_ref, x_ref, o_ref, tmp_ref):
    count = gates_ref.shape[1]
    gates = gates_ref[...]
    tmp_ref[...] = x_ref[...].astype(F32)
    for j in range(0, 8, 2):
        x = jnp.concatenate(
            [
                tmp_ref[pl.ds(j, count, stride=8), :].astype(BF),
                tmp_ref[pl.ds(j + 1, count, stride=8), :].astype(BF),
            ],
            axis=1,
        )
        o_ref[:, j * 128 : (j + 2) * 128] = jnp.dot(
            gates, x, preferred_element_type=F32
        ).astype(BF)


def gather(gates, rows):
    count = gates.shape[1]
    return pl.pallas_call(
        gather_kernel,
        out_shape=jax.ShapeDtypeStruct((gates.shape[0], 1024), BF),
        scratch_shapes=[pltpu.VMEM((count * 8, 128), F32)],
        compiler_params=pltpu.CompilerParams(vmem_limit_bytes=40 * 1024 * 1024),
        name="gather",
    )(gates, rows)


def after(value, other):
    first = other[(0,) * other.ndim]
    return value + jnp.where(first > 1 << 30, 1, 0).astype(value.dtype)


def local(
    residual,
    queries,
    key_vectors,
    value_vectors,
    output_weight,
    norm_gain,
    routes,
    gate_levels,
    expert_in,
    expert_out,
):
    tokens, width = residual.shape
    own_x = lax.axis_index("x")
    own_y = lax.axis_index("y2") * 2 + lax.axis_index("y1")
    own_core = lax.axis_index("dp")
    position = jnp.stack([own_x, own_y, own_core]).astype(jnp.int32)

    key_value = jnp.stack(
        [
            jnp.concatenate(
                [key_vectors[:, g : g + HD], value_vectors[:, g : g + HD]], axis=1
            ).reshape(4, 16, 2 * HD)
            for g in (0, HD)
        ],
        axis=1,
    )
    key_value = jnp.broadcast_to(key_value[:, :, None], (4, 2, 4, 16, 2 * HD)).reshape(
        32, 16, 2 * HD
    )
    key_value = lax.all_to_all(key_value, ("x", "z"), split_axis=0, concat_axis=0, tiled=True)
    up = [(i, (i + 1) % 8) for i in range(8)]
    down = [(i, (i - 1) % 8) for i in range(8)]
    ups, downs = [key_value.reshape(4, 128, 2 * HD)], [key_value.reshape(4, 128, 2 * HD)]
    for _ in range(3):
        ups.append(lax.ppermute(ups[-1], ("y2", "y1"), up))
        downs.append(lax.ppermute(downs[-1], ("y2", "y1"), down))
    key_values = ups + downs[1:]
    key_values.append(lax.ppermute(ups[3][0:2], ("y2", "y1"), up))
    key_values.append(lax.ppermute(downs[3][2:4], ("y2", "y1"), down))

    query = queries.reshape(tokens, 8, 2 * HD).transpose(1, 0, 2)
    query = jnp.broadcast_to(query[None], (4, 8, tokens, 2 * HD)).reshape(32, tokens, 2 * HD)
    query, _ = lax.optimization_barrier((query, key_value))
    query = lax.all_to_all(query, ("x", "z"), split_axis=0, concat_axis=0, tiled=True).reshape(
        4, 8, tokens, 2 * HD
    )

    head_weight = lax.dynamic_slice_in_dim(output_weight, own_core * HD, HD, 0)
    gathered = lax.all_gather(head_weight, "z", axis=0, tiled=True)

    shards = flash(position, query, key_values)
    parts = lax.all_to_all(
        shards.reshape(32, HD + STAT, 128), ("x", "z"), split_axis=0, concat_axis=0, tiled=True
    ).reshape(4, 8, HD + STAT, 128)
    gathered, own_in, own_out = lax.optimization_barrier((gathered, expert_in[0], expert_out[0]))
    gathered_other = lax.ppermute(gathered, "dp", SWAP)
    other_in = lax.ppermute(own_in, "y1", SWAP)
    other_out = lax.ppermute(own_out, "y1", SWAP)
    listing = after(jnp.concatenate([routes, gate_levels], axis=1), gathered)
    listing = lax.all_gather(listing, "x", axis=0, tiled=True).reshape(4, tokens, 16)
    named, levels = listing[:, :, 0:8], listing[:, :, 8:16]
    local_expert = jnp.arange(32, dtype=jnp.int32)
    wanted = (local_expert // 4) * 16 + own_x * 4 + local_expert % 4
    match = named[:, :, :, None] == wanted
    hits = jnp.any(match, axis=2)
    gates = jnp.sum(jnp.where(match, levels[:, :, :, None], 0), axis=2).astype(F32) / 256.0
    before = jnp.tril(jnp.ones((tokens, tokens), BF), -1)
    ranks = jnp.einsum(
        "ab,sbq->saq", before, hits.astype(BF), preferred_element_type=F32
    ).astype(jnp.int32)
    ranks = jnp.where(hits, ranks, -1)
    slots = jnp.arange(CAP, dtype=jnp.int32)
    same = jnp.eye(4, dtype=jnp.bool_)
    placed = (ranks.transpose(2, 0, 1)[:, None, None, :, :] == slots[None, None, :, None, None]) & (
        same[None, :, None, :, None]
    )
    chosen = placed.astype(BF).reshape(32 * 4 * CAP, 4 * tokens)
    back = (ranks[:, :, :, None, None] == slots) & same[:, None, None, :, None]
    shares = jnp.where(back, gates[:, :, :, None, None], 0.0).astype(BF)
    shares = shares.reshape(4 * tokens, 32 * 4 * CAP)

    hidden, spread = merge(
        position, parts, gathered, gathered_other, residual, norm_gain.reshape(1, width)
    )

    spread, other_in, other_out = lax.optimization_barrier((spread, other_in, other_out))
    half = own_in.shape[1] // 2
    weight_in = jnp.concatenate(
        [own_in[:, :half], other_in[:, :half], own_in[:, half:], other_in[:, half:]], axis=1
    )
    weight_out = jnp.concatenate([own_out, other_out], axis=0)
    spread = lax.all_to_all(spread, "x", split_axis=0, concat_axis=0, tiled=True)
    outgoing = select(chosen, spread.reshape(4 * tokens, width))
    arrived = lax.all_to_all(
        outgoing.reshape(32, 4 * CAP * 8, 128), ("z", "y2"), split_axis=0, concat_axis=0, tiled=True
    )
    done = expert(arrived.reshape(-1, 128), weight_in, weight_out)
    answers = lax.all_to_all(
        done.reshape(32, 4 * CAP * 8, 128), ("z", "y2"), split_axis=0, concat_axis=0, tiled=True
    )
    sums = gather(shares, answers.reshape(-1, 128))
    sums = lax.all_to_all(
        sums.reshape(4, tokens, width), "x", split_axis=0, concat_axis=0, tiled=True
    )
    return hidden + jnp.sum(sums.astype(F32), axis=0)


def solution(mesh):
    fine = Mesh(mesh.devices.reshape(8, 4, 4, 2, 2), ("z", "x", "y2", "y1", "dp"))
    rows = P(("dp", "x", "y2", "y1", "z"), None)
    halves = P(("z", "x", "y2", "y1"), None, None)
    return jax.shard_map(
        local,
        mesh=fine,
        in_specs=(rows, rows, rows, rows, P("z", None), P(), rows, rows, halves, halves),
        out_specs=rows,
        check_vma=False,
    )
```

```python
import math

import jax
import jax.numpy as jnp
from jax import lax
from jax.experimental import pallas as pl
from jax.experimental.pallas import tpu as pltpu
from jax.sharding import Mesh
from jax.sharding import PartitionSpec as P

HD = 128
CAP = 5
LOG2E = 1.4426950408889634
BF = jnp.bfloat16
F32 = jnp.float32
NEG = -1e30
LOW = -1e29
STAT = 8
SWAP = [(0, 1), (1, 0)]


def flash_kernel(
    pos_ref, q_ref, b0, b1, b2, b3, b4, b5, b6, b7, b8, o_ref, kv_ref, vt_ref, bias_ref, acc_ref, m_ref, top_ref
):
    block = pl.program_id(0)
    own_x = pos_ref[0]
    own_y = pos_ref[1]
    cols = 1024
    scale = LOG2E / math.sqrt(HD)

    def keys(c):
        return kv_ref[pl.ds(4 * (c % 2), 4), c // 2, :, 0:HD].reshape(512, HD)

    @pl.when(block == 0)
    def _():
        eye = (
            lax.broadcasted_iota(jnp.int32, (HD, HD), 0)
            == lax.broadcasted_iota(jnp.int32, (HD, HD), 1)
        ).astype(BF)
        for far, ref in ((0, b0), (7, b1), (6, b2), (5, b3), (1, b4), (2, b5), (3, b6)):
            kv_ref[(own_y + far) % 8] = ref[0:512, :].reshape(4, 128, 2 * HD)
        kv_ref[(own_y + 4) % 8, 0:2] = b7[...].reshape(2, 128, 2 * HD)
        kv_ref[(own_y + 4) % 8, 2:4] = b8[0:256, :].reshape(2, 128, 2 * HD)
        for c in range(8):
            v = kv_ref[4 * (c % 2) : 4 * (c % 2) + 4, c // 2, :, HD : 2 * HD].reshape(512, HD)
            turned = lax.dot_general(eye, v, (((1,), (1,)), ((), ())), preferred_element_type=F32)
            vt_ref[c, 0:HD, :] = turned.astype(BF)
            vt_ref[c, HD : HD + 16, :] = jnp.ones((16, 512), BF)
        row = lax.broadcasted_iota(jnp.int32, (512, 128), 0)
        col = lax.broadcasted_iota(jnp.int32, (512, 128), 1)
        inner = row % 128
        key_pos = (
            (row // 128 - own_y % 4) * 512 + (inner // 16) * 64 + inner % 16 + 16 * own_x - col % 64
        )
        for z in range(8):
            bias_ref[:, z * 128 : (z + 1) * 128] = jnp.where(key_pos <= z * 64, 0.0, NEG)

    tiles = block * 8 + own_y
    chunk_count = tiles // 4
    q_raw = q_ref[0]
    q = jnp.concatenate([q_raw[:, :, 0:HD], q_raw[:, :, HD : 2 * HD]], axis=1).reshape(cols, HD)
    group = 1024
    groups = [(g * group, q[g * group : (g + 1) * group]) for g in range(cols // group)]

    def scores(k, q_group):
        return lax.dot_general(k, q_group, (((1,), (1,)), ((), ())), preferred_element_type=F32)

    first_keys = kv_ref[0, 0, :, 0:HD]
    hide = jnp.where(tiles == 0, 1.0, 0.0)
    for start, q_group in groups:
        part = slice(start, start + group)
        s = scores(first_keys, q_group) + bias_ref[0:128, part] * hide
        m_ref[:, part] = jnp.maximum(jnp.max(s, axis=0, keepdims=True), LOW)
        top_ref[:, part] = jnp.max(s.reshape(16, 8, group), axis=0)
        acc_ref[:, part] = jnp.zeros((HD + 16, group), F32)

    def quick(c, masked):
        k = keys(c)
        values = vt_ref[c]
        found = [scores(k, q_group) for _, q_group in groups]
        for (start, _), s in zip(groups, found):
            part = slice(start, start + group)
            if masked:
                s = s + bias_ref[:, part]
            p = jnp.exp2(s * scale - m_ref[:, part] * scale).astype(BF)
            top_ref[:, part] = jnp.maximum(
                top_ref[:, part], jnp.max(s.reshape(64, 8, group), axis=0)
            )
            acc_ref[:, part] = acc_ref[:, part] + jnp.dot(values, p, preferred_element_type=F32)

    def quick_step(c, carry):
        quick(c, False)
        return carry

    lax.fori_loop(0, chunk_count, quick_step, 0)
    quick(chunk_count, True)

    def careful(c, masked):
        k = keys(c)
        values = vt_ref[c]
        for start, q_group in groups:
            part = slice(start, start + group)
            s = scores(k, q_group)
            if masked:
                s = s + bias_ref[:, part]
            m_old = m_ref[:, part]
            m = jnp.maximum(m_old, jnp.max(s, axis=0, keepdims=True))
            p = jnp.exp2((s - m) * scale).astype(BF)
            alpha = jnp.exp2((m_old - m) * scale)
            m_ref[:, part] = m
            acc_ref[:, part] = acc_ref[:, part] * alpha + jnp.dot(
                values, p, preferred_element_type=F32
            )

    def careful_step(c, carry):
        careful(c, False)
        return carry

    rise = jnp.max((top_ref[...] - m_ref[...]) * scale)

    @pl.when(rise > 64.0)
    def _():
        m_ref[...] = jnp.full((1, cols), LOW, F32)
        acc_ref[...] = jnp.zeros((HD + 16, cols), F32)
        lax.fori_loop(0, chunk_count, careful_step, 0)
        careful(chunk_count, True)

    total = acc_ref[HD : HD + 1, :]
    seen = total > 0.0
    safe = jnp.where(seen, total, 1.0)
    out = (acc_ref[0:HD, :] * (1.0 / safe)).astype(BF)
    level = jnp.where(seen, m_ref[...] * scale + jnp.log(safe) * LOG2E, NEG)
    first = level.astype(BF).astype(F32)
    second = (level - first).astype(BF).astype(F32)
    third = level - first - second
    pick = lax.broadcasted_iota(jnp.int32, (STAT, cols), 0)
    stats = jnp.where(pick == 0, first, jnp.where(pick == 1, second, jnp.where(pick == 2, third, 0.0)))
    stats = stats.astype(BF)
    for i in range(8):
        o_ref[0, i, 0:HD, :] = out[:, i * 128 : (i + 1) * 128]
        o_ref[0, i, HD : HD + STAT, :] = stats[:, i * 128 : (i + 1) * 128]


def flash(position, queries, key_values):
    return pl.pallas_call(
        flash_kernel,
        grid_spec=pltpu.PrefetchScalarGridSpec(
            num_scalar_prefetch=1,
            grid=(4,),
            in_specs=[
                pl.BlockSpec((1, 8, 64, 256), lambda i, s: (i, 0, 0, 0)),
            ]
            + [pl.BlockSpec(block.shape, lambda i, s: (0, 0)) for block in key_values],
            out_specs=pl.BlockSpec((1, 8, HD + STAT, 128), lambda i, s: (i, 0, 0, 0)),
            scratch_shapes=[
                pltpu.VMEM((8, 4, 128, 2 * HD), BF),
                pltpu.VMEM((8, HD + 16, 512), BF),
                pltpu.VMEM((512, 1024), F32),
                pltpu.VMEM((HD + 16, 1024), F32),
                pltpu.VMEM((1, 1024), F32),
                pltpu.VMEM((8, 1024), F32),
            ],
        ),
        out_shape=jax.ShapeDtypeStruct((4, 8, HD + STAT, 128), BF),
        compiler_params=pltpu.CompilerParams(vmem_limit_bytes=40 * 1024 * 1024),
        cost_estimate=pl.CostEstimate(
            flops=4 * 4096 * 2560 * HD, bytes_accessed=5 << 20, transcendentals=4096 * 2560
        ),
        name="flash",
    )(position, queries, *key_values)


def merge_kernel(parts_ref, w_ref, res_ref, gain_ref, hidden_ref, normed_ref):
    step = pl.program_id(0)
    found = []
    for c in range(2):
        levels = []
        for x in range(4):
            st = parts_ref[x, c, HD : HD + STAT, :].astype(F32)
            levels.append(st[0:1] + st[1:2] + st[2:3])
        top = jnp.maximum(jnp.maximum(levels[0], levels[1]), jnp.maximum(levels[2], levels[3]))
        shares = [jnp.exp2(level - top) for level in levels]
        inverse = 1.0 / (shares[0] + shares[1] + shares[2] + shares[3])
        mixed = parts_ref[0, c, 0:HD, :].astype(F32) * (shares[0] * inverse)
        for x in range(1, 4):
            mixed = mixed + parts_ref[x, c, 0:HD, :].astype(F32) * (shares[x] * inverse)
        rows = mixed.T.astype(BF)
        found += [rows[0:64], rows[64:128]]
    part = jnp.dot(jnp.concatenate(found, axis=1), w_ref[...], preferred_element_type=F32)

    @pl.when(step == 0)
    def _():
        hidden_ref[...] = res_ref[...].astype(F32) + part

    @pl.when(step > 0)
    def _():
        hidden_ref[...] = hidden_ref[...] + part

    @pl.when(step == 3)
    def _():
        hidden = hidden_ref[...]
        mean_square = jnp.mean(hidden * hidden, axis=1, keepdims=True)
        normed = (hidden * lax.rsqrt(mean_square + 1e-6) * gain_ref[...]).astype(BF)
        for i in range(4):
            normed_ref[i] = normed


def merge(parts, weight, residual, gain):
    tokens, width = residual.shape
    whole = pl.BlockSpec((tokens, width), lambda c: (0, 0))
    return pl.pallas_call(
        merge_kernel,
        grid=(4,),
        in_specs=[
            pl.BlockSpec((4, 2, HD + STAT, 128), lambda c: (0, c, 0, 0)),
            pl.BlockSpec((512, width), lambda c: (c, 0)),
            whole,
            pl.BlockSpec((1, width), lambda c: (0, 0)),
        ],
        out_specs=[whole, pl.BlockSpec((4, tokens, width), lambda c: (0, 0, 0))],
        out_shape=[
            jax.ShapeDtypeStruct((tokens, width), F32),
            jax.ShapeDtypeStruct((4, tokens, width), BF),
        ],
        name="merge",
    )(parts, weight, residual, gain)


def select_kernel(sel_ref, x_ref, o_ref, tmp_ref):
    count = sel_ref.shape[0]
    sel = sel_ref[...]
    for j in range(0, 8, 2):
        got = jnp.dot(sel, x_ref[:, j * 128 : (j + 2) * 128], preferred_element_type=F32)
        tmp_ref[pl.ds(j, count, stride=8), :] = got[:, 0:128]
        tmp_ref[pl.ds(j + 1, count, stride=8), :] = got[:, 128:256]
    o_ref[...] = tmp_ref[...].astype(BF)


def select(chosen, tokens):
    count = chosen.shape[0]
    return pl.pallas_call(
        select_kernel,
        out_shape=jax.ShapeDtypeStruct((count * 8, 128), BF),
        scratch_shapes=[pltpu.VMEM((count * 8, 128), F32)],
        compiler_params=pltpu.CompilerParams(vmem_limit_bytes=40 * 1024 * 1024),
        name="select",
    )(chosen, tokens)


def expert_kernel(x_ref, win_ref, wout_ref, o_ref, tmp_ref):
    rows = x_ref.shape[0] // 8
    inner = wout_ref.shape[0]
    tmp_ref[...] = x_ref[...].astype(F32)
    x = jnp.concatenate(
        [tmp_ref[pl.ds(j, rows, stride=8), :].astype(BF) for j in range(8)], axis=1
    )
    projection = jnp.dot(x, win_ref[...], preferred_element_type=F32)
    gate = projection[:, 0:inner]
    activated = (gate / (1.0 + jnp.exp(-gate)) * projection[:, inner:]).astype(BF)
    out = jnp.dot(activated, wout_ref[...], preferred_element_type=F32)
    for j in range(8):
        tmp_ref[pl.ds(j, rows, stride=8), :] = out[:, j * 128 : (j + 1) * 128]
    o_ref[...] = tmp_ref[...].astype(BF)


def expert(rows_in, weight_in, weight_out):
    total = rows_in.shape[0]
    block = total // 4
    return pl.pallas_call(
        expert_kernel,
        grid=(4,),
        in_specs=[
            pl.BlockSpec((block, 128), lambda i: (i, 0)),
            pl.BlockSpec(weight_in.shape, lambda i: (0, 0)),
            pl.BlockSpec(weight_out.shape, lambda i: (0, 0)),
        ],
        out_specs=pl.BlockSpec((block, 128), lambda i: (i, 0)),
        out_shape=jax.ShapeDtypeStruct((total, 128), BF),
        scratch_shapes=[pltpu.VMEM((block, 128), F32)],
        compiler_params=pltpu.CompilerParams(vmem_limit_bytes=40 * 1024 * 1024),
        name="expert",
    )(rows_in, weight_in, weight_out)


def gather_kernel(gates_ref, x_ref, o_ref, tmp_ref):
    count = gates_ref.shape[1]
    gates = gates_ref[...]
    tmp_ref[...] = x_ref[...].astype(F32)
    for j in range(0, 8, 2):
        x = jnp.concatenate(
            [
                tmp_ref[pl.ds(j, count, stride=8), :].astype(BF),
                tmp_ref[pl.ds(j + 1, count, stride=8), :].astype(BF),
            ],
            axis=1,
        )
        o_ref[:, j * 128 : (j + 2) * 128] = jnp.dot(
            gates, x, preferred_element_type=F32
        ).astype(BF)


def gather(gates, rows):
    count = gates.shape[1]
    return pl.pallas_call(
        gather_kernel,
        out_shape=jax.ShapeDtypeStruct((gates.shape[0], 1024), BF),
        scratch_shapes=[pltpu.VMEM((count * 8, 128), F32)],
        compiler_params=pltpu.CompilerParams(vmem_limit_bytes=40 * 1024 * 1024),
        name="gather",
    )(gates, rows)


def local(
    residual,
    queries,
    key_vectors,
    value_vectors,
    output_weight,
    norm_gain,
    routes,
    gate_levels,
    expert_in,
    expert_out,
):
    tokens, width = residual.shape
    own_x = lax.axis_index("x")
    own_y2 = lax.axis_index("y2")
    own_y = own_y2 * 2 + lax.axis_index("y1")
    position = jnp.stack([own_x, own_y]).astype(jnp.int32)

    key_value = jnp.stack(
        [
            jnp.concatenate(
                [key_vectors[:, g : g + HD], value_vectors[:, g : g + HD]], axis=1
            ).reshape(4, 16, 2 * HD)
            for g in (0, HD)
        ],
        axis=1,
    )
    key_value = jnp.broadcast_to(key_value[:, :, None], (4, 2, 4, 16, 2 * HD)).reshape(
        32, 16, 2 * HD
    )
    key_value = lax.all_to_all(key_value, ("x", "z"), split_axis=0, concat_axis=0, tiled=True)
    listing = jnp.concatenate([routes.T, gate_levels.T], axis=0).astype(BF)
    listing = jnp.pad(listing, ((0, 0), (0, 2 * HD - tokens)))
    block = jnp.concatenate([key_value.reshape(512, 2 * HD), listing], axis=0)
    up = [(i, (i + 1) % 8) for i in range(8)]
    down = [(i, (i - 1) % 8) for i in range(8)]
    ups, downs = [block], [block]
    for _ in range(3):
        ups.append(lax.ppermute(ups[-1], ("y2", "y1"), up))
        downs.append(lax.ppermute(downs[-1], ("y2", "y1"), down))
    key_values = ups + downs[1:]
    key_values.append(lax.ppermute(ups[3][0:256], ("y2", "y1"), up))
    key_values.append(lax.ppermute(downs[3][256:528], ("y2", "y1"), down))

    query = queries.reshape(tokens, 8, 2 * HD).transpose(1, 0, 2)
    query = jnp.broadcast_to(query[None], (4, 8, tokens, 2 * HD)).reshape(32, tokens, 2 * HD)
    query, _ = lax.optimization_barrier((query, key_value))
    query = lax.all_to_all(query, ("x", "z"), split_axis=0, concat_axis=0, tiled=True).reshape(
        4, 8, tokens, 2 * HD
    )

    whole_weight = lax.all_gather(output_weight, "z", axis=0, tiled=True)

    shards = flash(position, query, key_values)
    parts = lax.all_to_all(
        shards.reshape(32, HD + STAT, 128), ("x", "z"), split_axis=0, concat_axis=0, tiled=True
    ).reshape(4, 8, HD + STAT, 128)
    whole_weight, own_in, own_out = lax.optimization_barrier(
        (whole_weight, expert_in[0], expert_out[0])
    )
    other_in = lax.ppermute(own_in, "y1", SWAP)
    other_out = lax.ppermute(own_out, "y1", SWAP)
    turned = [ups[0][512:], ups[2][512:], key_values[8][256:], downs[2][512:]]
    listing = lax.dynamic_slice_in_dim(
        jnp.stack([turned[k][:, :tokens] for k in (3, 2, 1, 0, 3, 2, 1)]), 3 - own_y2, 4, 0
    ).astype(jnp.int32)
    named, levels = listing[:, None, 0:8], listing[:, None, 8:16]
    q = jnp.arange(32, dtype=jnp.int32)
    match = named == ((q % 8) * 16 + (q // 8) * 4 + own_y2)[None, :, None, None]
    hits = jnp.any(match, axis=2)
    gates = jnp.sum(jnp.where(match, levels, 0), axis=2).astype(F32) / 256.0
    before = jnp.triu(jnp.ones((tokens, tokens), BF), 1)
    ranks = jnp.einsum("sqb,ba->sqa", hits.astype(BF), before, preferred_element_type=F32)
    ranks = jnp.where(hits, ranks.astype(jnp.int32), -1)
    slots = jnp.arange(CAP, dtype=jnp.int32)[None, None, :, None, None]
    same = jnp.eye(4, dtype=jnp.bool_)[None, :, None, :, None]
    placed = (ranks.transpose(1, 0, 2)[:, None, None] == slots) & same
    chosen = placed.astype(BF).reshape(32 * 4 * CAP, 4 * tokens)
    shares = jnp.where(placed, gates.transpose(1, 0, 2)[:, None, None], 0.0).astype(BF)
    shares = shares.reshape(32 * 4 * CAP, 4 * tokens).T

    hidden, spread = merge(
        parts, whole_weight, residual, norm_gain.reshape(1, width)
    )

    spread, other_in, other_out = lax.optimization_barrier((spread, other_in, other_out))
    half = own_in.shape[1] // 2
    weight_in = jnp.concatenate(
        [own_in[:, :half], other_in[:, :half], own_in[:, half:], other_in[:, half:]], axis=1
    )
    weight_out = jnp.concatenate([own_out, other_out], axis=0)
    spread = lax.all_to_all(spread, "y2", split_axis=0, concat_axis=0, tiled=True)
    outgoing = select(chosen, spread.reshape(4 * tokens, width))
    arrived = lax.all_to_all(
        outgoing.reshape(32, 4 * CAP * 8, 128), ("x", "z"), split_axis=0, concat_axis=0, tiled=True
    )
    done = expert(arrived.reshape(-1, 128), weight_in, weight_out)
    answers = lax.all_to_all(
        done.reshape(32, 4 * CAP * 8, 128), ("x", "z"), split_axis=0, concat_axis=0, tiled=True
    )
    sums = gather(shares, answers.reshape(-1, 128))
    sums = lax.all_to_all(
        sums.reshape(4, tokens, width), "y2", split_axis=0, concat_axis=0, tiled=True
    )
    return hidden + jnp.sum(sums.astype(F32), axis=0)


def solution(mesh):
    fine = Mesh(mesh.devices.reshape(8, 4, 4, 2, 2), ("z", "x", "y2", "y1", "dp"))
    rows = P(("dp", "x", "y2", "y1", "z"), None)
    halves = P(("z", "x", "y2", "y1"), None, None)
    return jax.shard_map(
        local,
        mesh=fine,
        in_specs=(rows, rows, rows, rows, P("z", None), P(), rows, rows, halves, halves),
        out_specs=rows,
        check_vma=False,
    )
```

```python
import math

import jax
import jax.numpy as jnp
from jax import lax
from jax.experimental import pallas as pl
from jax.experimental.pallas import tpu as pltpu
from jax.sharding import Mesh
from jax.sharding import PartitionSpec as P

HD = 128
CAP = 5
LOG2E = 1.4426950408889634
BF = jnp.bfloat16
F32 = jnp.float32
NEG = -1e30
LOW = -1e29
STAT = 8
SWAP = [(0, 1), (1, 0)]


def flash_kernel(
    pos_ref, q_ref, b0, b1, b2, b3, b4, b5, b6, b7, o_ref, kv_ref, vt_ref, bias_ref, acc_ref, m_ref, top_ref
):
    block = pl.program_id(0)
    own_x = pos_ref[0]
    own_y = pos_ref[1]
    cols = 1024
    scale = LOG2E / math.sqrt(HD)

    def keys(c):
        return kv_ref[pl.ds(4 * (c % 2), 4), c // 2, :, 0:HD].reshape(512, HD)

    @pl.when(block == 0)
    def _():
        eye = (
            lax.broadcasted_iota(jnp.int32, (HD, HD), 0)
            == lax.broadcasted_iota(jnp.int32, (HD, HD), 1)
        ).astype(BF)
        for far, ref in enumerate((b0, b5, b6, b7, b4, b3, b2, b1)):
            kv_ref[(own_y + far) % 8] = ref[0:512, :].reshape(4, 128, 2 * HD)
        for c in range(8):
            v = kv_ref[4 * (c % 2) : 4 * (c % 2) + 4, c // 2, :, HD : 2 * HD].reshape(512, HD)
            turned = lax.dot_general(eye, v, (((1,), (1,)), ((), ())), preferred_element_type=F32)
            vt_ref[c, 0:HD, :] = turned.astype(BF)
            vt_ref[c, HD : HD + 16, :] = jnp.ones((16, 512), BF)
        row = lax.broadcasted_iota(jnp.int32, (512, 128), 0)
        col = lax.broadcasted_iota(jnp.int32, (512, 128), 1)
        inner = row % 128
        key_pos = (
            (row // 128 - own_y % 4) * 512 + (inner // 16) * 64 + inner % 16 + 16 * own_x - col % 64
        )
        for z in range(8):
            bias_ref[:, z * 128 : (z + 1) * 128] = jnp.where(key_pos <= z * 64, 0.0, NEG)

    tiles = block * 8 + own_y
    chunk_count = tiles // 4
    q_raw = q_ref[0]
    q = jnp.concatenate([q_raw[:, :, 0:HD], q_raw[:, :, HD : 2 * HD]], axis=1).reshape(cols, HD)
    group = 1024
    groups = [(g * group, q[g * group : (g + 1) * group]) for g in range(cols // group)]

    def scores(k, q_group):
        return lax.dot_general(k, q_group, (((1,), (1,)), ((), ())), preferred_element_type=F32)

    first_keys = kv_ref[0, 0, :, 0:HD]
    hide = jnp.where(tiles == 0, 1.0, 0.0)
    for start, q_group in groups:
        part = slice(start, start + group)
        s = scores(first_keys, q_group) + bias_ref[0:128, part] * hide
        m_ref[:, part] = jnp.maximum(jnp.max(s, axis=0, keepdims=True), LOW)
        top_ref[:, part] = jnp.max(s.reshape(16, 8, group), axis=0)
        acc_ref[:, part] = jnp.zeros((HD + 16, group), F32)

    def quick(c, masked):
        k = keys(c)
        values = vt_ref[c]
        found = [scores(k, q_group) for _, q_group in groups]
        for (start, _), s in zip(groups, found):
            part = slice(start, start + group)
            if masked:
                s = s + bias_ref[:, part]
            p = jnp.exp2(s * scale - m_ref[:, part] * scale).astype(BF)
            top_ref[:, part] = jnp.maximum(
                top_ref[:, part], jnp.max(s.reshape(64, 8, group), axis=0)
            )
            acc_ref[:, part] = acc_ref[:, part] + jnp.dot(values, p, preferred_element_type=F32)

    def quick_step(c, carry):
        quick(c, False)
        return carry

    lax.fori_loop(0, chunk_count, quick_step, 0)
    quick(chunk_count, True)

    def careful(c, masked):
        k = keys(c)
        values = vt_ref[c]
        for start, q_group in groups:
            part = slice(start, start + group)
            s = scores(k, q_group)
            if masked:
                s = s + bias_ref[:, part]
            m_old = m_ref[:, part]
            m = jnp.maximum(m_old, jnp.max(s, axis=0, keepdims=True))
            p = jnp.exp2((s - m) * scale).astype(BF)
            alpha = jnp.exp2((m_old - m) * scale)
            m_ref[:, part] = m
            acc_ref[:, part] = acc_ref[:, part] * alpha + jnp.dot(
                values, p, preferred_element_type=F32
            )

    def careful_step(c, carry):
        careful(c, False)
        return carry

    rise = jnp.max((top_ref[...] - m_ref[...]) * scale)

    @pl.when(rise > 64.0)
    def _():
        m_ref[...] = jnp.full((1, cols), LOW, F32)
        acc_ref[...] = jnp.zeros((HD + 16, cols), F32)
        lax.fori_loop(0, chunk_count, careful_step, 0)
        careful(chunk_count, True)

    total = acc_ref[HD : HD + 1, :]
    seen = total > 0.0
    safe = jnp.where(seen, total, 1.0)
    out = (acc_ref[0:HD, :] * (1.0 / safe)).astype(BF)
    level = jnp.where(seen, m_ref[...] * scale + jnp.log(safe) * LOG2E, NEG)
    first = level.astype(BF).astype(F32)
    second = (level - first).astype(BF).astype(F32)
    third = level - first - second
    pick = lax.broadcasted_iota(jnp.int32, (STAT, cols), 0)
    stats = jnp.where(pick == 0, first, jnp.where(pick == 1, second, jnp.where(pick == 2, third, 0.0)))
    stats = stats.astype(BF)
    for i in range(8):
        o_ref[0, i, 0:HD, :] = out[:, i * 128 : (i + 1) * 128]
        o_ref[0, i, HD : HD + STAT, :] = stats[:, i * 128 : (i + 1) * 128]


def flash(position, queries, key_values):
    return pl.pallas_call(
        flash_kernel,
        grid_spec=pltpu.PrefetchScalarGridSpec(
            num_scalar_prefetch=1,
            grid=(4,),
            in_specs=[
                pl.BlockSpec((1, 8, 64, 256), lambda i, s: (i, 0, 0, 0)),
            ]
            + [pl.BlockSpec(block.shape, lambda i, s: (0, 0)) for block in key_values],
            out_specs=pl.BlockSpec((1, 8, HD + STAT, 128), lambda i, s: (i, 0, 0, 0)),
            scratch_shapes=[
                pltpu.VMEM((8, 4, 128, 2 * HD), BF),
                pltpu.VMEM((8, HD + 16, 512), BF),
                pltpu.VMEM((512, 1024), F32),
                pltpu.VMEM((HD + 16, 1024), F32),
                pltpu.VMEM((1, 1024), F32),
                pltpu.VMEM((8, 1024), F32),
            ],
        ),
        out_shape=jax.ShapeDtypeStruct((4, 8, HD + STAT, 128), BF),
        compiler_params=pltpu.CompilerParams(vmem_limit_bytes=40 * 1024 * 1024),
        cost_estimate=pl.CostEstimate(
            flops=4 * 4096 * 2560 * HD, bytes_accessed=5 << 20, transcendentals=4096 * 2560
        ),
        name="flash",
    )(position, queries, *key_values)


def merge_kernel(parts_ref, w_ref, res_ref, gain_ref, hidden_ref, normed_ref):
    step = pl.program_id(0)
    found = []
    for c in range(2):
        levels = []
        for x in range(4):
            st = parts_ref[x, c, HD : HD + STAT, :].astype(F32)
            levels.append(st[0:1] + st[1:2] + st[2:3])
        top = jnp.maximum(jnp.maximum(levels[0], levels[1]), jnp.maximum(levels[2], levels[3]))
        shares = [jnp.exp2(level - top) for level in levels]
        inverse = 1.0 / (shares[0] + shares[1] + shares[2] + shares[3])
        mixed = parts_ref[0, c, 0:HD, :].astype(F32) * (shares[0] * inverse)
        for x in range(1, 4):
            mixed = mixed + parts_ref[x, c, 0:HD, :].astype(F32) * (shares[x] * inverse)
        rows = mixed.T.astype(BF)
        found += [rows[0:64], rows[64:128]]
    part = jnp.dot(jnp.concatenate(found, axis=1), w_ref[...], preferred_element_type=F32)

    @pl.when(step == 0)
    def _():
        hidden_ref[...] = res_ref[...].astype(F32) + part

    @pl.when(step > 0)
    def _():
        hidden_ref[...] = hidden_ref[...] + part

    @pl.when(step == 3)
    def _():
        hidden = hidden_ref[...]
        mean_square = jnp.mean(hidden * hidden, axis=1, keepdims=True)
        normed = (hidden * lax.rsqrt(mean_square + 1e-6) * gain_ref[...]).astype(BF)
        for i in range(4):
            normed_ref[i] = normed


def merge(parts, weight, residual, gain):
    tokens, width = residual.shape
    whole = pl.BlockSpec((tokens, width), lambda c: (0, 0))
    return pl.pallas_call(
        merge_kernel,
        grid=(4,),
        in_specs=[
            pl.BlockSpec((4, 2, HD + STAT, 128), lambda c: (0, c, 0, 0)),
            pl.BlockSpec((512, width), lambda c: (c, 0)),
            whole,
            pl.BlockSpec((1, width), lambda c: (0, 0)),
        ],
        out_specs=[whole, pl.BlockSpec((4, tokens, width), lambda c: (0, 0, 0))],
        out_shape=[
            jax.ShapeDtypeStruct((tokens, width), F32),
            jax.ShapeDtypeStruct((4, tokens, width), BF),
        ],
        name="merge",
    )(parts, weight, residual, gain)


def select_kernel(sel_ref, x_ref, o_ref, tmp_ref):
    count = sel_ref.shape[0]
    sel = sel_ref[...]
    for j in range(0, 8, 2):
        got = jnp.dot(sel, x_ref[:, j * 128 : (j + 2) * 128], preferred_element_type=F32)
        tmp_ref[pl.ds(j, count, stride=8), :] = got[:, 0:128]
        tmp_ref[pl.ds(j + 1, count, stride=8), :] = got[:, 128:256]
    o_ref[...] = tmp_ref[...].astype(BF)


def select(chosen, tokens):
    count = chosen.shape[0]
    return pl.pallas_call(
        select_kernel,
        out_shape=jax.ShapeDtypeStruct((count * 8, 128), BF),
        scratch_shapes=[pltpu.VMEM((count * 8, 128), F32)],
        compiler_params=pltpu.CompilerParams(vmem_limit_bytes=40 * 1024 * 1024),
        name="select",
    )(chosen, tokens)


def expert_kernel(x_ref, win_ref, wout_ref, o_ref, tmp_ref):
    rows = x_ref.shape[0] // 8
    inner = wout_ref.shape[0]
    tmp_ref[...] = x_ref[...].astype(F32)
    x = jnp.concatenate(
        [tmp_ref[pl.ds(j, rows, stride=8), :].astype(BF) for j in range(8)], axis=1
    )
    projection = jnp.dot(x, win_ref[...], preferred_element_type=F32)
    gate = projection[:, 0:inner]
    activated = (gate / (1.0 + jnp.exp(-gate)) * projection[:, inner:]).astype(BF)
    out = jnp.dot(activated, wout_ref[...], preferred_element_type=F32)
    for j in range(8):
        tmp_ref[pl.ds(j, rows, stride=8), :] = out[:, j * 128 : (j + 1) * 128]
    o_ref[...] = tmp_ref[...].astype(BF)


def expert(rows_in, weight_in, weight_out):
    total = rows_in.shape[0]
    block = total // 4
    return pl.pallas_call(
        expert_kernel,
        grid=(4,),
        in_specs=[
            pl.BlockSpec((block, 128), lambda i: (i, 0)),
            pl.BlockSpec(weight_in.shape, lambda i: (0, 0)),
            pl.BlockSpec(weight_out.shape, lambda i: (0, 0)),
        ],
        out_specs=pl.BlockSpec((block, 128), lambda i: (i, 0)),
        out_shape=jax.ShapeDtypeStruct((total, 128), BF),
        scratch_shapes=[pltpu.VMEM((block, 128), F32)],
        compiler_params=pltpu.CompilerParams(vmem_limit_bytes=40 * 1024 * 1024),
        name="expert",
    )(rows_in, weight_in, weight_out)


def gather_kernel(gates_ref, x_ref, o_ref, tmp_ref):
    count = gates_ref.shape[1]
    gates = gates_ref[...]
    tmp_ref[...] = x_ref[...].astype(F32)
    for j in range(0, 8, 2):
        x = jnp.concatenate(
            [
                tmp_ref[pl.ds(j, count, stride=8), :].astype(BF),
                tmp_ref[pl.ds(j + 1, count, stride=8), :].astype(BF),
            ],
            axis=1,
        )
        o_ref[:, j * 128 : (j + 2) * 128] = jnp.dot(
            gates, x, preferred_element_type=F32
        ).astype(BF)


def gather(gates, rows):
    count = gates.shape[1]
    return pl.pallas_call(
        gather_kernel,
        out_shape=jax.ShapeDtypeStruct((gates.shape[0], 1024), BF),
        scratch_shapes=[pltpu.VMEM((count * 8, 128), F32)],
        compiler_params=pltpu.CompilerParams(vmem_limit_bytes=40 * 1024 * 1024),
        name="gather",
    )(gates, rows)


def pack_kv_kernel(k_ref, v_ref, o_ref):
    for g in range(2):
        lanes = slice(g * HD, (g + 1) * HD)
        both = jnp.concatenate([k_ref[:, lanes], v_ref[:, lanes]], axis=1)
        for x in range(4):
            for i in range(4):
                o_ref[x * 8 + g * 4 + i] = both[16 * x : 16 * x + 16]


def pack_kv(keys, values):
    return pl.pallas_call(
        pack_kv_kernel,
        out_shape=jax.ShapeDtypeStruct((32, 16, 2 * HD), BF),
        name="pack_kv",
    )(keys, values)


def pack_q_kernel(q_ref, o_ref):
    for z in range(8):
        piece = q_ref[:, z * 2 * HD : (z + 1) * 2 * HD]
        for x in range(4):
            o_ref[x * 8 + z] = piece


def pack_q(queries):
    return pl.pallas_call(
        pack_q_kernel,
        out_shape=jax.ShapeDtypeStruct((32, queries.shape[0], 2 * HD), BF),
        cost_estimate=pl.CostEstimate(flops=0, bytes_accessed=5 << 18, transcendentals=0),
        name="pack_q",
    )(queries)


def local(
    residual,
    queries,
    key_vectors,
    value_vectors,
    output_weight,
    norm_gain,
    routes,
    gate_levels,
    expert_in,
    expert_out,
):
    tokens, width = residual.shape
    own_x = lax.axis_index("x")
    own_y2 = lax.axis_index("y2")
    own_y = own_y2 * 2 + lax.axis_index("y1")
    position = jnp.stack([own_x, own_y]).astype(jnp.int32)

    key_value = pack_kv(key_vectors, value_vectors)
    key_value = lax.all_to_all(key_value, ("x", "z"), split_axis=0, concat_axis=0, tiled=True)
    listing = jnp.concatenate([routes.T, gate_levels.T], axis=0).astype(BF)
    listing = jnp.pad(listing, ((0, 0), (0, 2 * HD - tokens)))
    block = jnp.concatenate([key_value.reshape(512, 2 * HD), listing], axis=0)
    up = [(i, (i + 1) % 8) for i in range(8)]
    down = [(i, (i - 1) % 8) for i in range(8)]
    ups, downs = [block], [block]
    for step in range(4):
        ups.append(lax.ppermute(ups[-1], ("y2", "y1"), up))
        if step < 3:
            downs.append(lax.ppermute(downs[-1], ("y2", "y1"), down))
    key_values = ups + downs[1:]

    query = lax.all_to_all(pack_q(queries), ("x", "z"), split_axis=0, concat_axis=0, tiled=True).reshape(
        4, 8, tokens, 2 * HD
    )

    whole_weight = lax.all_gather(output_weight, "z", axis=0, tiled=True)

    shards = flash(position, query, key_values)
    parts = lax.all_to_all(
        shards.reshape(32, HD + STAT, 128), ("x", "z"), split_axis=0, concat_axis=0, tiled=True
    ).reshape(4, 8, HD + STAT, 128)
    whole_weight, own_in, own_out = lax.optimization_barrier(
        (whole_weight, expert_in[0], expert_out[0])
    )
    other_in = lax.ppermute(own_in, "y1", SWAP)
    other_out = lax.ppermute(own_out, "y1", SWAP)
    turned = [ups[0][512:], ups[2][512:], ups[4][512:], downs[2][512:]]
    listing = lax.dynamic_slice_in_dim(
        jnp.stack([turned[k][:, :tokens] for k in (3, 2, 1, 0, 3, 2, 1)]), 3 - own_y2, 4, 0
    ).astype(jnp.int32)
    named, levels = listing[:, None, 0:8], listing[:, None, 8:16]
    q = jnp.arange(32, dtype=jnp.int32)
    match = named == ((q % 8) * 16 + (q // 8) * 4 + own_y2)[None, :, None, None]
    hits = jnp.any(match, axis=2)
    gates = jnp.sum(jnp.where(match, levels, 0), axis=2).astype(F32) / 256.0
    before = jnp.triu(jnp.ones((tokens, tokens), BF), 1)
    ranks = jnp.einsum("sqb,ba->sqa", hits.astype(BF), before, preferred_element_type=F32)
    ranks = jnp.where(hits, ranks.astype(jnp.int32), -1)
    slots = jnp.arange(CAP, dtype=jnp.int32)[None, None, :, None, None]
    same = jnp.eye(4, dtype=jnp.bool_)[None, :, None, :, None]
    placed = (ranks.transpose(1, 0, 2)[:, None, None] == slots) & same
    chosen = placed.astype(BF).reshape(32 * 4 * CAP, 4 * tokens)
    shares = jnp.where(placed, gates.transpose(1, 0, 2)[:, None, None], 0.0).astype(BF)
    shares = shares.reshape(32 * 4 * CAP, 4 * tokens).T

    hidden, spread = merge(
        parts, whole_weight, residual, norm_gain.reshape(1, width)
    )

    spread, other_in, other_out = lax.optimization_barrier((spread, other_in, other_out))
    half = own_in.shape[1] // 2
    weight_in = jnp.concatenate(
        [own_in[:, :half], other_in[:, :half], own_in[:, half:], other_in[:, half:]], axis=1
    )
    weight_out = jnp.concatenate([own_out, other_out], axis=0)
    spread = lax.all_to_all(spread, "y2", split_axis=0, concat_axis=0, tiled=True)
    outgoing = select(chosen, spread.reshape(4 * tokens, width))
    arrived = lax.all_to_all(
        outgoing.reshape(32, 4 * CAP * 8, 128), ("x", "z"), split_axis=0, concat_axis=0, tiled=True
    )
    done = expert(arrived.reshape(-1, 128), weight_in, weight_out)
    answers = lax.all_to_all(
        done.reshape(32, 4 * CAP * 8, 128), ("x", "z"), split_axis=0, concat_axis=0, tiled=True
    )
    sums = gather(shares, answers.reshape(-1, 128))
    sums = lax.all_to_all(
        sums.reshape(4, tokens, width), "y2", split_axis=0, concat_axis=0, tiled=True
    )
    return hidden + jnp.sum(sums.astype(F32), axis=0)


def solution(mesh):
    fine = Mesh(mesh.devices.reshape(8, 4, 4, 2, 2), ("z", "x", "y2", "y1", "dp"))
    rows = P(("dp", "x", "y2", "y1", "z"), None)
    halves = P(("z", "x", "y2", "y1"), None, None)
    return jax.shard_map(
        local,
        mesh=fine,
        in_specs=(rows, rows, rows, rows, P("z", None), P(), rows, rows, halves, halves),
        out_specs=rows,
        check_vma=False,
    )
```

```python
import math

import jax
import jax.numpy as jnp
from jax import lax
from jax.experimental import pallas as pl
from jax.experimental.pallas import tpu as pltpu
from jax.sharding import Mesh
from jax.sharding import PartitionSpec as P

HD = 128
CAP = 5
LOG2E = 1.4426950408889634
BF = jnp.bfloat16
F32 = jnp.float32
NEG = -1e30
LOW = -1e29
STAT = 8
SWAP = [(0, 1), (1, 0)]


def flash_kernel(
    pos_ref, q_ref, b0, b1, b2, b3, b4, b5, b6, b7, o_ref, kv_ref, vt_ref, bias_ref, acc_ref, m_ref, top_ref
):
    block = pl.program_id(0)
    own_x = pos_ref[0]
    own_y = pos_ref[1]
    cols = 1024
    scale = LOG2E / math.sqrt(HD)

    def keys(c):
        return kv_ref[pl.ds(4 * (c % 2), 4), c // 2, :, 0:HD].reshape(512, HD)

    @pl.when(block == 0)
    def _():
        eye = (
            lax.broadcasted_iota(jnp.int32, (HD, HD), 0)
            == lax.broadcasted_iota(jnp.int32, (HD, HD), 1)
        ).astype(BF)
        for far, ref in enumerate((b0, b5, b6, b7, b4, b3, b2, b1)):
            kv_ref[(own_y + far) % 8] = ref[0:512, :].reshape(4, 128, 2 * HD)
        for c in range(8):
            v = kv_ref[4 * (c % 2) : 4 * (c % 2) + 4, c // 2, :, HD : 2 * HD].reshape(512, HD)
            turned = lax.dot_general(eye, v, (((1,), (1,)), ((), ())), preferred_element_type=F32)
            vt_ref[c, 0:HD, :] = turned.astype(BF)
            vt_ref[c, HD : HD + 16, :] = jnp.ones((16, 512), BF)
        row = lax.broadcasted_iota(jnp.int32, (512, 128), 0)
        col = lax.broadcasted_iota(jnp.int32, (512, 128), 1)
        inner = row % 128
        key_pos = (
            (row // 128 - own_y % 4) * 512 + (inner // 16) * 64 + inner % 16 + 16 * own_x - col % 64
        )
        for z in range(8):
            bias_ref[:, z * 128 : (z + 1) * 128] = jnp.where(key_pos <= z * 64, 0.0, NEG)

    tiles = block * 8 + own_y
    chunk_count = tiles // 4
    q_raw = q_ref[0]
    q = jnp.concatenate([q_raw[:, :, 0:HD], q_raw[:, :, HD : 2 * HD]], axis=1).reshape(cols, HD)
    group = 1024
    groups = [(g * group, q[g * group : (g + 1) * group]) for g in range(cols // group)]

    def scores(k, q_group):
        return lax.dot_general(k, q_group, (((1,), (1,)), ((), ())), preferred_element_type=F32)

    first_keys = kv_ref[0, 0, :, 0:HD]
    hide = jnp.where(tiles == 0, 1.0, 0.0)
    for start, q_group in groups:
        part = slice(start, start + group)
        s = scores(first_keys, q_group) + bias_ref[0:128, part] * hide
        m_ref[:, part] = jnp.maximum(jnp.max(s, axis=0, keepdims=True), LOW)
        top_ref[:, part] = jnp.max(s.reshape(16, 8, group), axis=0)
        acc_ref[:, part] = jnp.zeros((HD + 16, group), F32)

    def quick(c, masked):
        k = keys(c)
        values = vt_ref[c]
        found = [scores(k, q_group) for _, q_group in groups]
        for (start, _), s in zip(groups, found):
            part = slice(start, start + group)
            if masked:
                s = s + bias_ref[:, part]
            p = jnp.exp2(s * scale - m_ref[:, part] * scale).astype(BF)
            top_ref[:, part] = jnp.maximum(
                top_ref[:, part], jnp.max(s.reshape(64, 8, group), axis=0)
            )
            acc_ref[:, part] = acc_ref[:, part] + jnp.dot(values, p, preferred_element_type=F32)

    def quick_step(c, carry):
        quick(c, False)
        return carry

    lax.fori_loop(0, chunk_count, quick_step, 0)
    quick(chunk_count, True)

    def careful(c, masked):
        k = keys(c)
        values = vt_ref[c]
        for start, q_group in groups:
            part = slice(start, start + group)
            s = scores(k, q_group)
            if masked:
                s = s + bias_ref[:, part]
            m_old = m_ref[:, part]
            m = jnp.maximum(m_old, jnp.max(s, axis=0, keepdims=True))
            p = jnp.exp2((s - m) * scale).astype(BF)
            alpha = jnp.exp2((m_old - m) * scale)
            m_ref[:, part] = m
            acc_ref[:, part] = acc_ref[:, part] * alpha + jnp.dot(
                values, p, preferred_element_type=F32
            )

    def careful_step(c, carry):
        careful(c, False)
        return carry

    rise = jnp.max((top_ref[...] - m_ref[...]) * scale)

    @pl.when(rise > 64.0)
    def _():
        m_ref[...] = jnp.full((1, cols), LOW, F32)
        acc_ref[...] = jnp.zeros((HD + 16, cols), F32)
        lax.fori_loop(0, chunk_count, careful_step, 0)
        careful(chunk_count, True)

    total = acc_ref[HD : HD + 1, :]
    seen = total > 0.0
    safe = jnp.where(seen, total, 1.0)
    out = (acc_ref[0:HD, :] * (1.0 / safe)).astype(BF)
    level = jnp.where(seen, m_ref[...] * scale + jnp.log(safe) * LOG2E, NEG)
    first = level.astype(BF).astype(F32)
    second = (level - first).astype(BF).astype(F32)
    third = level - first - second
    pick = lax.broadcasted_iota(jnp.int32, (STAT, cols), 0)
    stats = jnp.where(pick == 0, first, jnp.where(pick == 1, second, jnp.where(pick == 2, third, 0.0)))
    stats = stats.astype(BF)
    for i in range(8):
        o_ref[i, 0, 0:HD, :] = out[:, i * 128 : (i + 1) * 128]
        o_ref[i, 0, HD : HD + STAT, :] = stats[:, i * 128 : (i + 1) * 128]


def flash(position, queries, key_values):
    return pl.pallas_call(
        flash_kernel,
        grid_spec=pltpu.PrefetchScalarGridSpec(
            num_scalar_prefetch=1,
            grid=(4,),
            in_specs=[
                pl.BlockSpec((1, 8, 64, 256), lambda i, s: (i, 0, 0, 0)),
            ]
            + [pl.BlockSpec(block.shape, lambda i, s: (0, 0)) for block in key_values],
            out_specs=pl.BlockSpec((8, 1, HD + STAT, 128), lambda i, s: (0, i, 0, 0)),
            scratch_shapes=[
                pltpu.VMEM((8, 4, 128, 2 * HD), BF),
                pltpu.VMEM((8, HD + 16, 512), BF),
                pltpu.VMEM((512, 1024), F32),
                pltpu.VMEM((HD + 16, 1024), F32),
                pltpu.VMEM((1, 1024), F32),
                pltpu.VMEM((8, 1024), F32),
            ],
        ),
        out_shape=jax.ShapeDtypeStruct((8, 4, HD + STAT, 128), BF),
        compiler_params=pltpu.CompilerParams(vmem_limit_bytes=40 * 1024 * 1024),
        cost_estimate=pl.CostEstimate(
            flops=4 * 4096 * 2560 * HD, bytes_accessed=5 << 20, transcendentals=4096 * 2560
        ),
        name="flash",
    )(position, queries, *key_values)


def merge_kernel(parts_ref, w_ref, res_ref, gain_ref, hidden_ref, normed_ref):
    step = pl.program_id(0)
    found = []
    for c in range(2):
        levels = []
        for x in range(4):
            st = parts_ref[c, x, HD : HD + STAT, :].astype(F32)
            levels.append(st[0:1] + st[1:2] + st[2:3])
        top = jnp.maximum(jnp.maximum(levels[0], levels[1]), jnp.maximum(levels[2], levels[3]))
        shares = [jnp.exp2(level - top) for level in levels]
        inverse = 1.0 / (shares[0] + shares[1] + shares[2] + shares[3])
        mixed = parts_ref[c, 0, 0:HD, :].astype(F32) * (shares[0] * inverse)
        for x in range(1, 4):
            mixed = mixed + parts_ref[c, x, 0:HD, :].astype(F32) * (shares[x] * inverse)
        rows = mixed.T.astype(BF)
        found += [rows[0:64], rows[64:128]]
    part = jnp.dot(jnp.concatenate(found, axis=1), w_ref[...], preferred_element_type=F32)

    @pl.when(step == 0)
    def _():
        hidden_ref[...] = res_ref[...].astype(F32) + part

    @pl.when(step > 0)
    def _():
        hidden_ref[...] = hidden_ref[...] + part

    @pl.when(step == 3)
    def _():
        hidden = hidden_ref[...]
        mean_square = jnp.mean(hidden * hidden, axis=1, keepdims=True)
        normed = (hidden * lax.rsqrt(mean_square + 1e-6) * gain_ref[...]).astype(BF)
        for i in range(4):
            normed_ref[i] = normed


def merge(parts, weight, residual, gain):
    tokens, width = residual.shape
    whole = pl.BlockSpec((tokens, width), lambda c: (0, 0))
    return pl.pallas_call(
        merge_kernel,
        grid=(4,),
        in_specs=[
            pl.BlockSpec((2, 4, HD + STAT, 128), lambda c: (c, 0, 0, 0)),
            pl.BlockSpec((512, width), lambda c: (c, 0)),
            whole,
            pl.BlockSpec((1, width), lambda c: (0, 0)),
        ],
        out_specs=[whole, pl.BlockSpec((4, tokens, width), lambda c: (0, 0, 0))],
        out_shape=[
            jax.ShapeDtypeStruct((tokens, width), F32),
            jax.ShapeDtypeStruct((4, tokens, width), BF),
        ],
        name="merge",
    )(parts, weight, residual, gain)


def select_kernel(sel_ref, x_ref, o_ref, tmp_ref):
    count = sel_ref.shape[0]
    sel = sel_ref[...]
    for j in range(0, 8, 2):
        got = jnp.dot(sel, x_ref[:, j * 128 : (j + 2) * 128], preferred_element_type=F32)
        tmp_ref[pl.ds(j, count, stride=8), :] = got[:, 0:128]
        tmp_ref[pl.ds(j + 1, count, stride=8), :] = got[:, 128:256]
    o_ref[...] = tmp_ref[...].astype(BF)


def select(chosen, tokens):
    count = chosen.shape[0]
    return pl.pallas_call(
        select_kernel,
        out_shape=jax.ShapeDtypeStruct((count * 8, 128), BF),
        scratch_shapes=[pltpu.VMEM((count * 8, 128), F32)],
        compiler_params=pltpu.CompilerParams(vmem_limit_bytes=40 * 1024 * 1024),
        name="select",
    )(chosen, tokens)


def expert_kernel(x_ref, win_ref, wout_ref, o_ref, tmp_ref):
    rows = x_ref.shape[0] // 8
    inner = wout_ref.shape[0]
    tmp_ref[...] = x_ref[...].astype(F32)
    x = jnp.concatenate(
        [tmp_ref[pl.ds(j, rows, stride=8), :].astype(BF) for j in range(8)], axis=1
    )
    projection = jnp.dot(x, win_ref[...], preferred_element_type=F32)
    gate = projection[:, 0:inner]
    activated = (gate / (1.0 + jnp.exp(-gate)) * projection[:, inner:]).astype(BF)
    out = jnp.dot(activated, wout_ref[...], preferred_element_type=F32)
    for j in range(8):
        tmp_ref[pl.ds(j, rows, stride=8), :] = out[:, j * 128 : (j + 1) * 128]
    o_ref[...] = tmp_ref[...].astype(BF)


def expert(rows_in, weight_in, weight_out):
    total = rows_in.shape[0]
    block = total // 4
    return pl.pallas_call(
        expert_kernel,
        grid=(4,),
        in_specs=[
            pl.BlockSpec((block, 128), lambda i: (i, 0)),
            pl.BlockSpec(weight_in.shape, lambda i: (0, 0)),
            pl.BlockSpec(weight_out.shape, lambda i: (0, 0)),
        ],
        out_specs=pl.BlockSpec((block, 128), lambda i: (i, 0)),
        out_shape=jax.ShapeDtypeStruct((total, 128), BF),
        scratch_shapes=[pltpu.VMEM((block, 128), F32)],
        compiler_params=pltpu.CompilerParams(vmem_limit_bytes=40 * 1024 * 1024),
        name="expert",
    )(rows_in, weight_in, weight_out)


def gather_kernel(gates_ref, x_ref, o_ref, tmp_ref):
    count = gates_ref.shape[1]
    gates = gates_ref[...]
    tmp_ref[...] = x_ref[...].astype(F32)
    for j in range(0, 8, 2):
        x = jnp.concatenate(
            [
                tmp_ref[pl.ds(j, count, stride=8), :].astype(BF),
                tmp_ref[pl.ds(j + 1, count, stride=8), :].astype(BF),
            ],
            axis=1,
        )
        o_ref[:, j * 128 : (j + 2) * 128] = jnp.dot(
            gates, x, preferred_element_type=F32
        ).astype(BF)


def gather(gates, rows):
    count = gates.shape[1]
    return pl.pallas_call(
        gather_kernel,
        out_shape=jax.ShapeDtypeStruct((gates.shape[0], 1024), BF),
        scratch_shapes=[pltpu.VMEM((count * 8, 128), F32)],
        compiler_params=pltpu.CompilerParams(vmem_limit_bytes=40 * 1024 * 1024),
        name="gather",
    )(gates, rows)


def pack_kv_kernel(k_ref, v_ref, o_ref):
    for g in range(2):
        lanes = slice(g * HD, (g + 1) * HD)
        both = jnp.concatenate([k_ref[:, lanes], v_ref[:, lanes]], axis=1)
        for x in range(4):
            for i in range(4):
                o_ref[x * 8 + g * 4 + i] = both[16 * x : 16 * x + 16]


def pack_kv(keys, values):
    return pl.pallas_call(
        pack_kv_kernel,
        out_shape=jax.ShapeDtypeStruct((32, 16, 2 * HD), BF),
        name="pack_kv",
    )(keys, values)


def pack_q_kernel(q_ref, o_ref):
    for z in range(8):
        piece = q_ref[:, z * 2 * HD : (z + 1) * 2 * HD]
        for x in range(4):
            o_ref[x * 8 + z] = piece


def pack_q(queries):
    return pl.pallas_call(
        pack_q_kernel,
        out_shape=jax.ShapeDtypeStruct((32, queries.shape[0], 2 * HD), BF),
        cost_estimate=pl.CostEstimate(flops=0, bytes_accessed=5 << 18, transcendentals=0),
        name="pack_q",
    )(queries)


def local(
    residual,
    queries,
    key_vectors,
    value_vectors,
    output_weight,
    norm_gain,
    routes,
    gate_levels,
    expert_in,
    expert_out,
):
    tokens, width = residual.shape
    own_x = lax.axis_index("x")
    own_y2 = lax.axis_index("y2")
    own_y = own_y2 * 2 + lax.axis_index("y1")
    position = jnp.stack([own_x, own_y]).astype(jnp.int32)

    key_value = pack_kv(key_vectors, value_vectors)
    key_value = lax.all_to_all(key_value, ("x", "z"), split_axis=0, concat_axis=0, tiled=True)
    listing = jnp.concatenate([routes.T, gate_levels.T], axis=0).astype(BF)
    listing = jnp.pad(listing, ((0, 0), (0, 2 * HD - tokens)))
    block = jnp.concatenate([key_value.reshape(512, 2 * HD), listing], axis=0)
    up = [(i, (i + 1) % 8) for i in range(8)]
    down = [(i, (i - 1) % 8) for i in range(8)]
    ups, downs = [block], [block]
    for step in range(4):
        ups.append(lax.ppermute(ups[-1], ("y2", "y1"), up))
        if step < 3:
            downs.append(lax.ppermute(downs[-1], ("y2", "y1"), down))
    key_values = ups + downs[1:]

    query = lax.all_to_all(pack_q(queries), ("x", "z"), split_axis=0, concat_axis=0, tiled=True).reshape(
        4, 8, tokens, 2 * HD
    )

    whole_weight = lax.all_gather(output_weight, "z", axis=0, tiled=True)

    shards = flash(position, query, key_values)
    parts = lax.all_to_all(
        shards.reshape(32, HD + STAT, 128), ("z", "x"), split_axis=0, concat_axis=0, tiled=True
    ).reshape(8, 4, HD + STAT, 128)
    whole_weight, own_out = lax.optimization_barrier((whole_weight, expert_out[0]))
    other_out = lax.ppermute(own_out, "y1", SWAP)
    turned = [ups[0][512:], ups[2][512:], ups[4][512:], downs[2][512:]]
    listing = lax.dynamic_slice_in_dim(
        jnp.stack([turned[k][:, :tokens] for k in (3, 2, 1, 0, 3, 2, 1)]), 3 - own_y2, 4, 0
    ).astype(jnp.int32)
    named, levels = listing[:, None, 0:8], listing[:, None, 8:16]
    q = jnp.arange(32, dtype=jnp.int32)
    match = named == ((q // 4) * 16 + (q % 4) * 4 + own_y2)[None, :, None, None]
    hits = jnp.any(match, axis=2)
    gates = jnp.sum(jnp.where(match, levels, 0), axis=2).astype(F32) / 256.0
    before = jnp.triu(jnp.ones((tokens, tokens), BF), 1)
    ranks = jnp.einsum("sqb,ba->sqa", hits.astype(BF), before, preferred_element_type=F32)
    ranks = jnp.where(hits, ranks.astype(jnp.int32), -1)
    slots = jnp.arange(CAP, dtype=jnp.int32)[None, None, :, None, None]
    same = jnp.eye(4, dtype=jnp.bool_)[None, :, None, :, None]
    placed = (ranks.transpose(1, 0, 2)[:, None, None] == slots) & same
    chosen = placed.astype(BF).reshape(32 * 4 * CAP, 4 * tokens)
    shares = jnp.where(placed, gates.transpose(1, 0, 2)[:, None, None], 0.0).astype(BF)
    shares = shares.reshape(32 * 4 * CAP, 4 * tokens).T

    hidden, spread = merge(
        parts, whole_weight, residual, norm_gain.reshape(1, width)
    )

    spread, other_out = lax.optimization_barrier((spread, other_out))
    spread = lax.all_to_all(spread, "y2", split_axis=0, concat_axis=0, tiled=True)
    outgoing = select(chosen, spread.reshape(4 * tokens, width))
    outgoing, own_in = lax.optimization_barrier((outgoing, expert_in[0]))
    other_in = lax.ppermute(own_in, "y1", SWAP)
    half = own_in.shape[1] // 2
    weight_in = jnp.concatenate(
        [own_in[:, :half], other_in[:, :half], own_in[:, half:], other_in[:, half:]], axis=1
    )
    weight_out = jnp.concatenate([own_out, other_out], axis=0)
    arrived = lax.all_to_all(
        outgoing.reshape(32, 4 * CAP * 8, 128), ("z", "x"), split_axis=0, concat_axis=0, tiled=True
    )
    done = expert(arrived.reshape(-1, 128), weight_in, weight_out)
    answers = lax.all_to_all(
        done.reshape(32, 4 * CAP * 8, 128), ("z", "x"), split_axis=0, concat_axis=0, tiled=True
    )
    sums = gather(shares, answers.reshape(-1, 128))
    sums = lax.all_to_all(
        sums.reshape(4, tokens, width), "y2", split_axis=0, concat_axis=0, tiled=True
    )
    return hidden + jnp.sum(sums.astype(F32), axis=0)


def solution(mesh):
    fine = Mesh(mesh.devices.reshape(8, 4, 4, 2, 2), ("z", "x", "y2", "y1", "dp"))
    rows = P(("dp", "x", "y2", "y1", "z"), None)
    halves = P(("z", "x", "y2", "y1"), None, None)
    return jax.shard_map(
        local,
        mesh=fine,
        in_specs=(rows, rows, rows, rows, P("z", None), P(), rows, rows, halves, halves),
        out_specs=rows,
        check_vma=False,
    )
```

```python
import math

import jax
import jax.numpy as jnp
from jax import lax
from jax.experimental import pallas as pl
from jax.experimental.pallas import tpu as pltpu
from jax.sharding import Mesh
from jax.sharding import PartitionSpec as P

HD = 128
CAP = 5
LOG2E = 1.4426950408889634
BF = jnp.bfloat16
F32 = jnp.float32
NEG = -1e30
LOW = -1e29
STAT = 8
SWAP = [(i, i ^ 1) for i in range(8)]
CLASSES = [[0, 2, 5, 7], [1, 3, 4, 6]]


def flash_kernel(
    pos_ref, q_ref, b0, b1, b2, b3, b4, b5, b6, b7, o_ref, kv_ref, vt_ref, bias_ref, acc_ref, m_ref, top_ref
):
    block = pl.program_id(0)
    own_x = pos_ref[0]
    own_y = pos_ref[1]
    cols = 1024
    scale = LOG2E / math.sqrt(HD)

    def keys(c):
        return kv_ref[pl.ds(4 * (c % 2), 4), c // 2, :, 0:HD].reshape(512, HD)

    @pl.when(block == 0)
    def _():
        eye = (
            lax.broadcasted_iota(jnp.int32, (HD, HD), 0)
            == lax.broadcasted_iota(jnp.int32, (HD, HD), 1)
        ).astype(BF)
        for far, ref in enumerate((b0, b5, b6, b7, b4, b3, b2, b1)):
            kv_ref[(own_y + far) % 8] = ref[0:512, :].reshape(4, 128, 2 * HD)
        for c in range(8):
            v = kv_ref[4 * (c % 2) : 4 * (c % 2) + 4, c // 2, :, HD : 2 * HD].reshape(512, HD)
            turned = lax.dot_general(eye, v, (((1,), (1,)), ((), ())), preferred_element_type=F32)
            vt_ref[c, 0:HD, :] = turned.astype(BF)
            vt_ref[c, HD : HD + 16, :] = jnp.ones((16, 512), BF)
        row = lax.broadcasted_iota(jnp.int32, (512, 128), 0)
        col = lax.broadcasted_iota(jnp.int32, (512, 128), 1)
        inner = row % 128
        key_pos = (
            (row // 128 - own_y % 4) * 512 + (inner // 16) * 64 + inner % 16 + 16 * own_x - col % 64
        )
        for z in range(8):
            bias_ref[:, z * 128 : (z + 1) * 128] = jnp.where(key_pos <= z * 64, 0.0, NEG)

    tiles = block * 8 + own_y
    chunk_count = tiles // 4
    q_raw = q_ref[0]
    q = jnp.concatenate([q_raw[:, :, 0:HD], q_raw[:, :, HD : 2 * HD]], axis=1).reshape(cols, HD)
    group = 1024
    groups = [(g * group, q[g * group : (g + 1) * group]) for g in range(cols // group)]

    def scores(k, q_group):
        return lax.dot_general(k, q_group, (((1,), (1,)), ((), ())), preferred_element_type=F32)

    first_keys = kv_ref[0, 0, :, 0:HD]
    hide = jnp.where(tiles == 0, 1.0, 0.0)
    for start, q_group in groups:
        part = slice(start, start + group)
        s = scores(first_keys, q_group) + bias_ref[0:128, part] * hide
        m_ref[:, part] = jnp.maximum(jnp.max(s, axis=0, keepdims=True), LOW)
        top_ref[:, part] = jnp.max(s.reshape(16, 8, group), axis=0)
        acc_ref[:, part] = jnp.zeros((HD + 16, group), F32)

    def quick(c, masked):
        k = keys(c)
        values = vt_ref[c]
        found = [scores(k, q_group) for _, q_group in groups]
        for (start, _), s in zip(groups, found):
            part = slice(start, start + group)
            if masked:
                s = s + bias_ref[:, part]
            p = jnp.exp2(s * scale - m_ref[:, part] * scale).astype(BF)
            top_ref[:, part] = jnp.maximum(
                top_ref[:, part], jnp.max(s.reshape(64, 8, group), axis=0)
            )
            acc_ref[:, part] = acc_ref[:, part] + jnp.dot(values, p, preferred_element_type=F32)

    def quick_step(c, carry):
        quick(c, False)
        return carry

    lax.fori_loop(0, chunk_count, quick_step, 0)
    quick(chunk_count, True)

    def careful(c, masked):
        k = keys(c)
        values = vt_ref[c]
        for start, q_group in groups:
            part = slice(start, start + group)
            s = scores(k, q_group)
            if masked:
                s = s + bias_ref[:, part]
            m_old = m_ref[:, part]
            m = jnp.maximum(m_old, jnp.max(s, axis=0, keepdims=True))
            p = jnp.exp2((s - m) * scale).astype(BF)
            alpha = jnp.exp2((m_old - m) * scale)
            m_ref[:, part] = m
            acc_ref[:, part] = acc_ref[:, part] * alpha + jnp.dot(
                values, p, preferred_element_type=F32
            )

    def careful_step(c, carry):
        careful(c, False)
        return carry

    rise = jnp.max((top_ref[...] - m_ref[...]) * scale)

    @pl.when(rise > 64.0)
    def _():
        m_ref[...] = jnp.full((1, cols), LOW, F32)
        acc_ref[...] = jnp.zeros((HD + 16, cols), F32)
        lax.fori_loop(0, chunk_count, careful_step, 0)
        careful(chunk_count, True)

    total = acc_ref[HD : HD + 1, :]
    seen = total > 0.0
    safe = jnp.where(seen, total, 1.0)
    out = (acc_ref[0:HD, :] * (1.0 / safe)).astype(BF)
    level = jnp.where(seen, m_ref[...] * scale + jnp.log(safe) * LOG2E, NEG)
    first = level.astype(BF).astype(F32)
    second = (level - first).astype(BF).astype(F32)
    third = level - first - second
    pick = lax.broadcasted_iota(jnp.int32, (STAT, cols), 0)
    stats = jnp.where(pick == 0, first, jnp.where(pick == 1, second, jnp.where(pick == 2, third, 0.0)))
    stats = stats.astype(BF)
    for i in range(8):
        o_ref[0, i, 0:HD, :] = out[:, i * 128 : (i + 1) * 128]
        o_ref[0, i, HD : HD + STAT, :] = stats[:, i * 128 : (i + 1) * 128]


def flash(position, queries, key_values):
    return pl.pallas_call(
        flash_kernel,
        grid_spec=pltpu.PrefetchScalarGridSpec(
            num_scalar_prefetch=1,
            grid=(4,),
            in_specs=[
                pl.BlockSpec((1, 8, 64, 256), lambda i, s: (i, 0, 0, 0)),
            ]
            + [pl.BlockSpec(block.shape, lambda i, s: (0, 0)) for block in key_values],
            out_specs=pl.BlockSpec((1, 8, HD + STAT, 128), lambda i, s: (i, 0, 0, 0)),
            scratch_shapes=[
                pltpu.VMEM((8, 4, 128, 2 * HD), BF),
                pltpu.VMEM((8, HD + 16, 512), BF),
                pltpu.VMEM((512, 1024), F32),
                pltpu.VMEM((HD + 16, 1024), F32),
                pltpu.VMEM((1, 1024), F32),
                pltpu.VMEM((8, 1024), F32),
            ],
        ),
        out_shape=jax.ShapeDtypeStruct((4, 8, HD + STAT, 128), BF),
        compiler_params=pltpu.CompilerParams(vmem_limit_bytes=40 * 1024 * 1024),
        cost_estimate=pl.CostEstimate(
            flops=4 * 4096 * 2560 * HD, bytes_accessed=5 << 20, transcendentals=4096 * 2560
        ),
        name="flash",
    )(position, queries, *key_values)


def merge_kernel(parts_ref, w_ref, res_ref, gain_ref, hidden_ref, normed_ref):
    step = pl.program_id(0)
    found = []
    for c in range(2):
        levels = []
        for x in range(4):
            st = parts_ref[x, c, HD : HD + STAT, :].astype(F32)
            levels.append(st[0:1] + st[1:2] + st[2:3])
        top = jnp.maximum(jnp.maximum(levels[0], levels[1]), jnp.maximum(levels[2], levels[3]))
        shares = [jnp.exp2(level - top) for level in levels]
        inverse = 1.0 / (shares[0] + shares[1] + shares[2] + shares[3])
        mixed = parts_ref[0, c, 0:HD, :].astype(F32) * (shares[0] * inverse)
        for x in range(1, 4):
            mixed = mixed + parts_ref[x, c, 0:HD, :].astype(F32) * (shares[x] * inverse)
        rows = mixed.T.astype(BF)
        found += [rows[0:64], rows[64:128]]
    part = jnp.dot(jnp.concatenate(found, axis=1), w_ref[...], preferred_element_type=F32)

    @pl.when(step == 0)
    def _():
        hidden_ref[...] = res_ref[...].astype(F32) + part

    @pl.when(step > 0)
    def _():
        hidden_ref[...] = hidden_ref[...] + part

    @pl.when(step == 3)
    def _():
        hidden = hidden_ref[...]
        mean_square = jnp.mean(hidden * hidden, axis=1, keepdims=True)
        normed = (hidden * lax.rsqrt(mean_square + 1e-6) * gain_ref[...]).astype(BF)
        for i in range(4):
            normed_ref[i] = normed


def merge(parts, weight, residual, gain):
    tokens, width = residual.shape
    whole = pl.BlockSpec((tokens, width), lambda c: (0, 0))
    return pl.pallas_call(
        merge_kernel,
        grid=(4,),
        in_specs=[
            pl.BlockSpec((4, 2, HD + STAT, 128), lambda c: (0, c, 0, 0)),
            pl.BlockSpec((512, width), lambda c: (c, 0)),
            whole,
            pl.BlockSpec((1, width), lambda c: (0, 0)),
        ],
        out_specs=[whole, pl.BlockSpec((4, tokens, width), lambda c: (0, 0, 0))],
        out_shape=[
            jax.ShapeDtypeStruct((tokens, width), F32),
            jax.ShapeDtypeStruct((4, tokens, width), BF),
        ],
        name="merge",
    )(parts, weight, residual, gain)


def select_kernel(sel_ref, x_ref, o_ref, tmp_ref):
    count = sel_ref.shape[0]
    sel = sel_ref[...]
    for j in range(0, 8, 2):
        got = jnp.dot(sel, x_ref[:, j * 128 : (j + 2) * 128], preferred_element_type=F32)
        tmp_ref[pl.ds(j, count, stride=8), :] = got[:, 0:128]
        tmp_ref[pl.ds(j + 1, count, stride=8), :] = got[:, 128:256]
    o_ref[...] = tmp_ref[...].astype(BF)


def select(chosen, tokens):
    count = chosen.shape[0]
    return pl.pallas_call(
        select_kernel,
        out_shape=jax.ShapeDtypeStruct((count * 8, 128), BF),
        scratch_shapes=[pltpu.VMEM((count * 8, 128), F32)],
        compiler_params=pltpu.CompilerParams(vmem_limit_bytes=40 * 1024 * 1024),
        name="select",
    )(chosen, tokens)


def expert_kernel(x_ref, win_ref, wout_ref, o_ref, tmp_ref):
    rows = x_ref.shape[0] // 8
    inner = wout_ref.shape[0]
    tmp_ref[...] = x_ref[...].astype(F32)
    x = jnp.concatenate(
        [tmp_ref[pl.ds(j, rows, stride=8), :].astype(BF) for j in range(8)], axis=1
    )
    projection = jnp.dot(x, win_ref[...], preferred_element_type=F32)
    gate = projection[:, 0:inner]
    activated = (gate / (1.0 + jnp.exp(-gate)) * projection[:, inner:]).astype(BF)
    out = jnp.dot(activated, wout_ref[...], preferred_element_type=F32)
    for j in range(8):
        tmp_ref[pl.ds(j, rows, stride=8), :] = out[:, j * 128 : (j + 1) * 128]
    o_ref[...] = tmp_ref[...].astype(BF)


def expert(rows_in, weight_in, weight_out):
    total = rows_in.shape[0]
    block = total // 4
    return pl.pallas_call(
        expert_kernel,
        grid=(4,),
        in_specs=[
            pl.BlockSpec((block, 128), lambda i: (i, 0)),
            pl.BlockSpec(weight_in.shape, lambda i: (0, 0)),
            pl.BlockSpec(weight_out.shape, lambda i: (0, 0)),
        ],
        out_specs=pl.BlockSpec((block, 128), lambda i: (i, 0)),
        out_shape=jax.ShapeDtypeStruct((total, 128), BF),
        scratch_shapes=[pltpu.VMEM((block, 128), F32)],
        compiler_params=pltpu.CompilerParams(vmem_limit_bytes=40 * 1024 * 1024),
        name="expert",
    )(rows_in, weight_in, weight_out)


def gather_kernel(gates_ref, x_ref, o_ref, tmp_ref):
    count = gates_ref.shape[1]
    gates = gates_ref[...]
    tmp_ref[...] = x_ref[...].astype(F32)
    for j in range(0, 8, 2):
        x = jnp.concatenate(
            [
                tmp_ref[pl.ds(j, count, stride=8), :].astype(BF),
                tmp_ref[pl.ds(j + 1, count, stride=8), :].astype(BF),
            ],
            axis=1,
        )
        o_ref[:, j * 128 : (j + 2) * 128] = jnp.dot(
            gates, x, preferred_element_type=F32
        ).astype(BF)


def gather(gates, rows):
    count = gates.shape[1]
    return pl.pallas_call(
        gather_kernel,
        out_shape=jax.ShapeDtypeStruct((gates.shape[0], 1024), BF),
        scratch_shapes=[pltpu.VMEM((count * 8, 128), F32)],
        compiler_params=pltpu.CompilerParams(vmem_limit_bytes=40 * 1024 * 1024),
        name="gather",
    )(gates, rows)


def pack_kv_kernel(k_ref, v_ref, o_ref):
    for g in range(2):
        lanes = slice(g * HD, (g + 1) * HD)
        both = jnp.concatenate([k_ref[:, lanes], v_ref[:, lanes]], axis=1)
        for x in range(4):
            for i in range(4):
                o_ref[x * 8 + g * 4 + i] = both[16 * x : 16 * x + 16]


def pack_kv(keys, values):
    return pl.pallas_call(
        pack_kv_kernel,
        out_shape=jax.ShapeDtypeStruct((32, 16, 2 * HD), BF),
        name="pack_kv",
    )(keys, values)


def pack_q_kernel(q_ref, o_ref):
    for z in range(8):
        piece = q_ref[:, z * 2 * HD : (z + 1) * 2 * HD]
        for x in range(4):
            o_ref[x * 8 + z] = piece


def pack_q(queries):
    return pl.pallas_call(
        pack_q_kernel,
        out_shape=jax.ShapeDtypeStruct((32, queries.shape[0], 2 * HD), BF),
        cost_estimate=pl.CostEstimate(flops=0, bytes_accessed=5 << 18, transcendentals=0),
        name="pack_q",
    )(queries)


def local(
    residual,
    queries,
    key_vectors,
    value_vectors,
    output_weight,
    norm_gain,
    routes,
    gate_levels,
    expert_in,
    expert_out,
):
    tokens, width = residual.shape
    own_x = lax.axis_index("x")
    own_y = lax.axis_index("y")
    own_y2 = own_y // 2
    position = jnp.stack([own_x, own_y]).astype(jnp.int32)

    key_value = pack_kv(key_vectors, value_vectors)
    key_value = lax.all_to_all(key_value, ("x", "z"), split_axis=0, concat_axis=0, tiled=True)
    listing = jnp.concatenate([routes.T, gate_levels.T], axis=0).astype(BF)
    listing = jnp.pad(listing, ((0, 0), (0, 2 * HD - tokens)))
    block = jnp.concatenate([key_value.reshape(512, 2 * HD), listing], axis=0)
    up = [(i, (i + 1) % 8) for i in range(8)]
    down = [(i, (i - 1) % 8) for i in range(8)]
    ups, downs = [block], [block]
    for step in range(4):
        ups.append(lax.ppermute(ups[-1], "y", up))
        if step < 3:
            downs.append(lax.ppermute(downs[-1], "y", down))
    key_values = ups + downs[1:]

    query = lax.all_to_all(pack_q(queries), ("x", "z"), split_axis=0, concat_axis=0, tiled=True).reshape(
        4, 8, tokens, 2 * HD
    )

    whole_weight = lax.all_gather(output_weight, "z", axis=0, tiled=True)

    shards = flash(position, query, key_values)
    parts = lax.all_to_all(
        shards.reshape(32, HD + STAT, 128), ("x", "z"), split_axis=0, concat_axis=0, tiled=True
    ).reshape(4, 8, HD + STAT, 128)
    whole_weight, own_in, own_out = lax.optimization_barrier(
        (whole_weight, expert_in[0], expert_out[0])
    )
    other_in = lax.ppermute(own_in, "y", SWAP)
    other_out = lax.ppermute(own_out, "y", SWAP)
    ringed = jnp.stack([part[512:, :tokens] for part in [block, *downs[1:], ups[4], ups[3], ups[2], ups[1]]])
    members = jnp.where((own_y % 2) == own_y // 4, jnp.array(CLASSES[0]), jnp.array(CLASSES[1]))
    listing = jnp.stack(
        [lax.dynamic_index_in_dim(ringed, (members[i] - own_y) & 7, 0, False) for i in range(4)]
    ).astype(jnp.int32)
    named, levels = listing[:, None, 0:8], listing[:, None, 8:16]
    q = jnp.arange(32, dtype=jnp.int32)
    match = named == ((q % 8) * 16 + (q // 8) * 4 + own_y2)[None, :, None, None]
    hits = jnp.any(match, axis=2)
    gates = jnp.sum(jnp.where(match, levels, 0), axis=2).astype(F32) / 256.0
    before = jnp.triu(jnp.ones((tokens, tokens), BF), 1)
    ranks = jnp.einsum("sqb,ba->sqa", hits.astype(BF), before, preferred_element_type=F32)
    ranks = jnp.where(hits, ranks.astype(jnp.int32), -1)
    slots = jnp.arange(CAP, dtype=jnp.int32)[None, None, :, None, None]
    same = jnp.eye(4, dtype=jnp.bool_)[None, :, None, :, None]
    placed = (ranks.transpose(1, 0, 2)[:, None, None] == slots) & same
    chosen = placed.astype(BF).reshape(32 * 4 * CAP, 4 * tokens)
    shares = jnp.where(placed, gates.transpose(1, 0, 2)[:, None, None], 0.0).astype(BF)
    shares = shares.reshape(32 * 4 * CAP, 4 * tokens).T

    hidden, spread = merge(
        parts, whole_weight, residual, norm_gain.reshape(1, width)
    )

    spread, other_in, other_out = lax.optimization_barrier((spread, other_in, other_out))
    half = own_in.shape[1] // 2
    weight_in = jnp.concatenate(
        [own_in[:, :half], other_in[:, :half], own_in[:, half:], other_in[:, half:]], axis=1
    )
    weight_out = jnp.concatenate([own_out, other_out], axis=0)
    spread = lax.all_to_all(
        spread, "y", split_axis=0, concat_axis=0, axis_index_groups=CLASSES, tiled=True
    )
    outgoing = select(chosen, spread.reshape(4 * tokens, width))
    arrived = lax.all_to_all(
        outgoing.reshape(32, 4 * CAP * 8, 128), ("x", "z"), split_axis=0, concat_axis=0, tiled=True
    )
    done = expert(arrived.reshape(-1, 128), weight_in, weight_out)
    answers = lax.all_to_all(
        done.reshape(32, 4 * CAP * 8, 128), ("x", "z"), split_axis=0, concat_axis=0, tiled=True
    )
    sums = gather(shares, answers.reshape(-1, 128))
    sums = lax.all_to_all(
        sums.reshape(4, tokens, width),
        "y",
        split_axis=0,
        concat_axis=0,
        axis_index_groups=CLASSES,
        tiled=True,
    )
    return hidden + jnp.sum(sums.astype(F32), axis=0)


def solution(mesh):
    fine = Mesh(mesh.devices.reshape(8, 4, 8, 2), ("z", "x", "y", "dp"))
    rows = P(("dp", "x", "y", "z"), None)
    halves = P(("z", "x", "y"), None, None)
    return jax.shard_map(
        local,
        mesh=fine,
        in_specs=(rows, rows, rows, rows, P("z", None), P(), rows, rows, halves, halves),
        out_specs=rows,
        check_vma=False,
    )
```

```python
import math

import jax
import jax.numpy as jnp
from jax import lax
from jax.experimental import pallas as pl
from jax.experimental.pallas import tpu as pltpu
from jax.sharding import Mesh
from jax.sharding import PartitionSpec as P

HD = 128
CAP = 5
LOG2E = 1.4426950408889634
BF = jnp.bfloat16
F32 = jnp.float32
NEG = -1e30
LOW = -1e29
STAT = 8
SWAP = [(i, i ^ 1) for i in range(8)]
CLASSES = [[z * 8 + y for z in range(8) for y in ys] for ys in ((0, 2, 5, 7), (1, 3, 4, 6))]


def flash_kernel(
    pos_ref, q_ref, b0, b1, b2, b3, b4, b5, b6, b7, o_ref, kv_ref, vt_ref, bias_ref, acc_ref, m_ref, top_ref
):
    block = pl.program_id(0)
    own_x = pos_ref[0]
    own_y = pos_ref[1]
    cols = 1024
    scale = LOG2E / math.sqrt(HD)

    def keys(c):
        return kv_ref[pl.ds(4 * (c % 2), 4), c // 2, :, 0:HD].reshape(512, HD)

    @pl.when(block == 0)
    def _():
        eye = (
            lax.broadcasted_iota(jnp.int32, (HD, HD), 0)
            == lax.broadcasted_iota(jnp.int32, (HD, HD), 1)
        ).astype(BF)
        for far, ref in enumerate((b0, b5, b6, b7, b4, b3, b2, b1)):
            kv_ref[(own_y + far) % 8] = ref[...].reshape(4, 128, 2 * HD)
        for c in range(8):
            v = kv_ref[4 * (c % 2) : 4 * (c % 2) + 4, c // 2, :, HD : 2 * HD].reshape(512, HD)
            turned = lax.dot_general(eye, v, (((1,), (1,)), ((), ())), preferred_element_type=F32)
            vt_ref[c, 0:HD, :] = turned.astype(BF)
            vt_ref[c, HD : HD + 16, :] = jnp.ones((16, 512), BF)
        row = lax.broadcasted_iota(jnp.int32, (512, 128), 0)
        col = lax.broadcasted_iota(jnp.int32, (512, 128), 1)
        inner = row % 128
        key_pos = (
            (row // 128 - own_y % 4) * 512 + (inner // 16) * 64 + inner % 16 + 16 * own_x - col % 64
        )
        for z in range(8):
            bias_ref[:, z * 128 : (z + 1) * 128] = jnp.where(key_pos <= z * 64, 0.0, NEG)

    tiles = block * 8 + own_y
    chunk_count = tiles // 4
    q_raw = q_ref[0]
    q = jnp.concatenate([q_raw[:, :, 0:HD], q_raw[:, :, HD : 2 * HD]], axis=1).reshape(cols, HD)
    group = 1024
    groups = [(g * group, q[g * group : (g + 1) * group]) for g in range(cols // group)]

    def scores(k, q_group):
        return lax.dot_general(k, q_group, (((1,), (1,)), ((), ())), preferred_element_type=F32)

    first_keys = kv_ref[0, 0, :, 0:HD]
    hide = jnp.where(tiles == 0, 1.0, 0.0)
    for start, q_group in groups:
        part = slice(start, start + group)
        s = scores(first_keys, q_group) + bias_ref[0:128, part] * hide
        m_ref[:, part] = jnp.maximum(jnp.max(s, axis=0, keepdims=True), LOW)
        top_ref[:, part] = jnp.max(s.reshape(16, 8, group), axis=0)
        acc_ref[:, part] = jnp.zeros((HD + 16, group), F32)

    def quick(c, masked):
        k = keys(c)
        values = vt_ref[c]
        found = [scores(k, q_group) for _, q_group in groups]
        for (start, _), s in zip(groups, found):
            part = slice(start, start + group)
            if masked:
                s = s + bias_ref[:, part]
            p = jnp.exp2(s * scale - m_ref[:, part] * scale).astype(BF)
            top_ref[:, part] = jnp.maximum(
                top_ref[:, part], jnp.max(s.reshape(64, 8, group), axis=0)
            )
            acc_ref[:, part] = acc_ref[:, part] + jnp.dot(values, p, preferred_element_type=F32)

    def quick_step(c, carry):
        quick(c, False)
        return carry

    lax.fori_loop(0, chunk_count, quick_step, 0)
    quick(chunk_count, True)

    def careful(c, masked):
        k = keys(c)
        values = vt_ref[c]
        for start, q_group in groups:
            part = slice(start, start + group)
            s = scores(k, q_group)
            if masked:
                s = s + bias_ref[:, part]
            m_old = m_ref[:, part]
            m = jnp.maximum(m_old, jnp.max(s, axis=0, keepdims=True))
            p = jnp.exp2((s - m) * scale).astype(BF)
            alpha = jnp.exp2((m_old - m) * scale)
            m_ref[:, part] = m
            acc_ref[:, part] = acc_ref[:, part] * alpha + jnp.dot(
                values, p, preferred_element_type=F32
            )

    def careful_step(c, carry):
        careful(c, False)
        return carry

    rise = jnp.max((top_ref[...] - m_ref[...]) * scale)

    @pl.when(rise > 64.0)
    def _():
        m_ref[...] = jnp.full((1, cols), LOW, F32)
        acc_ref[...] = jnp.zeros((HD + 16, cols), F32)
        lax.fori_loop(0, chunk_count, careful_step, 0)
        careful(chunk_count, True)

    total = acc_ref[HD : HD + 1, :]
    seen = total > 0.0
    safe = jnp.where(seen, total, 1.0)
    out = (acc_ref[0:HD, :] * (1.0 / safe)).astype(BF)
    level = jnp.where(seen, m_ref[...] * scale + jnp.log(safe) * LOG2E, NEG)
    first = level.astype(BF).astype(F32)
    second = (level - first).astype(BF).astype(F32)
    third = level - first - second
    pick = lax.broadcasted_iota(jnp.int32, (STAT, cols), 0)
    stats = jnp.where(pick == 0, first, jnp.where(pick == 1, second, jnp.where(pick == 2, third, 0.0)))
    stats = stats.astype(BF)
    for i in range(8):
        o_ref[0, i, 0:HD, :] = out[:, i * 128 : (i + 1) * 128]
        o_ref[0, i, HD : HD + STAT, :] = stats[:, i * 128 : (i + 1) * 128]


def flash(position, queries, key_values):
    return pl.pallas_call(
        flash_kernel,
        grid_spec=pltpu.PrefetchScalarGridSpec(
            num_scalar_prefetch=1,
            grid=(4,),
            in_specs=[
                pl.BlockSpec((1, 8, 64, 256), lambda i, s: (i, 0, 0, 0)),
            ]
            + [pl.BlockSpec(block.shape, lambda i, s: (0, 0)) for block in key_values],
            out_specs=pl.BlockSpec((1, 8, HD + STAT, 128), lambda i, s: (i, 0, 0, 0)),
            scratch_shapes=[
                pltpu.VMEM((8, 4, 128, 2 * HD), BF),
                pltpu.VMEM((8, HD + 16, 512), BF),
                pltpu.VMEM((512, 1024), F32),
                pltpu.VMEM((HD + 16, 1024), F32),
                pltpu.VMEM((1, 1024), F32),
                pltpu.VMEM((8, 1024), F32),
            ],
        ),
        out_shape=jax.ShapeDtypeStruct((4, 8, HD + STAT, 128), BF),
        compiler_params=pltpu.CompilerParams(vmem_limit_bytes=40 * 1024 * 1024),
        cost_estimate=pl.CostEstimate(
            flops=4 * 4096 * 2560 * HD, bytes_accessed=5 << 20, transcendentals=4096 * 2560
        ),
        name="flash",
    )(position, queries, *key_values)


def merge_kernel(parts_ref, w_ref, res_ref, gain_ref, hidden_ref, normed_ref):
    step = pl.program_id(0)
    found = []
    for c in range(2):
        levels = []
        for x in range(4):
            st = parts_ref[x, c, HD : HD + STAT, :].astype(F32)
            levels.append(st[0:1] + st[1:2] + st[2:3])
        top = jnp.maximum(jnp.maximum(levels[0], levels[1]), jnp.maximum(levels[2], levels[3]))
        shares = [jnp.exp2(level - top) for level in levels]
        inverse = 1.0 / (shares[0] + shares[1] + shares[2] + shares[3])
        mixed = parts_ref[0, c, 0:HD, :].astype(F32) * (shares[0] * inverse)
        for x in range(1, 4):
            mixed = mixed + parts_ref[x, c, 0:HD, :].astype(F32) * (shares[x] * inverse)
        rows = mixed.T.astype(BF)
        found += [rows[0:64], rows[64:128]]
    part = jnp.dot(jnp.concatenate(found, axis=1), w_ref[...], preferred_element_type=F32)

    @pl.when(step == 0)
    def _():
        hidden_ref[...] = res_ref[...].astype(F32) + part

    @pl.when(step > 0)
    def _():
        hidden_ref[...] = hidden_ref[...] + part

    @pl.when(step == 3)
    def _():
        hidden = hidden_ref[...]
        mean_square = jnp.mean(hidden * hidden, axis=1, keepdims=True)
        normed = (hidden * lax.rsqrt(mean_square + 1e-6) * gain_ref[...]).astype(BF)
        for i in range(4):
            normed_ref[i] = normed


def merge(parts, weight, residual, gain):
    tokens, width = residual.shape
    whole = pl.BlockSpec((tokens, width), lambda c: (0, 0))
    return pl.pallas_call(
        merge_kernel,
        grid=(4,),
        in_specs=[
            pl.BlockSpec((4, 2, HD + STAT, 128), lambda c: (0, c, 0, 0)),
            pl.BlockSpec((512, width), lambda c: (c, 0)),
            whole,
            pl.BlockSpec((1, width), lambda c: (0, 0)),
        ],
        out_specs=[whole, pl.BlockSpec((4, tokens, width), lambda c: (0, 0, 0))],
        out_shape=[
            jax.ShapeDtypeStruct((tokens, width), F32),
            jax.ShapeDtypeStruct((4, tokens, width), BF),
        ],
        name="merge",
    )(parts, weight, residual, gain)


def select_kernel(sel_ref, x_ref, o_ref, tmp_ref):
    count = sel_ref.shape[0]
    sel = sel_ref[...]
    for j in range(0, 8, 2):
        got = jnp.dot(sel, x_ref[:, j * 128 : (j + 2) * 128], preferred_element_type=F32)
        tmp_ref[pl.ds(j, count, stride=8), :] = got[:, 0:128]
        tmp_ref[pl.ds(j + 1, count, stride=8), :] = got[:, 128:256]
    o_ref[...] = tmp_ref[...].astype(BF)


def select(chosen, tokens):
    count = chosen.shape[0]
    return pl.pallas_call(
        select_kernel,
        out_shape=jax.ShapeDtypeStruct((count * 8, 128), BF),
        scratch_shapes=[pltpu.VMEM((count * 8, 128), F32)],
        compiler_params=pltpu.CompilerParams(vmem_limit_bytes=40 * 1024 * 1024),
        name="select",
    )(chosen, tokens)


def expert_kernel(x_ref, win_ref, wout_ref, o_ref, tmp_ref):
    rows = x_ref.shape[0] // 8
    inner = wout_ref.shape[0]
    tmp_ref[...] = x_ref[...].astype(F32)
    x = jnp.concatenate(
        [tmp_ref[pl.ds(j, rows, stride=8), :].astype(BF) for j in range(8)], axis=1
    )
    projection = jnp.dot(x, win_ref[...], preferred_element_type=F32)
    gate = projection[:, 0:inner]
    activated = (gate / (1.0 + jnp.exp(-gate)) * projection[:, inner:]).astype(BF)
    out = jnp.dot(activated, wout_ref[...], preferred_element_type=F32)
    for j in range(8):
        tmp_ref[pl.ds(j, rows, stride=8), :] = out[:, j * 128 : (j + 1) * 128]
    o_ref[...] = tmp_ref[...].astype(BF)


def expert(rows_in, weight_in, weight_out):
    total = rows_in.shape[0]
    block = total // 4
    return pl.pallas_call(
        expert_kernel,
        grid=(4,),
        in_specs=[
            pl.BlockSpec((block, 128), lambda i: (i, 0)),
            pl.BlockSpec(weight_in.shape, lambda i: (0, 0)),
            pl.BlockSpec(weight_out.shape, lambda i: (0, 0)),
        ],
        out_specs=pl.BlockSpec((block, 128), lambda i: (i, 0)),
        out_shape=jax.ShapeDtypeStruct((total, 128), BF),
        scratch_shapes=[pltpu.VMEM((block, 128), F32)],
        compiler_params=pltpu.CompilerParams(vmem_limit_bytes=40 * 1024 * 1024),
        name="expert",
    )(rows_in, weight_in, weight_out)


def gather_kernel(gates_ref, x_ref, o_ref, tmp_ref):
    count = gates_ref.shape[1]
    gates = gates_ref[...]
    tmp_ref[...] = x_ref[...].astype(F32)
    for j in range(0, 8, 2):
        x = jnp.concatenate(
            [
                tmp_ref[pl.ds(j, count, stride=8), :].astype(BF),
                tmp_ref[pl.ds(j + 1, count, stride=8), :].astype(BF),
            ],
            axis=1,
        )
        o_ref[:, j * 128 : (j + 2) * 128] = jnp.dot(
            gates, x, preferred_element_type=F32
        ).astype(BF)


def gather(gates, rows):
    count = gates.shape[1]
    return pl.pallas_call(
        gather_kernel,
        out_shape=jax.ShapeDtypeStruct((gates.shape[0], 1024), BF),
        scratch_shapes=[pltpu.VMEM((count * 8, 128), F32)],
        compiler_params=pltpu.CompilerParams(vmem_limit_bytes=40 * 1024 * 1024),
        name="gather",
    )(gates, rows)


def pack_kv_kernel(k_ref, v_ref, o_ref):
    for g in range(2):
        lanes = slice(g * HD, (g + 1) * HD)
        both = jnp.concatenate([k_ref[:, lanes], v_ref[:, lanes]], axis=1)
        for x in range(4):
            for i in range(4):
                o_ref[x * 8 + g * 4 + i] = both[16 * x : 16 * x + 16]


def pack_kv(keys, values):
    return pl.pallas_call(
        pack_kv_kernel,
        out_shape=jax.ShapeDtypeStruct((32, 16, 2 * HD), BF),
        name="pack_kv",
    )(keys, values)


def pack_q_kernel(q_ref, routes_ref, levels_ref, o_ref):
    tokens = q_ref.shape[0]
    listing = jnp.concatenate(
        [
            routes_ref[...].astype(F32),
            levels_ref[...].astype(F32),
            jnp.zeros((8, 2 * HD - 2 * tokens), F32),
        ],
        axis=1,
    ).astype(BF)
    for z in range(8):
        piece = q_ref[:, z * 2 * HD : (z + 1) * 2 * HD]
        for x in range(4):
            o_ref[x * 8 + z, 0:tokens] = piece
            o_ref[x * 8 + z, tokens : tokens + 8] = listing


def pack_q(queries, routes, levels):
    return pl.pallas_call(
        pack_q_kernel,
        out_shape=jax.ShapeDtypeStruct((32, queries.shape[0] + 8, 2 * HD), BF),
        cost_estimate=pl.CostEstimate(flops=0, bytes_accessed=5 << 18, transcendentals=0),
        name="pack_q",
    )(queries, routes, levels)


def local(
    residual,
    queries,
    key_vectors,
    value_vectors,
    output_weight,
    norm_gain,
    routes,
    gate_levels,
    expert_in,
    expert_out,
):
    tokens, width = residual.shape
    own_x = lax.axis_index("x")
    own_y = lax.axis_index("y")
    position = jnp.stack([own_x, own_y]).astype(jnp.int32)

    key_value = pack_kv(key_vectors, value_vectors)
    key_value = lax.all_to_all(key_value, ("x", "z"), split_axis=0, concat_axis=0, tiled=True)
    block = key_value.reshape(512, 2 * HD)
    up = [(i, (i + 1) % 8) for i in range(8)]
    down = [(i, (i - 1) % 8) for i in range(8)]
    ups, downs = [block], [block]
    for step in range(4):
        ups.append(lax.ppermute(ups[-1], "y", up))
        if step < 3:
            downs.append(lax.ppermute(downs[-1], "y", down))
    key_values = ups + downs[1:]

    query = lax.all_to_all(
        pack_q(queries, routes.T, gate_levels.T), ("x", "z"), split_axis=0, concat_axis=0, tiled=True
    ).reshape(4, 8, tokens + 8, 2 * HD)

    whole_weight = lax.all_gather(output_weight, "z", axis=0, tiled=True)

    shards = flash(position, query, key_values)
    parts = lax.all_to_all(
        shards.reshape(32, HD + STAT, 128), ("x", "z"), split_axis=0, concat_axis=0, tiled=True
    ).reshape(4, 8, HD + STAT, 128)
    whole_weight, own_in, own_out = lax.optimization_barrier(
        (whole_weight, expert_in[0], expert_out[0])
    )
    other_in = lax.ppermute(own_in, "y", SWAP)
    other_out = lax.ppermute(own_out, "y", SWAP)
    listing = lax.dynamic_index_in_dim(query, lax.axis_index("z"), 1, False)[:, tokens:]
    listing = listing.astype(jnp.int32)
    named, levels = listing[:, None, :, 0:tokens], listing[:, None, :, tokens : 2 * tokens]
    q = jnp.arange(32, dtype=jnp.int32)
    match = named == ((q // 4) * 16 + own_x * 4 + q % 4)[None, :, None, None]
    hits = jnp.any(match, axis=2)
    gates = jnp.sum(jnp.where(match, levels, 0), axis=2).astype(F32) / 256.0
    before = jnp.triu(jnp.ones((tokens, tokens), BF), 1)
    ranks = jnp.einsum("sqb,ba->sqa", hits.astype(BF), before, preferred_element_type=F32)
    ranks = jnp.where(hits, ranks.astype(jnp.int32), -1)
    slots = jnp.arange(CAP, dtype=jnp.int32)[None, None, :, None, None]
    same = jnp.eye(4, dtype=jnp.bool_)[None, :, None, :, None]
    placed = (ranks.transpose(1, 0, 2)[:, None, None] == slots) & same
    chosen = placed.astype(BF).reshape(32 * 4 * CAP, 4 * tokens)
    shares = jnp.where(placed, gates.transpose(1, 0, 2)[:, None, None], 0.0).astype(BF)
    shares = shares.reshape(32 * 4 * CAP, 4 * tokens).T

    hidden, spread = merge(
        parts, whole_weight, residual, norm_gain.reshape(1, width)
    )

    spread, other_in, other_out = lax.optimization_barrier((spread, other_in, other_out))
    half = own_in.shape[1] // 2
    weight_in = jnp.concatenate(
        [own_in[:, :half], other_in[:, :half], own_in[:, half:], other_in[:, half:]], axis=1
    )
    weight_out = jnp.concatenate([own_out, other_out], axis=0)
    spread = lax.all_to_all(
        spread, "x", split_axis=0, concat_axis=0, tiled=True
    )
    outgoing = select(chosen, spread.reshape(4 * tokens, width))
    arrived = lax.all_to_all(
        outgoing.reshape(32, 4 * CAP * 8, 128), ("z", "y"), split_axis=0, concat_axis=0,
        axis_index_groups=CLASSES, tiled=True,
    )
    done = expert(arrived.reshape(-1, 128), weight_in, weight_out)
    answers = lax.all_to_all(
        done.reshape(32, 4 * CAP * 8, 128), ("z", "y"), split_axis=0, concat_axis=0,
        axis_index_groups=CLASSES, tiled=True,
    )
    sums = gather(shares, answers.reshape(-1, 128))
    sums = lax.all_to_all(
        sums.reshape(4, tokens, width),
        "x",
        split_axis=0,
        concat_axis=0,
        tiled=True,
    )
    return hidden + jnp.sum(sums.astype(F32), axis=0)


def solution(mesh):
    fine = Mesh(mesh.devices.reshape(8, 4, 8, 2), ("z", "x", "y", "dp"))
    rows = P(("dp", "x", "y", "z"), None)
    halves = P(("z", "x", "y"), None, None)
    return jax.shard_map(
        local,
        mesh=fine,
        in_specs=(rows, rows, rows, rows, P("z", None), P(), rows, rows, halves, halves),
        out_specs=rows,
        check_vma=False,
    )
```

```python
import math

import jax
import jax.numpy as jnp
from jax import lax
from jax.experimental import pallas as pl
from jax.experimental.pallas import tpu as pltpu
from jax.sharding import Mesh
from jax.sharding import PartitionSpec as P

HD = 128
CAP = 5
LOG2E = 1.4426950408889634
BF = jnp.bfloat16
F32 = jnp.float32
NEG = -1e30
LOW = -1e29
STAT = 8
SWAP = [(0, 1), (1, 0)]


def flash_kernel(
    pos_ref, q_ref, b0, b1, b2, b3, b4, b5, b6, b7, o_ref, kv_ref, vt_ref, bias_ref, acc_ref, m_ref, top_ref
):
    block = pl.program_id(0)
    own_x = pos_ref[0]
    own_y = pos_ref[1]
    cols = 1024
    scale = LOG2E / math.sqrt(HD)

    def keys(c):
        return kv_ref[pl.ds(4 * (c % 2), 4), c // 2, :, 0:HD].reshape(512, HD)

    @pl.when(block == 0)
    def _():
        eye = (
            lax.broadcasted_iota(jnp.int32, (HD, HD), 0)
            == lax.broadcasted_iota(jnp.int32, (HD, HD), 1)
        ).astype(BF)
        for far, ref in enumerate((b0, b5, b6, b7, b4, b3, b2, b1)):
            kv_ref[(own_y + far) % 8] = ref[0:512, :].reshape(4, 128, 2 * HD)
        for c in range(8):
            v = kv_ref[4 * (c % 2) : 4 * (c % 2) + 4, c // 2, :, HD : 2 * HD].reshape(512, HD)
            turned = lax.dot_general(eye, v, (((1,), (1,)), ((), ())), preferred_element_type=F32)
            vt_ref[c, 0:HD, :] = turned.astype(BF)
            vt_ref[c, HD : HD + 16, :] = jnp.ones((16, 512), BF)
        row = lax.broadcasted_iota(jnp.int32, (512, 128), 0)
        col = lax.broadcasted_iota(jnp.int32, (512, 128), 1)
        inner = row % 128
        key_pos = (
            (row // 128 - own_y % 4) * 512 + (inner // 16) * 64 + inner % 16 + 16 * own_x - col % 64
        )
        for z in range(8):
            bias_ref[:, z * 128 : (z + 1) * 128] = jnp.where(key_pos <= z * 64, 0.0, NEG)

    tiles = block * 8 + own_y
    chunk_count = tiles // 4
    q_raw = q_ref[0]
    q = jnp.concatenate([q_raw[:, :, 0:HD], q_raw[:, :, HD : 2 * HD]], axis=1).reshape(cols, HD)
    group = 1024
    groups = [(g * group, q[g * group : (g + 1) * group]) for g in range(cols // group)]

    def scores(k, q_group):
        return lax.dot_general(k, q_group, (((1,), (1,)), ((), ())), preferred_element_type=F32)

    first_keys = kv_ref[0, 0, :, 0:HD]
    hide = jnp.where(tiles == 0, 1.0, 0.0)
    for start, q_group in groups:
        part = slice(start, start + group)
        s = scores(first_keys, q_group) + bias_ref[0:128, part] * hide
        m_ref[:, part] = jnp.maximum(jnp.max(s, axis=0, keepdims=True), LOW)
        top_ref[:, part] = jnp.max(s.reshape(16, 8, group), axis=0)
        acc_ref[:, part] = jnp.zeros((HD + 16, group), F32)

    def quick(c, masked):
        k = keys(c)
        values = vt_ref[c]
        found = [scores(k, q_group) for _, q_group in groups]
        for (start, _), s in zip(groups, found):
            part = slice(start, start + group)
            if masked:
                s = s + bias_ref[:, part]
            p = jnp.exp2(s * scale - m_ref[:, part] * scale).astype(BF)
            top_ref[:, part] = jnp.maximum(
                top_ref[:, part], jnp.max(s.reshape(64, 8, group), axis=0)
            )
            acc_ref[:, part] = acc_ref[:, part] + jnp.dot(values, p, preferred_element_type=F32)

    def quick_step(c, carry):
        quick(c, False)
        return carry

    lax.fori_loop(0, chunk_count, quick_step, 0)
    quick(chunk_count, True)

    def careful(c, masked):
        k = keys(c)
        values = vt_ref[c]
        for start, q_group in groups:
            part = slice(start, start + group)
            s = scores(k, q_group)
            if masked:
                s = s + bias_ref[:, part]
            m_old = m_ref[:, part]
            m = jnp.maximum(m_old, jnp.max(s, axis=0, keepdims=True))
            p = jnp.exp2((s - m) * scale).astype(BF)
            alpha = jnp.exp2((m_old - m) * scale)
            m_ref[:, part] = m
            acc_ref[:, part] = acc_ref[:, part] * alpha + jnp.dot(
                values, p, preferred_element_type=F32
            )

    def careful_step(c, carry):
        careful(c, False)
        return carry

    rise = jnp.max((top_ref[...] - m_ref[...]) * scale)

    @pl.when(rise > 64.0)
    def _():
        m_ref[...] = jnp.full((1, cols), LOW, F32)
        acc_ref[...] = jnp.zeros((HD + 16, cols), F32)
        lax.fori_loop(0, chunk_count, careful_step, 0)
        careful(chunk_count, True)

    total = acc_ref[HD : HD + 1, :]
    seen = total > 0.0
    safe = jnp.where(seen, total, 1.0)
    out = (acc_ref[0:HD, :] * (1.0 / safe)).astype(BF)
    level = jnp.where(seen, m_ref[...] * scale + jnp.log(safe) * LOG2E, NEG)
    first = level.astype(BF).astype(F32)
    second = (level - first).astype(BF).astype(F32)
    third = level - first - second
    pick = lax.broadcasted_iota(jnp.int32, (STAT, cols), 0)
    stats = jnp.where(pick == 0, first, jnp.where(pick == 1, second, jnp.where(pick == 2, third, 0.0)))
    stats = stats.astype(BF)
    for i in range(8):
        o_ref[0, i, 0:HD, :] = out[:, i * 128 : (i + 1) * 128]
        o_ref[0, i, HD : HD + STAT, :] = stats[:, i * 128 : (i + 1) * 128]


def flash(position, queries, key_values):
    return pl.pallas_call(
        flash_kernel,
        grid_spec=pltpu.PrefetchScalarGridSpec(
            num_scalar_prefetch=1,
            grid=(4,),
            in_specs=[
                pl.BlockSpec((1, 8, 64, 256), lambda i, s: (i, 0, 0, 0)),
            ]
            + [pl.BlockSpec(block.shape, lambda i, s: (0, 0)) for block in key_values],
            out_specs=pl.BlockSpec((1, 8, HD + STAT, 128), lambda i, s: (i, 0, 0, 0)),
            scratch_shapes=[
                pltpu.VMEM((8, 4, 128, 2 * HD), BF),
                pltpu.VMEM((8, HD + 16, 512), BF),
                pltpu.VMEM((512, 1024), F32),
                pltpu.VMEM((HD + 16, 1024), F32),
                pltpu.VMEM((1, 1024), F32),
                pltpu.VMEM((8, 1024), F32),
            ],
        ),
        out_shape=jax.ShapeDtypeStruct((4, 8, HD + STAT, 128), BF),
        compiler_params=pltpu.CompilerParams(vmem_limit_bytes=40 * 1024 * 1024),
        cost_estimate=pl.CostEstimate(
            flops=4 * 4096 * 2560 * HD, bytes_accessed=5 << 20, transcendentals=4096 * 2560
        ),
        name="flash",
    )(position, queries, *key_values)


def merge_kernel(parts_ref, w_ref, res_ref, gain_ref, hidden_ref, normed_ref):
    step = pl.program_id(0)
    found = []
    for c in range(2):
        levels = []
        for x in range(4):
            st = parts_ref[x, c, HD : HD + STAT, :].astype(F32)
            levels.append(st[0:1] + st[1:2] + st[2:3])
        top = jnp.maximum(jnp.maximum(levels[0], levels[1]), jnp.maximum(levels[2], levels[3]))
        shares = [jnp.exp2(level - top) for level in levels]
        inverse = 1.0 / (shares[0] + shares[1] + shares[2] + shares[3])
        mixed = parts_ref[0, c, 0:HD, :].astype(F32) * (shares[0] * inverse)
        for x in range(1, 4):
            mixed = mixed + parts_ref[x, c, 0:HD, :].astype(F32) * (shares[x] * inverse)
        rows = mixed.T.astype(BF)
        found += [rows[0:64], rows[64:128]]
    part = jnp.dot(jnp.concatenate(found, axis=1), w_ref[...], preferred_element_type=F32)

    @pl.when(step == 0)
    def _():
        hidden_ref[...] = res_ref[...].astype(F32) + part

    @pl.when(step > 0)
    def _():
        hidden_ref[...] = hidden_ref[...] + part

    @pl.when(step == 3)
    def _():
        hidden = hidden_ref[...]
        mean_square = jnp.mean(hidden * hidden, axis=1, keepdims=True)
        normed = (hidden * lax.rsqrt(mean_square + 1e-6) * gain_ref[...]).astype(BF)
        for i in range(4):
            normed_ref[i] = normed


def merge(parts, weight, residual, gain):
    tokens, width = residual.shape
    whole = pl.BlockSpec((tokens, width), lambda c: (0, 0))
    return pl.pallas_call(
        merge_kernel,
        grid=(4,),
        in_specs=[
            pl.BlockSpec((4, 2, HD + STAT, 128), lambda c: (0, c, 0, 0)),
            pl.BlockSpec((512, width), lambda c: (c, 0)),
            whole,
            pl.BlockSpec((1, width), lambda c: (0, 0)),
        ],
        out_specs=[whole, pl.BlockSpec((4, tokens, width), lambda c: (0, 0, 0))],
        out_shape=[
            jax.ShapeDtypeStruct((tokens, width), F32),
            jax.ShapeDtypeStruct((4, tokens, width), BF),
        ],
        compiler_params=pltpu.CompilerParams(vmem_limit_bytes=48 * 1024 * 1024),
        name="merge",
    )(parts, weight, residual, gain)


def select_kernel(sel_ref, x_ref, o_ref, tmp_ref):
    count = sel_ref.shape[0]
    sel = sel_ref[...]
    for j in range(0, 8, 2):
        got = jnp.dot(sel, x_ref[:, j * 128 : (j + 2) * 128], preferred_element_type=F32)
        tmp_ref[pl.ds(j, count, stride=8), :] = got[:, 0:128]
        tmp_ref[pl.ds(j + 1, count, stride=8), :] = got[:, 128:256]
    o_ref[...] = tmp_ref[...].astype(BF)


def select(chosen, tokens):
    count = chosen.shape[0]
    return pl.pallas_call(
        select_kernel,
        out_shape=jax.ShapeDtypeStruct((count * 8, 128), BF),
        scratch_shapes=[pltpu.VMEM((count * 8, 128), F32)],
        compiler_params=pltpu.CompilerParams(vmem_limit_bytes=14 * 1024 * 1024),
        name="select",
    )(chosen, tokens)


def expert_kernel(x_ref, win_ref, wout_ref, o_ref, tmp_ref):
    rows = x_ref.shape[0] // 8
    inner = wout_ref.shape[0]
    tmp_ref[...] = x_ref[...].astype(F32)
    x = jnp.concatenate(
        [tmp_ref[pl.ds(j, rows, stride=8), :].astype(BF) for j in range(8)], axis=1
    )
    projection = jnp.dot(x, win_ref[...], preferred_element_type=F32)
    gate = projection[:, 0:inner]
    activated = (gate / (1.0 + jnp.exp(-gate)) * projection[:, inner:]).astype(BF)
    out = jnp.dot(activated, wout_ref[...], preferred_element_type=F32)
    for j in range(8):
        tmp_ref[pl.ds(j, rows, stride=8), :] = out[:, j * 128 : (j + 1) * 128]
    o_ref[...] = tmp_ref[...].astype(BF)


def expert(rows_in, weight_in, weight_out):
    total = rows_in.shape[0]
    block = total // 4
    return pl.pallas_call(
        expert_kernel,
        grid=(4,),
        in_specs=[
            pl.BlockSpec((block, 128), lambda i: (i, 0)),
            pl.BlockSpec(weight_in.shape, lambda i: (0, 0)),
            pl.BlockSpec(weight_out.shape, lambda i: (0, 0)),
        ],
        out_specs=pl.BlockSpec((block, 128), lambda i: (i, 0)),
        out_shape=jax.ShapeDtypeStruct((total, 128), BF),
        scratch_shapes=[pltpu.VMEM((block, 128), F32)],
        compiler_params=pltpu.CompilerParams(vmem_limit_bytes=14 * 1024 * 1024),
        name="expert",
    )(rows_in, weight_in, weight_out)


def gather_kernel(gates_ref, x_ref, o_ref, tmp_ref):
    count = gates_ref.shape[1]
    gates = gates_ref[...]
    tmp_ref[...] = x_ref[...].astype(F32)
    for j in range(0, 8, 2):
        x = jnp.concatenate(
            [
                tmp_ref[pl.ds(j, count, stride=8), :].astype(BF),
                tmp_ref[pl.ds(j + 1, count, stride=8), :].astype(BF),
            ],
            axis=1,
        )
        o_ref[:, j * 128 : (j + 2) * 128] = jnp.dot(
            gates, x, preferred_element_type=F32
        ).astype(BF)


def gather(gates, rows):
    count = gates.shape[1]
    return pl.pallas_call(
        gather_kernel,
        out_shape=jax.ShapeDtypeStruct((gates.shape[0], 1024), BF),
        scratch_shapes=[pltpu.VMEM((count * 8, 128), F32)],
        compiler_params=pltpu.CompilerParams(vmem_limit_bytes=14 * 1024 * 1024),
        name="gather",
    )(gates, rows)


def pack_kv_kernel(k_ref, v_ref, o_ref):
    for g in range(2):
        lanes = slice(g * HD, (g + 1) * HD)
        both = jnp.concatenate([k_ref[:, lanes], v_ref[:, lanes]], axis=1)
        for x in range(4):
            for i in range(4):
                o_ref[x * 8 + g * 4 + i] = both[16 * x : 16 * x + 16]


def pack_kv(keys, values):
    return pl.pallas_call(
        pack_kv_kernel,
        out_shape=jax.ShapeDtypeStruct((32, 16, 2 * HD), BF),
        name="pack_kv",
    )(keys, values)


def pack_q_kernel(q_ref, o_ref):
    for z in range(8):
        piece = q_ref[:, z * 2 * HD : (z + 1) * 2 * HD]
        for x in range(4):
            o_ref[x * 8 + z] = piece


def pack_q(queries):
    return pl.pallas_call(
        pack_q_kernel,
        out_shape=jax.ShapeDtypeStruct((32, queries.shape[0], 2 * HD), BF),
        cost_estimate=pl.CostEstimate(flops=0, bytes_accessed=5 << 18, transcendentals=0),
        name="pack_q",
    )(queries)


def local(
    residual,
    queries,
    key_vectors,
    value_vectors,
    output_weight,
    norm_gain,
    routes,
    gate_levels,
    expert_in,
    expert_out,
):
    tokens, width = residual.shape
    own_x = lax.axis_index("x")
    own_y2 = lax.axis_index("y2")
    own_y = own_y2 * 2 + lax.axis_index("y1")
    position = jnp.stack([own_x, own_y]).astype(jnp.int32)

    key_value = pack_kv(key_vectors, value_vectors)
    key_value = lax.all_to_all(key_value, ("x", "z"), split_axis=0, concat_axis=0, tiled=True)
    listing = jnp.concatenate([routes.T, gate_levels.T], axis=0).astype(BF)
    listing = jnp.pad(listing, ((0, 0), (0, 2 * HD - tokens)))
    block = jnp.concatenate([key_value.reshape(512, 2 * HD), listing], axis=0)
    up = [(i, (i + 1) % 8) for i in range(8)]
    down = [(i, (i - 1) % 8) for i in range(8)]
    ups, downs = [block], [block]
    for step in range(4):
        ups.append(lax.ppermute(ups[-1], ("y2", "y1"), up))
        if step < 3:
            downs.append(lax.ppermute(downs[-1], ("y2", "y1"), down))
    key_values = ups + downs[1:]

    query = lax.all_to_all(pack_q(queries), ("x", "z"), split_axis=0, concat_axis=0, tiled=True).reshape(
        4, 8, tokens, 2 * HD
    )

    whole_weight = lax.all_gather(output_weight, "z", axis=0, tiled=True)

    shards = flash(position, query, key_values)
    parts = lax.all_to_all(
        shards.reshape(32, HD + STAT, 128), ("x", "z"), split_axis=0, concat_axis=0, tiled=True
    ).reshape(4, 8, HD + STAT, 128)
    whole_weight, own_in, own_out = lax.optimization_barrier(
        (whole_weight, expert_in[0], expert_out[0])
    )
    other_in = lax.ppermute(own_in, "y1", SWAP)
    other_out = lax.ppermute(own_out, "y1", SWAP)
    turned = [ups[0][512:], ups[2][512:], ups[4][512:], downs[2][512:]]
    listing = lax.dynamic_slice_in_dim(
        jnp.stack([turned[k][:, :tokens] for k in (3, 2, 1, 0, 3, 2, 1)]), 3 - own_y2, 4, 0
    ).astype(jnp.int32)
    named, levels = listing[:, None, 0:8], listing[:, None, 8:16]
    q = jnp.arange(32, dtype=jnp.int32)
    match = named == ((q % 8) * 16 + (q // 8) * 4 + own_y2)[None, :, None, None]
    hits = jnp.any(match, axis=2)
    gates = jnp.sum(jnp.where(match, levels, 0), axis=2).astype(F32) / 256.0
    before = jnp.triu(jnp.ones((tokens, tokens), BF), 1)
    ranks = jnp.einsum("sqb,ba->sqa", hits.astype(BF), before, preferred_element_type=F32)
    ranks = jnp.where(hits, ranks.astype(jnp.int32), -1)
    slots = jnp.arange(CAP, dtype=jnp.int32)[None, None, :, None, None]
    same = jnp.eye(4, dtype=jnp.bool_)[None, :, None, :, None]
    placed = (ranks.transpose(1, 0, 2)[:, None, None] == slots) & same
    chosen = placed.astype(BF).reshape(32 * 4 * CAP, 4 * tokens)
    shares = jnp.where(placed, gates.transpose(1, 0, 2)[:, None, None], 0.0).astype(BF)
    shares = shares.reshape(32 * 4 * CAP, 4 * tokens).T

    hidden, spread = merge(
        parts, whole_weight, residual, norm_gain.reshape(1, width)
    )

    spread, other_in, other_out = lax.optimization_barrier((spread, other_in, other_out))
    half = own_in.shape[1] // 2
    weight_in = jnp.concatenate(
        [own_in[:, :half], other_in[:, :half], own_in[:, half:], other_in[:, half:]], axis=1
    )
    weight_out = jnp.concatenate([own_out, other_out], axis=0)
    spread = lax.all_to_all(spread, "y2", split_axis=0, concat_axis=0, tiled=True)
    outgoing = select(chosen, spread.reshape(4 * tokens, width))
    arrived = lax.all_to_all(
        outgoing.reshape(32, 4 * CAP * 8, 128), ("x", "z"), split_axis=0, concat_axis=0, tiled=True
    )
    done = expert(arrived.reshape(-1, 128), weight_in, weight_out)
    answers = lax.all_to_all(
        done.reshape(32, 4 * CAP * 8, 128), ("x", "z"), split_axis=0, concat_axis=0, tiled=True
    )
    sums = gather(shares, answers.reshape(-1, 128))
    sums = lax.all_to_all(
        sums.reshape(4, tokens, width), "y2", split_axis=0, concat_axis=0, tiled=True
    )
    return hidden + jnp.sum(sums.astype(F32), axis=0)


def solution(mesh):
    fine = Mesh(mesh.devices.reshape(8, 4, 4, 2, 2), ("z", "x", "y2", "y1", "dp"))
    rows = P(("dp", "x", "y2", "y1", "z"), None)
    halves = P(("z", "x", "y2", "y1"), None, None)
    return jax.shard_map(
        local,
        mesh=fine,
        in_specs=(rows, rows, rows, rows, P("z", None), P(), rows, rows, halves, halves),
        out_specs=rows,
        check_vma=False,
    )
```

```python
import math

import jax
import jax.numpy as jnp
from jax import lax
from jax.experimental import pallas as pl
from jax.experimental.pallas import tpu as pltpu
from jax.sharding import Mesh
from jax.sharding import PartitionSpec as P

HD = 128
CAP = 5
LOG2E = 1.4426950408889634
BF = jnp.bfloat16
F32 = jnp.float32
NEG = -1e30
LOW = -1e29
STAT = 8
SWAP = [(0, 1), (1, 0)]


def flash_kernel(
    pos_ref, q_ref, b0, b1, b2, b3, b4, b5, b6, b7, o_ref, kv_ref, vt_ref, bias_ref, acc_ref, m_ref, top_ref
):
    block = pl.program_id(0)
    own_x = pos_ref[0]
    own_y = pos_ref[1]
    cols = 1024
    scale = LOG2E / math.sqrt(HD)

    def keys(c):
        return kv_ref[pl.ds(4 * (c % 2), 4), c // 2, :, 0:HD].reshape(512, HD)

    @pl.when(block == 0)
    def _():
        eye = (
            lax.broadcasted_iota(jnp.int32, (HD, HD), 0)
            == lax.broadcasted_iota(jnp.int32, (HD, HD), 1)
        ).astype(BF)
        for far, ref in enumerate((b0, b5, b6, b7, b4, b3, b2, b1)):
            kv_ref[(own_y + far) % 8] = ref[0:512, :].reshape(4, 128, 2 * HD)
        for c in range(8):
            v = kv_ref[4 * (c % 2) : 4 * (c % 2) + 4, c // 2, :, HD : 2 * HD].reshape(512, HD)
            turned = lax.dot_general(eye, v, (((1,), (1,)), ((), ())), preferred_element_type=F32)
            vt_ref[c, 0:HD, :] = turned.astype(BF)
            vt_ref[c, HD : HD + 16, :] = jnp.ones((16, 512), BF)
        row = lax.broadcasted_iota(jnp.int32, (512, 128), 0)
        col = lax.broadcasted_iota(jnp.int32, (512, 128), 1)
        inner = row % 128
        key_pos = (
            (row // 128 - own_y % 4) * 512 + (inner // 16) * 64 + inner % 16 + 16 * own_x - col % 64
        )
        for z in range(8):
            bias_ref[:, z * 128 : (z + 1) * 128] = jnp.where(key_pos <= z * 64, 0.0, NEG)

    tiles = block * 8 + own_y
    chunk_count = tiles // 4
    q_raw = q_ref[0]
    q = jnp.concatenate([q_raw[:, :, 0:HD], q_raw[:, :, HD : 2 * HD]], axis=1).reshape(cols, HD)
    group = 1024
    groups = [(g * group, q[g * group : (g + 1) * group]) for g in range(cols // group)]

    def scores(k, q_group):
        return lax.dot_general(k, q_group, (((1,), (1,)), ((), ())), preferred_element_type=F32)

    first_keys = kv_ref[0, 0, :, 0:HD]
    hide = jnp.where(tiles == 0, 1.0, 0.0)
    for start, q_group in groups:
        part = slice(start, start + group)
        s = scores(first_keys, q_group) + bias_ref[0:128, part] * hide
        m_ref[:, part] = jnp.maximum(jnp.max(s, axis=0, keepdims=True), LOW)
        top_ref[:, part] = jnp.max(s.reshape(16, 8, group), axis=0)
        acc_ref[:, part] = jnp.zeros((HD + 16, group), F32)

    def quick(c, masked):
        k = keys(c)
        values = vt_ref[c]
        found = [scores(k, q_group) for _, q_group in groups]
        for (start, _), s in zip(groups, found):
            part = slice(start, start + group)
            if masked:
                s = s + bias_ref[:, part]
            p = jnp.exp2(s * scale - m_ref[:, part] * scale).astype(BF)
            top_ref[:, part] = jnp.maximum(
                top_ref[:, part], jnp.max(s.reshape(64, 8, group), axis=0)
            )
            acc_ref[:, part] = acc_ref[:, part] + jnp.dot(values, p, preferred_element_type=F32)

    def quick_step(c, carry):
        quick(c, False)
        return carry

    lax.fori_loop(0, chunk_count, quick_step, 0)
    quick(chunk_count, True)

    def careful(c, masked):
        k = keys(c)
        values = vt_ref[c]
        for start, q_group in groups:
            part = slice(start, start + group)
            s = scores(k, q_group)
            if masked:
                s = s + bias_ref[:, part]
            m_old = m_ref[:, part]
            m = jnp.maximum(m_old, jnp.max(s, axis=0, keepdims=True))
            p = jnp.exp2((s - m) * scale).astype(BF)
            alpha = jnp.exp2((m_old - m) * scale)
            m_ref[:, part] = m
            acc_ref[:, part] = acc_ref[:, part] * alpha + jnp.dot(
                values, p, preferred_element_type=F32
            )

    def careful_step(c, carry):
        careful(c, False)
        return carry

    rise = jnp.max((top_ref[...] - m_ref[...]) * scale)

    @pl.when(rise > 64.0)
    def _():
        m_ref[...] = jnp.full((1, cols), LOW, F32)
        acc_ref[...] = jnp.zeros((HD + 16, cols), F32)
        lax.fori_loop(0, chunk_count, careful_step, 0)
        careful(chunk_count, True)

    total = acc_ref[HD : HD + 1, :]
    seen = total > 0.0
    safe = jnp.where(seen, total, 1.0)
    out = (acc_ref[0:HD, :] * (1.0 / safe)).astype(BF)
    level = jnp.where(seen, m_ref[...] * scale + jnp.log(safe) * LOG2E, NEG)
    first = level.astype(BF).astype(F32)
    second = (level - first).astype(BF).astype(F32)
    third = level - first - second
    pick = lax.broadcasted_iota(jnp.int32, (STAT, cols), 0)
    stats = jnp.where(pick == 0, first, jnp.where(pick == 1, second, jnp.where(pick == 2, third, 0.0)))
    stats = stats.astype(BF)
    for i in range(8):
        o_ref[0, i, 0:HD, :] = out[:, i * 128 : (i + 1) * 128]
        o_ref[0, i, HD : HD + STAT, :] = stats[:, i * 128 : (i + 1) * 128]


def flash(position, queries, key_values):
    return pl.pallas_call(
        flash_kernel,
        grid_spec=pltpu.PrefetchScalarGridSpec(
            num_scalar_prefetch=1,
            grid=(4,),
            in_specs=[
                pl.BlockSpec((1, 8, 64, 256), lambda i, s: (i, 0, 0, 0)),
            ]
            + [pl.BlockSpec(block.shape, lambda i, s: (0, 0)) for block in key_values],
            out_specs=pl.BlockSpec((1, 8, HD + STAT, 128), lambda i, s: (i, 0, 0, 0)),
            scratch_shapes=[
                pltpu.VMEM((8, 4, 128, 2 * HD), BF),
                pltpu.VMEM((8, HD + 16, 512), BF),
                pltpu.VMEM((512, 1024), F32),
                pltpu.VMEM((HD + 16, 1024), F32),
                pltpu.VMEM((1, 1024), F32),
                pltpu.VMEM((8, 1024), F32),
            ],
        ),
        out_shape=jax.ShapeDtypeStruct((4, 8, HD + STAT, 128), BF),
        compiler_params=pltpu.CompilerParams(vmem_limit_bytes=40 * 1024 * 1024),
        cost_estimate=pl.CostEstimate(
            flops=4 * 4096 * 2560 * HD, bytes_accessed=5 << 20, transcendentals=4096 * 2560
        ),
        name="flash",
    )(position, queries, *key_values)


def merge_kernel(parts_ref, w_ref, res_ref, gain_ref, hidden_ref, normed_ref):
    step = pl.program_id(0)
    found = []
    for c in range(2):
        levels = []
        for x in range(4):
            st = parts_ref[x, c, HD : HD + STAT, :].astype(F32)
            levels.append(st[0:1] + st[1:2] + st[2:3])
        top = jnp.maximum(jnp.maximum(levels[0], levels[1]), jnp.maximum(levels[2], levels[3]))
        shares = [jnp.exp2(level - top) for level in levels]
        inverse = 1.0 / (shares[0] + shares[1] + shares[2] + shares[3])
        mixed = parts_ref[0, c, 0:HD, :].astype(F32) * (shares[0] * inverse)
        for x in range(1, 4):
            mixed = mixed + parts_ref[x, c, 0:HD, :].astype(F32) * (shares[x] * inverse)
        rows = mixed.T.astype(BF)
        found += [rows[0:64], rows[64:128]]
    part = jnp.dot(jnp.concatenate(found, axis=1), w_ref[...], preferred_element_type=F32)

    @pl.when(step == 0)
    def _():
        hidden_ref[...] = res_ref[...].astype(F32) + part

    @pl.when(step > 0)
    def _():
        hidden_ref[...] = hidden_ref[...] + part

    @pl.when(step == 3)
    def _():
        hidden = hidden_ref[...]
        mean_square = jnp.mean(hidden * hidden, axis=1, keepdims=True)
        normed = (hidden * lax.rsqrt(mean_square + 1e-6) * gain_ref[...]).astype(BF)
        for i in range(4):
            normed_ref[i] = normed


def merge(parts, weight, residual, gain):
    tokens, width = residual.shape
    whole = pl.BlockSpec((tokens, width), lambda c: (0, 0))
    return pl.pallas_call(
        merge_kernel,
        grid=(4,),
        in_specs=[
            pl.BlockSpec((4, 2, HD + STAT, 128), lambda c: (0, c, 0, 0)),
            pl.BlockSpec((512, width), lambda c: (c, 0)),
            whole,
            pl.BlockSpec((1, width), lambda c: (0, 0)),
        ],
        out_specs=[whole, pl.BlockSpec((4, tokens, width), lambda c: (0, 0, 0))],
        out_shape=[
            jax.ShapeDtypeStruct((tokens, width), F32),
            jax.ShapeDtypeStruct((4, tokens, width), BF),
        ],
        compiler_params=pltpu.CompilerParams(vmem_limit_bytes=48 * 1024 * 1024),
        name="merge",
    )(parts, weight, residual, gain)


def select_kernel(sel_ref, x_ref, o_ref, tmp_ref):
    count = sel_ref.shape[0]
    sel = sel_ref[...]
    for j in range(0, 8, 2):
        got = jnp.dot(sel, x_ref[:, j * 128 : (j + 2) * 128], preferred_element_type=F32)
        tmp_ref[pl.ds(j, count, stride=8), :] = got[:, 0:128]
        tmp_ref[pl.ds(j + 1, count, stride=8), :] = got[:, 128:256]
    o_ref[...] = tmp_ref[...].astype(BF)


def select(chosen, tokens):
    count = chosen.shape[0]
    return pl.pallas_call(
        select_kernel,
        out_shape=jax.ShapeDtypeStruct((count * 8, 128), BF),
        scratch_shapes=[pltpu.VMEM((count * 8, 128), F32)],
        compiler_params=pltpu.CompilerParams(vmem_limit_bytes=14 * 1024 * 1024),
        name="select",
    )(chosen, tokens)


def expert_kernel(x_ref, win_ref, wout_ref, o_ref, tmp_ref):
    rows = x_ref.shape[0] // 8
    inner = wout_ref.shape[0]
    tmp_ref[...] = x_ref[...].astype(F32)
    x = jnp.concatenate(
        [tmp_ref[pl.ds(j, rows, stride=8), :].astype(BF) for j in range(8)], axis=1
    )
    projection = jnp.dot(x, win_ref[...], preferred_element_type=F32)
    gate = projection[:, 0:inner]
    activated = (gate / (1.0 + jnp.exp(-gate)) * projection[:, inner:]).astype(BF)
    out = jnp.dot(activated, wout_ref[...], preferred_element_type=F32)
    for j in range(8):
        tmp_ref[pl.ds(j, rows, stride=8), :] = out[:, j * 128 : (j + 1) * 128]
    o_ref[...] = tmp_ref[...].astype(BF)


def expert(rows_in, weight_in, weight_out):
    total = rows_in.shape[0]
    block = total // 4
    return pl.pallas_call(
        expert_kernel,
        grid=(4,),
        in_specs=[
            pl.BlockSpec((block, 128), lambda i: (i, 0)),
            pl.BlockSpec(weight_in.shape, lambda i: (0, 0)),
            pl.BlockSpec(weight_out.shape, lambda i: (0, 0)),
        ],
        out_specs=pl.BlockSpec((block, 128), lambda i: (i, 0)),
        out_shape=jax.ShapeDtypeStruct((total, 128), BF),
        scratch_shapes=[pltpu.VMEM((block, 128), F32)],
        compiler_params=pltpu.CompilerParams(vmem_limit_bytes=52 * 1024 * 1024),
        name="expert",
    )(rows_in, weight_in, weight_out)


def gather_kernel(gates_ref, x_ref, o_ref, tmp_ref):
    count = gates_ref.shape[1]
    gates = gates_ref[...]
    tmp_ref[...] = x_ref[...].astype(F32)
    for j in range(0, 8, 2):
        x = jnp.concatenate(
            [
                tmp_ref[pl.ds(j, count, stride=8), :].astype(BF),
                tmp_ref[pl.ds(j + 1, count, stride=8), :].astype(BF),
            ],
            axis=1,
        )
        o_ref[:, j * 128 : (j + 2) * 128] = jnp.dot(
            gates, x, preferred_element_type=F32
        ).astype(BF)


def gather(gates, rows):
    count = gates.shape[1]
    return pl.pallas_call(
        gather_kernel,
        out_shape=jax.ShapeDtypeStruct((gates.shape[0], 1024), BF),
        scratch_shapes=[pltpu.VMEM((count * 8, 128), F32)],
        compiler_params=pltpu.CompilerParams(vmem_limit_bytes=14 * 1024 * 1024),
        name="gather",
    )(gates, rows)


def pack_kv_kernel(k_ref, v_ref, o_ref):
    for g in range(2):
        lanes = slice(g * HD, (g + 1) * HD)
        both = jnp.concatenate([k_ref[:, lanes], v_ref[:, lanes]], axis=1)
        for x in range(4):
            for i in range(4):
                o_ref[x * 8 + g * 4 + i] = both[16 * x : 16 * x + 16]


def pack_kv(keys, values):
    return pl.pallas_call(
        pack_kv_kernel,
        out_shape=jax.ShapeDtypeStruct((32, 16, 2 * HD), BF),
        name="pack_kv",
    )(keys, values)


def pack_q_kernel(q_ref, o_ref):
    for z in range(8):
        piece = q_ref[:, z * 2 * HD : (z + 1) * 2 * HD]
        for x in range(4):
            o_ref[x * 8 + z] = piece


def pack_q(queries):
    return pl.pallas_call(
        pack_q_kernel,
        out_shape=jax.ShapeDtypeStruct((32, queries.shape[0], 2 * HD), BF),
        cost_estimate=pl.CostEstimate(flops=0, bytes_accessed=5 << 18, transcendentals=0),
        name="pack_q",
    )(queries)


def local(
    residual,
    queries,
    key_vectors,
    value_vectors,
    output_weight,
    norm_gain,
    routes,
    gate_levels,
    expert_in,
    expert_out,
):
    tokens, width = residual.shape
    own_x = lax.axis_index("x")
    own_y2 = lax.axis_index("y2")
    own_y = own_y2 * 2 + lax.axis_index("y1")
    position = jnp.stack([own_x, own_y]).astype(jnp.int32)

    key_value = pack_kv(key_vectors, value_vectors)
    key_value = lax.all_to_all(key_value, ("x", "z"), split_axis=0, concat_axis=0, tiled=True)
    listing = jnp.concatenate([routes.T, gate_levels.T], axis=0).astype(BF)
    listing = jnp.pad(listing, ((0, 0), (0, 2 * HD - tokens)))
    block = jnp.concatenate([key_value.reshape(512, 2 * HD), listing], axis=0)
    up = [(i, (i + 1) % 8) for i in range(8)]
    down = [(i, (i - 1) % 8) for i in range(8)]
    ups, downs = [block], [block]
    for step in range(4):
        ups.append(lax.ppermute(ups[-1], ("y2", "y1"), up))
        if step < 3:
            downs.append(lax.ppermute(downs[-1], ("y2", "y1"), down))
    key_values = ups + downs[1:]

    query = lax.all_to_all(pack_q(queries), ("x", "z"), split_axis=0, concat_axis=0, tiled=True).reshape(
        4, 8, tokens, 2 * HD
    )

    whole_weight = lax.all_gather(output_weight, "z", axis=0, tiled=True)

    shards = flash(position, query, key_values)
    parts = lax.all_to_all(
        shards.reshape(32, HD + STAT, 128), ("x", "z"), split_axis=0, concat_axis=0, tiled=True
    ).reshape(4, 8, HD + STAT, 128)
    whole_weight, own_in, own_out = lax.optimization_barrier(
        (whole_weight, expert_in[0], expert_out[0])
    )
    other_in = lax.ppermute(own_in, "y1", SWAP)
    other_out = lax.ppermute(own_out, "y1", SWAP)
    turned = [ups[0][512:], ups[2][512:], ups[4][512:], downs[2][512:]]
    listing = lax.dynamic_slice_in_dim(
        jnp.stack([turned[k][:, :tokens] for k in (3, 2, 1, 0, 3, 2, 1)]), 3 - own_y2, 4, 0
    ).astype(jnp.int32)
    named, levels = listing[:, None, 0:8], listing[:, None, 8:16]
    q = jnp.arange(32, dtype=jnp.int32)
    match = named == ((q % 8) * 16 + (q // 8) * 4 + own_y2)[None, :, None, None]
    hits = jnp.any(match, axis=2)
    gates = jnp.sum(jnp.where(match, levels, 0), axis=2).astype(F32) / 256.0
    before = jnp.triu(jnp.ones((tokens, tokens), BF), 1)
    ranks = jnp.einsum("sqb,ba->sqa", hits.astype(BF), before, preferred_element_type=F32)
    ranks = jnp.where(hits, ranks.astype(jnp.int32), -1)
    slots = jnp.arange(CAP, dtype=jnp.int32)[None, None, :, None, None]
    same = jnp.eye(4, dtype=jnp.bool_)[None, :, None, :, None]
    placed = (ranks.transpose(1, 0, 2)[:, None, None] == slots) & same
    chosen = placed.astype(BF).reshape(32 * 4 * CAP, 4 * tokens)
    shares = jnp.where(placed, gates.transpose(1, 0, 2)[:, None, None], 0.0).astype(BF)
    shares = shares.reshape(32 * 4 * CAP, 4 * tokens).T

    hidden, spread = merge(
        parts, whole_weight, residual, norm_gain.reshape(1, width)
    )

    spread, other_in, other_out = lax.optimization_barrier((spread, other_in, other_out))
    half = own_in.shape[1] // 2
    weight_in = jnp.concatenate(
        [own_in[:, :half], other_in[:, :half], own_in[:, half:], other_in[:, half:]], axis=1
    )
    weight_out = jnp.concatenate([own_out, other_out], axis=0)
    spread = lax.all_to_all(spread, "y2", split_axis=0, concat_axis=0, tiled=True)
    outgoing = select(chosen, spread.reshape(4 * tokens, width))
    arrived = lax.all_to_all(
        outgoing.reshape(32, 4 * CAP * 8, 128), ("x", "z"), split_axis=0, concat_axis=0, tiled=True
    )
    done = expert(arrived.reshape(-1, 128), weight_in, weight_out)
    answers = lax.all_to_all(
        done.reshape(32, 4 * CAP * 8, 128), ("x", "z"), split_axis=0, concat_axis=0, tiled=True
    )
    sums = gather(shares, answers.reshape(-1, 128))
    sums = lax.all_to_all(
        sums.reshape(4, tokens, width), "y2", split_axis=0, concat_axis=0, tiled=True
    )
    return hidden + jnp.sum(sums.astype(F32), axis=0)


def solution(mesh):
    fine = Mesh(mesh.devices.reshape(8, 4, 4, 2, 2), ("z", "x", "y2", "y1", "dp"))
    rows = P(("dp", "x", "y2", "y1", "z"), None)
    halves = P(("z", "x", "y2", "y1"), None, None)
    return jax.shard_map(
        local,
        mesh=fine,
        in_specs=(rows, rows, rows, rows, P("z", None), P(), rows, rows, halves, halves),
        out_specs=rows,
        check_vma=False,
    )
```
